128 devices in a mesh: chan: 16 (over y, z_hi, core), seq: 8 (over x, z_lo).
Axes of the slice: x: 4, y: 4, z: 4 (z_hi: 2, z_lo: 2; z = z_hi * 2 + z_lo), core: 2. Of those that a mesh axis runs over, the one named last changes fastest.
Arguments:
- value: bfloat16 [16, 128, 32768], P('seq', 'chan'), may hold values from -6 to 6
- gate_in: bfloat16 [16, 128, 32768], P('seq', 'chan'), may hold values from -6 to 6
- gate_out: bfloat16 [16, 128, 32768], P('seq', 'chan'), may hold values from -6 to 6
- cotangent: bfloat16 [16, 128, 32768], P('seq', 'chan'), may hold values from -6 to 6
- skip_gain: float32 [128], P('chan'), may hold values from 0.25 to 1.5
- weight_in: float32 [64, 33], replicated, may hold values from -1 to 1
- bias_in: float32 [64], replicated, may hold values from -1 to 1
- weight_mid: float32 [2, 64, 64], replicated, may hold values from -0.75 to 0.75
- bias_mid: float32 [2, 64], replicated, may hold values from -1 to 1
- weight_out: float32 [128, 64], replicated, may hold values from -0.75 to 0.75
- decay_rate: float32 [128], replicated, may hold values from 3 to 15
Outputs:
- grad_value: bfloat16 [16, 128, 32768], P('seq', 'chan')
- grad_gate_in: bfloat16 [16, 128, 32768], P('seq', 'chan')
- grad_gate_out: bfloat16 [16, 128, 32768], P('seq', 'chan')
- grad_skip: float32 [128], P('chan')
- grad_weight_in: float32 [64, 33], replicated
- grad_bias_in: float32 [64], replicated
- grad_weight_mid: float32 [2, 64, 64], replicated
- grad_bias_mid: float32 [2, 64], replicated
- grad_weight_out: float32 [128, 64], replicated
- grad_rate: float32 [128], replicated
The draws below stay inside these ranges and needn't reach their ends.
All inputs are finite; a program needn't handle non-finite values.
Results may differ from the reference program's by a relative error of at most 0.009.
Values sent between devices are 32-bit elements; how exact they have to be, the bound alone decides.
A program may use at most 128 MiB of HBM per device.

```python
import math
import jax
import jax.numpy as jnp
import numpy as np
from jax import lax

L = 32768
CH = 128
ORDER = 64
EMB = 33
BATCH = 16


def levels(key, shape, split, least, largest):
    level = 1.0
    for dim, parts in split:
        heights = jax.random.uniform(jax.random.fold_in(jax.random.fold_in(key, 6), dim), (parts,), jnp.float32, least / len(split), largest / len(split))
        level = level * jnp.repeat(jnp.exp(heights), shape[dim] // parts).reshape((-1,) + (1,) * (len(shape) - 1 - dim))
    return level


def centred(rng, extent, scale, reach, shards=(), kind=jnp.bfloat16):
    loudness = levels(rng, extent, shards, -0.22, 0.18) if shards else 1.0
    entries = jax.random.normal(rng, extent, jnp.float32) * scale * loudness
    return jnp.minimum(jnp.maximum(entries, -reach), reach).astype(kind)


def setup_inputs(seed: int = 0) -> dict:
    key_of = jax.random.split(jax.random.key(seed), 12)
    return {
        "value": centred(key_of[0], (BATCH, CH, L), 1.0, 6.0, ((0, 8), (1, 16))),
        "gate_in": centred(key_of[1], (BATCH, CH, L), 1.0, 6.0, ((0, 8), (1, 16))),
        "gate_out": centred(key_of[2], (BATCH, CH, L), 1.0, 6.0, ((0, 8), (1, 16))),
        "cotangent": centred(key_of[3], (BATCH, CH, L), 1.0, 6.0, ((0, 8), (1, 16))),
        "skip_gain": jnp.clip(0.25 + 1.25 * jax.random.uniform(key_of[4], (CH,), jnp.float32) ** levels(key_of[4], (CH,), ((0, 16),), -0.2, 0.2), 0.25, 1.5),
        "weight_in": centred(key_of[5], (ORDER, EMB), EMB ** -0.5, 1.0, (), jnp.float32),
        "bias_in": jnp.clip(jax.random.uniform(key_of[6], (ORDER,), jnp.float32, -1.0, 1.0), -1.0, 1.0),
        "weight_mid": centred(key_of[7], (2, ORDER, ORDER), ORDER ** -0.5, 0.75, (), jnp.float32),
        "bias_mid": jnp.clip(jax.random.uniform(key_of[8], (2, ORDER), jnp.float32, -1.0, 1.0), -1.0, 1.0),
        "weight_out": centred(key_of[9], (CH, ORDER), ORDER ** -0.5, 0.75, (), jnp.float32),
        "decay_rate": jnp.clip(jnp.exp(jax.random.uniform(key_of[10], (CH,), jnp.float32, math.log(3.0), math.log(15.0))), 3.0, 15.0),
    }


EPSILON = 1e-06
HIGHEST = lax.Precision.HIGHEST

def band_table(length, bands):
    highest = length / 4.0
    return np.array([math.floor(highest ** (number / (bands - 1)) + 0.5) for number in range(bands)], np.int32)

def embedding(positions, length, bands):
    band_freq = jnp.asarray(band_table(length, bands)).astype(jnp.int32)
    phase = positions[None, :] * band_freq[:, None] % length
    angle = 2.0 * math.pi / length * phase.astype(jnp.float32)
    linear = (positions.astype(jnp.float32) / length)[None, :]
    return jnp.concatenate([linear, jnp.cos(angle), jnp.sin(angle)], axis=0)

def filter_rows(weight_in, bias_in, weight_mid, bias_mid, weight_out, decay_rate, positions, length):
    bands = (weight_in.shape[1] - 1) // 2
    feature = embedding(positions, length, bands)
    hidden = jnp.sin(jnp.dot(weight_in, feature, precision=HIGHEST) + bias_in[:, None])
    for middle in range(2):
        hidden = jnp.sin(jnp.dot(weight_mid[middle], hidden, precision=HIGHEST) + bias_mid[middle][:, None])
    shaped = jnp.dot(weight_out, hidden, precision=HIGHEST)
    scaled_pos = (positions.astype(jnp.float32) / length)[None, :]
    return shaped * jnp.exp(-decay_rate[:, None] * scaled_pos)

def normalized(raw):
    return raw / jnp.sqrt(lax.optimization_barrier(jnp.sum(raw * raw, axis=-1, keepdims=True)) + EPSILON)

def rounded(array):
    return lax.optimization_barrier(array.astype(jnp.bfloat16)).astype(jnp.float32)

def dft_tables(length):
    total = 2 * length
    col_count = 128
    row_count = total // col_count
    row_ids = jnp.arange(row_count, dtype=jnp.int32)
    half_ids = jnp.arange(row_count // 2, dtype=jnp.int32)
    col_ids = jnp.arange(col_count, dtype=jnp.int32)
    angle_rows = 2.0 * math.pi / row_count * (row_ids[:, None] * half_ids[None, :] % row_count).astype(jnp.float32)
    angle_cols = 2.0 * math.pi / col_count * (col_ids[:, None] * col_ids[None, :] % col_count).astype(jnp.float32)
    angle_twist = 2.0 * math.pi / total * (row_ids[:, None] * col_ids[None, :] % total).astype(jnp.float32)
    return (row_count, col_count, total, rounded(jnp.cos(angle_rows)), rounded(jnp.sin(angle_rows)), rounded(jnp.cos(angle_cols)), rounded(jnp.sin(angle_cols)), jnp.cos(angle_twist), jnp.sin(angle_twist))

def forward(signal, tables):
    row_count, col_count, total, cos_rows, sin_rows, cos_cols, sin_cols, cos_twist, sin_twist = tables
    shaped = rounded(signal.reshape(signal.shape[:-1] + (row_count // 2, col_count)))
    first_re = jnp.einsum('ka,...ab->...kb', cos_rows, shaped, precision=HIGHEST)
    first_im = -jnp.einsum('ka,...ab->...kb', sin_rows, shaped, precision=HIGHEST)
    twist_re = rounded(first_re * cos_twist + first_im * sin_twist)
    twist_im = rounded(first_im * cos_twist - first_re * sin_twist)
    spec_re = jnp.einsum('...kb,bq->...kq', twist_re, cos_cols, precision=HIGHEST) + jnp.einsum('...kb,bq->...kq', twist_im, sin_cols, precision=HIGHEST)
    spec_im = jnp.einsum('...kb,bq->...kq', twist_im, cos_cols, precision=HIGHEST) - jnp.einsum('...kb,bq->...kq', twist_re, sin_cols, precision=HIGHEST)
    return (spec_re, spec_im)

def inverse(spec_re, spec_im, tables):
    row_count, col_count, total, cos_rows, sin_rows, cos_cols, sin_cols, cos_twist, sin_twist = tables
    part_re = rounded(spec_re)
    part_im = rounded(spec_im)
    back_re = jnp.einsum('...kq,qb->...kb', part_re, cos_cols, precision=HIGHEST) - jnp.einsum('...kq,qb->...kb', part_im, sin_cols, precision=HIGHEST)
    back_im = jnp.einsum('...kq,qb->...kb', part_re, sin_cols, precision=HIGHEST) + jnp.einsum('...kq,qb->...kb', part_im, cos_cols, precision=HIGHEST)
    turn_re = rounded(back_re * cos_twist - back_im * sin_twist)
    turn_im = rounded(back_re * sin_twist + back_im * cos_twist)
    signal = jnp.einsum('ka,...kb->...ab', cos_rows, turn_re, precision=HIGHEST) - jnp.einsum('ka,...kb->...ab', sin_rows, turn_im, precision=HIGHEST)
    return signal.reshape(signal.shape[:-2] + (total // 2,)) / total

def reference(value, gate_in, gate_out, cotangent, skip_gain, weight_in, bias_in, weight_mid, bias_mid, weight_out, decay_rate):
    length = value.shape[-1]
    batch_count = value.shape[0]
    channels = value.shape[1]
    positions = jnp.arange(length, dtype=jnp.int32)

    def filter_all(wgt_in, bia_in, wgt_mid, bia_mid, wgt_out, rates):
        return normalized(filter_rows(wgt_in, bia_in, wgt_mid, bia_mid, wgt_out, rates, positions, length))
    kernel, pullback = jax.vjp(filter_all, weight_in, bias_in, weight_mid, bias_mid, weight_out, decay_rate)
    tables = dft_tables(length)
    kernel_re, kernel_im = forward(kernel, tables)

    def one_sequence(carry, inputs):
        kernel_sum, skip_sum = carry
        val_one, gin_one, gout_one, cot_one = inputs
        val_f = val_one.astype(jnp.float32)
        gin_f = gin_one.astype(jnp.float32)
        gout_f = gout_one.astype(jnp.float32)
        cot_f = cot_one.astype(jnp.float32)
        mixed = gin_f * val_f
        mixed_re, mixed_im = forward(mixed, tables)
        conv_re = mixed_re * kernel_re - mixed_im * kernel_im
        conv_im = mixed_re * kernel_im + mixed_im * kernel_re
        inner = inverse(conv_re, conv_im, tables) + skip_gain[:, None] * mixed
        grad_out = (cot_f * inner).astype(jnp.bfloat16)
        grad_inner = cot_f * gout_f
        inner_re, inner_im = forward(grad_inner, tables)
        back_re = inner_re * kernel_re + inner_im * kernel_im
        back_im = inner_im * kernel_re - inner_re * kernel_im
        grad_mixed = inverse(back_re, back_im, tables) + skip_gain[:, None] * grad_inner
        grad_val = (grad_mixed * gin_f).astype(jnp.bfloat16)
        grad_gin = (grad_mixed * val_f).astype(jnp.bfloat16)
        cross_re = mixed_re * inner_re + mixed_im * inner_im
        cross_im = mixed_re * inner_im - mixed_im * inner_re
        kernel_part = inverse(cross_re, cross_im, tables)
        carry_next = (kernel_sum + kernel_part, skip_sum + lax.optimization_barrier(jnp.sum(grad_inner * mixed, axis=-1)))
        return (carry_next, (grad_val, grad_gin, grad_out))
    start = (jnp.zeros((channels, length), jnp.float32), jnp.zeros((channels,), jnp.float32))
    final, stacked = lax.scan(one_sequence, start, (value, gate_in, gate_out, cotangent))
    grad_kernel, skip_sum = final
    grads = pullback(grad_kernel)
    factor = 1.0 / math.sqrt(batch_count * length)
    return (stacked[0], stacked[1], stacked[2], skip_sum * factor, grads[0] * factor, grads[1] * factor, grads[2] * factor, grads[3] * factor, grads[4] * factor, grads[5] * factor)
```

```python
import functools
import math

import jax
import jax.numpy as jnp
import numpy as np
from jax import lax
from jax.experimental import pallas as pl
from jax.experimental.pallas import tpu as pltpu
from jax.sharding import PartitionSpec as P

EPSILON = 1e-06
HIGHEST = lax.Precision.HIGHEST
L = 32768
A = 256
B = 128
CH = 8
NSEQ = 8
NCHAN = 16
ABLK = A // NSEQ
TB = L // NSEQ
CHUNK = 512
LOW = jnp.bfloat16
F32 = jnp.float32
MESH = pl.DeviceIdType.MESH


def band_table(length, bands):
    highest = length / 4.0
    return np.array(
        [math.floor(highest ** (number / (bands - 1)) + 0.5) for number in range(bands)], np.int64
    )


def row_constants():
    freq = np.zeros((40, 128), np.int32)
    off = np.zeros((40, 128), np.int32)
    bands = band_table(L, 16)
    freq[1:17] = bands[:, None]
    off[1:17] = L // 4
    freq[17:33] = bands[:, None]
    return freq, off


def transform_tables():
    k = np.arange(A)[:, None]
    rows = 2.0 * np.pi * (((4 * k + 1) * np.arange(A)[None, :]) % 1024) / 1024.0
    w1 = np.concatenate([np.cos(rows), -np.sin(rows)], axis=0)
    turn = 2.0 * np.pi * (((4 * k + 1) * np.arange(B)[None, :]) % (4 * L)) / (4.0 * L)
    q = np.arange(B)
    cols = 2.0 * np.pi * ((q[:, None] * q[None, :]) % B) / B
    c, s = np.cos(cols), np.sin(cols)
    fwd = np.block([[c, -s], [s, c]])
    inv = np.block([[c, s], [-s, c]])
    low = np.dtype(LOW)
    return (
        w1.astype(low),
        w1.T.astype(low),
        fwd.astype(low),
        inv.astype(low),
        np.stack([np.cos(turn), np.sin(turn)]).astype(np.float32),
    )


def poly_fit():
    x = (np.cos(np.pi * (np.arange(64) + 0.5) / 64) + 1) / 2 * (np.pi / 2 * 1.002) ** 2
    r = np.sqrt(x)
    sin_c = np.polynomial.polynomial.polyfit(x, np.sin(r) / r, 5)
    cos_c = np.polynomial.polynomial.polyfit(x, np.cos(r), 6)
    return [float(v) for v in sin_c], [float(v) for v in cos_c]


SIN_C, COS_C = poly_fit()


def horner(x, coefs):
    acc = jnp.full_like(x, coefs[-1])
    for value in coefs[-2::-1]:
        acc = acc * x + value
    return acc


def sin_small(r):
    return r * horner(r * r, SIN_C)


def sin_cos(z):
    n = jnp.floor(z * (1.0 / math.pi) + 0.5)
    r = z - n * 3.140625
    r = r - n * 9.67502593994140625e-4
    r = r - n * 1.509957990978376e-7
    half = n * 0.5
    sign = 1.0 - 4.0 * (half - jnp.floor(half))
    r2 = r * r
    return sign * (r * horner(r2, SIN_C)), sign * horner(r2, COS_C)


def dot_full(x, y):
    return jnp.dot(x, y, precision=HIGHEST, preferred_element_type=F32)


def dot_nt(x, y):
    return lax.dot_general(x, y, (((1,), (1,)), ((), ())), precision=HIGHEST, preferred_element_type=F32)


def dot_tn(x, y):
    return lax.dot_general(x, y, (((0,), (0,)), ((), ())), precision=HIGHEST, preferred_element_type=F32)


def to_column(row, size, shift):
    n = row.shape[1]
    i = lax.broadcasted_iota(jnp.int32, (size, n), 0) + shift
    j = lax.broadcasted_iota(jnp.int32, (size, n), 1)
    return jnp.sum(jnp.where(i == j, jnp.broadcast_to(row, (size, n)), 0.0), axis=1, keepdims=True)


def to_row(col):
    n = col.shape[0]
    i = lax.broadcasted_iota(jnp.int32, (n, n), 0)
    j = lax.broadcasted_iota(jnp.int32, (n, n), 1)
    return jnp.sum(jnp.where(i == j, jnp.broadcast_to(col, (n, n)), 0.0), axis=0, keepdims=True)


def net_forward(
    freq_ref, off_ref, w_in, b_in, w_mid, b_mid, w_out, rate, put_raw, seq, chan,
    feat, act1, act2, act3, der1, der2, der3,
):
    bias1 = to_column(b_in[...], 64, 0)
    bias2 = to_column(b_mid[0:1, :], 64, 0)
    bias3 = to_column(b_mid[1:2, :], 64, 0)
    rate_col = to_column(rate[...], CH, chan * CH)
    w_own = w_out[pl.ds(pl.multiple_of(chan * CH, CH), CH), :]
    weights = w_in[...]
    mid0, mid1 = w_mid[0], w_mid[1]

    def step(j, carry):
        base = pl.multiple_of(j * CHUNK, CHUNK)
        lanes = pl.ds(base, CHUNK)
        pos = seq * TB + base + lax.broadcasted_iota(jnp.int32, (40, CHUNK), 1)
        row = lax.broadcasted_iota(jnp.int32, (40, CHUNK), 0)
        freq = jnp.concatenate([freq_ref[...]] * (CHUNK // 128), axis=1)
        off = jnp.concatenate([off_ref[...]] * (CHUNK // 128), axis=1)
        phase = ((freq * pos + (off + L // 2)) & (L - 1)) - L // 2
        phase = jnp.where(phase > L // 4, L // 2 - phase, phase)
        phase = jnp.where(phase < -(L // 4), -(L // 2) - phase, phase)
        wave = sin_small(phase.astype(F32) * (2.0 * math.pi / L))
        frac = pos.astype(F32) * (1.0 / L)
        e = jnp.where(row == 0, frac, jnp.where(row == 33, 1.0, wave))
        feat[:, lanes] = e
        ones = jnp.where(lax.broadcasted_iota(jnp.int32, (8, CHUNK), 0) == 0, 1.0, 0.0)
        s1, c1 = sin_cos(dot_full(weights, e[0:33, :]) + bias1)
        act1[0:64, lanes] = s1
        act1[64:72, lanes] = ones
        der1[:, lanes] = c1
        s2, c2 = sin_cos(dot_full(mid0, s1) + bias2)
        act2[0:64, lanes] = s2
        act2[64:72, lanes] = ones
        der2[:, lanes] = c2
        s3, c3 = sin_cos(dot_full(mid1, s2) + bias3)
        act3[:, lanes] = s3
        der3[:, lanes] = c3
        raw = dot_full(w_own, s3) * jnp.exp(-rate_col * frac[0:CH, :])
        for i in range(CHUNK // 128):
            put_raw(j * (CHUNK // 128) + i, raw[:, 128 * i : 128 * i + 128])
        return carry

    lax.fori_loop(0, TB // CHUNK, step, 0)


def net_backward(
    get_raw, get_grad, w_mid, w_out, rate, seq, chan,
    feat, act1, act2, act3, der1, der2, der3,
    acc_in, acc_mid0, acc_mid1, acc_out, acc_rate,
):
    rate_col = to_column(rate[...], CH, chan * CH)
    w_own = w_out[pl.ds(pl.multiple_of(chan * CH, CH), CH), :]
    mid0, mid1 = w_mid[0], w_mid[1]
    acc_in[...] = jnp.zeros_like(acc_in)
    acc_mid0[...] = jnp.zeros_like(acc_mid0)
    acc_mid1[...] = jnp.zeros_like(acc_mid1)
    acc_out[...] = jnp.zeros_like(acc_out)
    acc_rate[...] = jnp.zeros_like(acc_rate)

    def step(j, carry):
        base = pl.multiple_of(j * CHUNK, CHUNK)
        lanes = pl.ds(base, CHUNK)
        per = CHUNK // 128
        grad = jnp.concatenate([get_grad(j * per + i) for i in range(per)], axis=1)
        raw = jnp.concatenate([get_raw(j * per + i) for i in range(per)], axis=1)
        frac = (seq * TB + base + lax.broadcasted_iota(jnp.int32, (CH, CHUNK), 1)).astype(F32) * (1.0 / L)
        acc_rate[...] += jnp.sum(grad * raw * -frac, axis=1, keepdims=True)
        shaped = grad * jnp.exp(-rate_col * frac)
        acc_out[...] += dot_nt(shaped, act3[:, lanes])
        d3 = dot_tn(w_own, shaped) * der3[:, lanes]
        acc_mid1[...] += dot_nt(d3, act2[:, lanes])
        d2 = dot_tn(mid1, d3) * der2[:, lanes]
        acc_mid0[...] += dot_nt(d2, act1[:, lanes])
        d1 = dot_tn(mid0, d2) * der1[:, lanes]
        acc_in[...] += dot_nt(d1, feat[:, lanes])
        return carry

    lax.fori_loop(0, TB // CHUNK, step, 0)


def greet(seq_peers, chan_peers):
    chan, seq = lax.axis_index("chan"), lax.axis_index("seq")
    barrier = pltpu.get_barrier_semaphore()

    def hail_seq(d, carry):
        pl.semaphore_signal(barrier, inc=1, device_id=(chan, lax.rem(seq + d, NSEQ)), device_id_type=MESH)
        return carry

    def hail_chan(d, carry):
        pl.semaphore_signal(barrier, inc=1, device_id=(lax.rem(chan + d, NCHAN), seq), device_id_type=MESH)
        return carry

    if seq_peers:
        lax.fori_loop(1, NSEQ, hail_seq, 0)
    if chan_peers:
        lax.fori_loop(1, NCHAN, hail_chan, 0)
    return barrier


def exchange(axis, size, make):
    def start(d, carry):
        make(d).start()
        return carry

    def wait(d, carry):
        make(d).wait()
        return carry

    lax.fori_loop(1, size, start, 0)
    return lambda: lax.fori_loop(1, size, wait, 0)


def filter_kernel(
    freq_ref, off_ref, w_in, b_in, w_mid, b_mid, w_out, rate,
    raw_all, feat, act1, act2, act3, der1, der2, der3,
    send_sem, recv_sem,
):
    chan, seq = lax.axis_index("chan"), lax.axis_index("seq")
    barrier = greet(True, False)
    start = seq * ABLK

    def put_raw(i, block):
        raw_all[start + i] = block

    net_forward(
        freq_ref, off_ref, w_in, b_in, w_mid, b_mid, w_out, rate, put_raw, seq, chan,
        feat, act1, act2, act3, der1, der2, der3,
    )
    pl.semaphore_wait(barrier, NSEQ - 1)
    own = raw_all.at[pl.ds(start, ABLK)]

    def make(d):
        return pltpu.make_async_remote_copy(
            src_ref=own, dst_ref=own, send_sem=send_sem.at[d], recv_sem=recv_sem.at[d],
            device_id=(chan, lax.rem(seq + d, NSEQ)), device_id_type=MESH,
        )

    exchange("seq", NSEQ, make)()


def to_low(x):
    return x.astype(LOW)


def conv_kernel(
    val, gin, gout, cot, raw, skip, w1, w1t, fwd, inv, turn,
    o_val, o_gin, o_gout, grad_raw, skip_part,
    mixed, inner, f_mixed, f_inner, gk, kern, conv, back,
):
    tc, ts = turn[0], turn[1]

    def products(i, acc):
        n = i // A
        a = lax.rem(i, A)
        rows = pl.ds(pl.multiple_of(a * CH, CH), CH)
        m = val[n, a].astype(F32) * gin[n, a].astype(F32)
        g = cot[n, a].astype(F32) * gout[n, a].astype(F32)
        mixed[n, rows, :] = m
        inner[n, rows, :] = g
        return acc + m * g

    acc = lax.fori_loop(0, 2 * A, products, jnp.zeros((CH, B), F32), unroll=8)
    skip_part[...] = jnp.broadcast_to(jnp.sum(acc, axis=1, keepdims=True), (CH, B))

    def forward(x):
        g = jnp.dot(w1[...], x, preferred_element_type=F32)
        parts = []
        for n in range(2):
            re, im = g[0:A, n * B : n * B + B], g[A:, n * B : n * B + B]
            parts.append(jnp.concatenate([to_low(re * tc + im * ts), to_low(im * tc - re * ts)], axis=1))
        h = jnp.concatenate(parts, axis=0)
        f = jnp.dot(h, fwd[...], preferred_element_type=F32)
        return f[0:A], f[A:]

    def inverse(specs):
        s = jnp.concatenate([jnp.concatenate([to_low(re), to_low(im)], axis=1) for re, im in specs], axis=0)
        t = jnp.dot(s, inv[...], preferred_element_type=F32)
        cols = []
        for n in range(len(specs)):
            re, im = t[n * A : n * A + A, 0:B], t[n * A : n * A + A, B:]
            cols.append(jnp.concatenate([to_low(re * tc - im * ts), to_low(re * ts + im * tc)], axis=0))
        x = jnp.concatenate(cols, axis=1) if len(cols) > 1 else cols[0]
        y = jnp.dot(w1t[...], x, preferred_element_type=F32)
        return [y[:, n * B : n * B + B] for n in range(len(specs))]

    def channel_rows(c):
        return pl.ds(c, A, stride=CH)

    def spectra(c, carry):
        rows = channel_rows(c)
        x = jnp.concatenate([to_low(mixed[n, rows, :]) for n in range(2)], axis=1)
        fm = forward(x)
        x = jnp.concatenate([to_low(inner[n, rows, :]) for n in range(2)], axis=1)
        fg = forward(x)
        re = im = 0.0
        for n in range(2):
            f_mixed[c, n] = fm[n]
            f_inner[c, n] = fg[n]
            mr, mi = fm[n][:, 0:B], fm[n][:, B:]
            gr, gi = fg[n][:, 0:B], fg[n][:, B:]
            re = re + (mr * gr + mi * gi)
            im = im + (mr * gi - mi * gr)
        gk[rows, :] = inverse([(re, im)])[0]
        return carry

    lax.fori_loop(0, CH, spectra, 0)

    def sums(a, carry):
        square, along = carry
        rows = pl.ds(pl.multiple_of(a * CH, CH), CH)
        r = raw[a]
        return square + r * r, along + r * gk[rows, :]

    zero = jnp.zeros((CH, B), F32)
    square, along = lax.fori_loop(0, A, sums, (zero, zero), unroll=8)
    norm = jnp.sqrt(jnp.sum(square, axis=1, keepdims=True) + EPSILON)
    along = jnp.sum(along, axis=1, keepdims=True) * (1.0 / L)
    recip = jnp.broadcast_to(1.0 / norm, (CH, B))
    scale_gk = recip * (1.0 / L)
    scale_raw = jnp.broadcast_to(along / (norm * norm * norm), (CH, B))
    scale_kern = recip * (1.0 / L)
    unit = recip

    def settle(a, carry):
        rows = pl.ds(pl.multiple_of(a * CH, CH), CH)
        r = raw[a]
        grad_raw[a] = gk[rows, :] * scale_gk - r * scale_raw
        kern[rows, :] = r * unit
        return carry

    lax.fori_loop(0, A, settle, 0, unroll=8)

    def products_with_filter(p, carry):
        x = jnp.concatenate([to_low(kern[channel_rows(2 * p + i), :]) for i in range(2)], axis=1)
        fk = forward(x)
        for i in range(2):
            c = 2 * p + i
            rows = channel_rows(c)
            kr, ki = fk[i][:, 0:B] * (1.0 / L), fk[i][:, B:] * (1.0 / L)
            specs = []
            for n in range(2):
                mr, mi = f_mixed[c, n, :, 0:B], f_mixed[c, n, :, B:]
                specs.append((mr * kr - mi * ki, mr * ki + mi * kr))
            ys = inverse(specs)
            for n in range(2):
                conv[n, rows, :] = ys[n]
            specs = []
            for n in range(2):
                gr, gi = f_inner[c, n, :, 0:B], f_inner[c, n, :, B:]
                specs.append((gr * kr + gi * ki, gi * kr - gr * ki))
            ys = inverse(specs)
            for n in range(2):
                back[n, rows, :] = ys[n]
        return carry

    lax.fori_loop(0, CH // 2, products_with_filter, 0)

    gain = jnp.broadcast_to(to_column(skip[...], CH, 0), (CH, B))

    def finish(i, carry):
        n = i // A
        a = lax.rem(i, A)
        rows = pl.ds(pl.multiple_of(a * CH, CH), CH)
        full = conv[n, rows, :] + gain * mixed[n, rows, :]
        o_gout[n, a] = (cot[n, a].astype(F32) * full).astype(LOW)
        full = back[n, rows, :] + gain * inner[n, rows, :]
        o_val[n, a] = (full * gin[n, a].astype(F32)).astype(LOW)
        o_gin[n, a] = (full * val[n, a].astype(F32)).astype(LOW)
        return carry

    lax.fori_loop(0, 2 * A, finish, 0, unroll=8)


def gradient_kernel(
    grad_all, raw_all, skip_part, w_mid, w_out, rate, feat, act1, act2, act3, der1, der2, der3,
    g_skip, g_in, g_bin, g_mid, g_bmid, g_out, g_rate,
    parts, acc_in, acc_mid0, acc_mid1, acc_out, acc_rate, share, first, second, third, sums,
    send_a, recv_a, send_b, recv_b, send_c, recv_c, send_d, recv_d,
):
    chan, seq = lax.axis_index("chan"), lax.axis_index("seq")
    barrier = greet(True, True)
    pl.semaphore_wait(barrier, NSEQ - 1 + NCHAN - 1)

    def seq_peer(d):
        return (chan, lax.rem(seq + d, NSEQ))

    def make_a(d):
        to = lax.rem(seq + d, NSEQ)
        return pltpu.make_async_remote_copy(
            src_ref=grad_all.at[pl.ds(to * ABLK, ABLK)], dst_ref=parts.at[d],
            send_sem=send_a.at[d], recv_sem=recv_a.at[d], device_id=seq_peer(d), device_id_type=MESH,
        )

    exchange("seq", NSEQ, make_a)()
    start = seq * ABLK

    def fold(i, carry):
        total = grad_all[start + i]
        for d in range(1, NSEQ):
            total = total + parts[d, i]
        parts[0, i] = total
        return carry

    lax.fori_loop(0, ABLK, fold, 0)
    net_backward(
        lambda i: raw_all[start + i], lambda i: parts[0, i], w_mid, w_out, rate, seq, chan,
        feat, act1, act2, act3, der1, der2, der3,
        acc_in, acc_mid0, acc_mid1, acc_out, acc_rate,
    )
    lane = lax.broadcasted_iota(jnp.int32, (CH, B), 1)
    own = jnp.concatenate([acc_out[...], jnp.zeros((CH, 64), F32)], axis=1)
    own = jnp.where(lane == 64, acc_rate[...], own)
    own = jnp.where(lane == 65, skip_part[...], own)
    for s in range(NSEQ):
        share[s, :, 0:72] = acc_mid0[8 * s : 8 * s + 8, :]
        share[s, :, 72:128] = jnp.zeros((8, 56), F32)
        share[s, :, 128:200] = acc_mid1[8 * s : 8 * s + 8, :]
        share[s, :, 200:256] = jnp.zeros((8, 56), F32)
        share[s, :, 256:296] = acc_in[8 * s : 8 * s + 8, :]
        share[s, :, 296:384] = jnp.zeros((8, 88), F32)
        share[s, :, 384:512] = own

    def make_b(d):
        to = lax.rem(seq + d, NSEQ)
        return pltpu.make_async_remote_copy(
            src_ref=share.at[to], dst_ref=first.at[d],
            send_sem=send_b.at[d], recv_sem=recv_b.at[d], device_id=seq_peer(d), device_id_type=MESH,
        )

    exchange("seq", NSEQ, make_b)()
    total = share[seq]
    for d in range(1, NSEQ):
        total = total + first[d]
    second[chan] = total
    factor = 1.0 / math.sqrt(16 * L)
    g_skip[...] = to_row(total[:, 449:450]) * factor

    def make_c(d):
        return pltpu.make_async_remote_copy(
            src_ref=second.at[chan], dst_ref=second.at[chan],
            send_sem=send_c.at[d], recv_sem=recv_c.at[d],
            device_id=(lax.rem(chan + d, NCHAN), seq), device_id_type=MESH,
        )

    exchange("chan", NCHAN, make_c)()
    total = second[0, :, 0:384]
    for c in range(1, NCHAN):
        total = total + second[c, :, 0:384]
    third[seq] = total * factor
    for c in range(NCHAN):
        g_out[8 * c : 8 * c + 8, :] = second[c, :, 384:448] * factor
        sums[8 * c : 8 * c + 8, :] = second[c, :, 384:512] * factor
    g_rate[...] = to_row(sums[:, 64:65])

    def make_d(d):
        return pltpu.make_async_remote_copy(
            src_ref=third.at[seq], dst_ref=third.at[seq],
            send_sem=send_d.at[d], recv_sem=recv_d.at[d], device_id=seq_peer(d), device_id_type=MESH,
        )

    exchange("seq", NSEQ, make_d)()
    hidden = jnp.concatenate([third[s] for s in range(NSEQ)], axis=0)
    g_mid[0] = hidden[:, 0:64]
    g_mid[1] = hidden[:, 128:192]
    g_in[...] = hidden[:, 256:289]
    g_bin[...] = to_row(hidden[:, 289:290])
    g_bmid[0:1, :] = to_row(hidden[:, 64:65])
    g_bmid[1:2, :] = to_row(hidden[:, 192:193])


def sds(shape, dtype=F32):
    return jax.ShapeDtypeStruct(shape, dtype)


VM = pl.BlockSpec(memory_space=pltpu.VMEM)
DMA = pltpu.SemaphoreType.DMA


def to_natural(x):
    return x.reshape(2, CH, A, B).transpose(0, 2, 1, 3)


def from_natural(x):
    return x.transpose(0, 2, 1, 3).reshape(2, CH, L)


def local(
    value, gate_in, gate_out, cotangent, skip_gain,
    weight_in, bias_in, weight_mid, bias_mid, weight_out, decay_rate,
):
    freq, off = row_constants()
    w1, w1t, fwd, inv, turn = transform_tables()
    rate = decay_rate.reshape(1, 128)
    saved = [sds((40, TB)), sds((72, TB)), sds((72, TB))] + [sds((64, TB))] * 4
    raw_all, *kept = pl.pallas_call(
        filter_kernel,
        out_shape=[sds((A, CH, B))] + saved,
        in_specs=[VM] * 8,
        out_specs=[VM] * 8,
        scratch_shapes=[DMA((NSEQ,)), DMA((NSEQ,))],
        compiler_params=pltpu.CompilerParams(
            collective_id=0, has_side_effects=True, vmem_limit_bytes=24 << 20
        ),
        name="filter_gather",
    )(freq, off, weight_in, bias_in.reshape(1, 64), weight_mid, bias_mid, weight_out, rate)
    big = sds((2, A, CH, B), LOW)
    o_val, o_gin, o_gout, grad_all, skip_part = pl.pallas_call(
        conv_kernel,
        out_shape=[big, big, big, sds((A, CH, B)), sds((CH, B))],
        in_specs=[VM] * 11,
        out_specs=[VM] * 5,
        scratch_shapes=[
            pltpu.VMEM((2, A * CH, B), F32),
            pltpu.VMEM((2, A * CH, B), F32),
            pltpu.VMEM((CH, 2, A, 2 * B), F32),
            pltpu.VMEM((CH, 2, A, 2 * B), F32),
            pltpu.VMEM((A * CH, B), F32),
            pltpu.VMEM((A * CH, B), F32),
            pltpu.VMEM((2, A * CH, B), F32),
            pltpu.VMEM((2, A * CH, B), F32),
        ],
        compiler_params=pltpu.CompilerParams(vmem_limit_bytes=50 << 20),
        name="transforms",
    )(
        to_natural(value), to_natural(gate_in), to_natural(gate_out), to_natural(cotangent),
        raw_all, skip_gain.reshape(1, CH), w1, w1t, fwd, inv, turn,
    )
    g_skip, g_in, g_bin, g_mid, g_bmid, g_out, g_rate = pl.pallas_call(
        gradient_kernel,
        out_shape=[
            sds((1, CH)), sds((64, 33)), sds((1, 64)), sds((2, 64, 64)), sds((2, 64)),
            sds((128, 64)), sds((1, 128)),
        ],
        in_specs=[VM] * 13,
        out_specs=[VM] * 7,
        scratch_shapes=[
            pltpu.VMEM((NSEQ, ABLK, CH, B), F32),
            pltpu.VMEM((64, 40), F32),
            pltpu.VMEM((64, 72), F32),
            pltpu.VMEM((64, 72), F32),
            pltpu.VMEM((CH, 64), F32),
            pltpu.VMEM((CH, 1), F32),
            pltpu.VMEM((NSEQ, 8, 512), F32),
            pltpu.VMEM((NSEQ, 8, 512), F32),
            pltpu.VMEM((NCHAN, 8, 512), F32),
            pltpu.VMEM((NSEQ, 8, 384), F32),
            pltpu.VMEM((128, 128), F32),
            DMA((NSEQ,)), DMA((NSEQ,)), DMA((NSEQ,)), DMA((NSEQ,)),
            DMA((NCHAN,)), DMA((NCHAN,)), DMA((NSEQ,)), DMA((NSEQ,)),
        ],
        compiler_params=pltpu.CompilerParams(
            collective_id=1, has_side_effects=True, vmem_limit_bytes=32 << 20
        ),
        name="filter_gradients",
    )(grad_all, raw_all, skip_part, weight_mid, weight_out, rate, *kept)
    return (
        from_natural(o_val), from_natural(o_gin), from_natural(o_gout), g_skip.reshape(CH),
        g_in, g_bin.reshape(64), g_mid, g_bmid, g_out, g_rate.reshape(128),
    )


def solution(mesh):
    return jax.shard_map(
        local,
        mesh=mesh,
        in_specs=(
            P("seq", "chan", None), P("seq", "chan", None), P("seq", "chan", None), P("seq", "chan", None),
            P("chan"), P(), P(), P(), P(), P(), P(),
        ),
        out_specs=(
            P("seq", "chan", None), P("seq", "chan", None), P("seq", "chan", None),
            P("chan"), P(), P(), P(), P(), P(), P(),
        ),
        check_vma=False,
    )
```

```python
import functools
import math

import jax
import jax.numpy as jnp
import numpy as np
from jax import lax
from jax.experimental import pallas as pl
from jax.experimental.pallas import tpu as pltpu
from jax.sharding import PartitionSpec as P

EPSILON = 1e-06
HIGHEST = lax.Precision.HIGHEST
L = 32768
A = 256
B = 128
CH = 8
NSEQ = 8
NCHAN = 16
ABLK = A // NSEQ
TB = L // NSEQ
CHUNK = 1024
LOW = jnp.bfloat16
F32 = jnp.float32
MESH = pl.DeviceIdType.MESH


def band_table(length, bands):
    highest = length / 4.0
    return np.array(
        [math.floor(highest ** (number / (bands - 1)) + 0.5) for number in range(bands)], np.int64
    )


def row_constants():
    freq = np.zeros((48, 128), np.int32)
    off = np.zeros((48, 128), np.int32)
    bands = band_table(L, 16)
    freq[1:17] = bands[:, None]
    off[1:17] = L // 4
    freq[17:33] = bands[:, None]
    return np.stack([freq, off])


def transform_tables():
    k = np.arange(A)[:, None]
    rows = 2.0 * np.pi * (((4 * k + 1) * np.arange(A)[None, :]) % 1024) / 1024.0
    w1 = np.concatenate([np.cos(rows), -np.sin(rows)], axis=0)
    turn = 2.0 * np.pi * (((4 * k + 1) * np.arange(B)[None, :]) % (4 * L)) / (4.0 * L)
    q = np.arange(B)
    cols = 2.0 * np.pi * ((q[:, None] * q[None, :]) % B) / B
    c, s = np.cos(cols), np.sin(cols)
    fwd = np.block([[c, -s], [s, c]])
    inv = np.block([[c, s], [-s, c]])
    low = np.dtype(LOW)
    return (
        w1.astype(low),
        w1.T.astype(low),
        fwd.astype(low),
        inv.astype(low),
        np.stack([np.cos(turn), np.sin(turn)]).astype(np.float32),
    )


def poly_fit():
    x = (np.cos(np.pi * (np.arange(64) + 0.5) / 64) + 1) / 2 * (np.pi / 2 * 1.002) ** 2
    r = np.sqrt(x)
    sin_c = np.polynomial.polynomial.polyfit(x, np.sin(r) / r, 5)
    cos_c = np.polynomial.polynomial.polyfit(x, np.cos(r), 6)
    return [float(v) for v in sin_c], [float(v) for v in cos_c]


SIN_C, COS_C = poly_fit()


def horner(x, coefs):
    acc = jnp.full_like(x, coefs[-1])
    for value in coefs[-2::-1]:
        acc = acc * x + value
    return acc


def sin_small(r):
    return r * horner(r * r, SIN_C)


def sin_cos(z):
    n = jnp.floor(z * (1.0 / math.pi) + 0.5)
    r = z - n * 3.140625
    r = r - n * 9.67653589793e-4
    half = n * 0.5
    sign = 1.0 - 4.0 * (half - jnp.floor(half))
    r2 = r * r
    return sign * (r * horner(r2, SIN_C)), sign * horner(r2, COS_C)


def dot_full(x, y):
    return jnp.dot(x, y, precision=HIGHEST, preferred_element_type=F32)


def dot_nt(x, y, precision=None):
    return lax.dot_general(x, y, (((1,), (1,)), ((), ())), precision=precision, preferred_element_type=F32)


def dot_tn(x, y, precision=None):
    return lax.dot_general(x, y, (((0,), (0,)), ((), ())), precision=precision, preferred_element_type=F32)


def low_dot(x, y):
    return jnp.dot(x, y, preferred_element_type=F32)


def split(x):
    hi = x.astype(LOW)
    return hi, (x - hi.astype(F32)).astype(LOW)


def iota(shape, dim):
    return lax.broadcasted_iota(jnp.int32, shape, dim)


def to_column(row, size, shift):
    n = row.shape[1]
    pick = iota((size, n), 0) + shift == iota((size, n), 1)
    return jnp.sum(jnp.where(pick, jnp.broadcast_to(row, (size, n)), 0.0), axis=1, keepdims=True)


def to_row(col):
    n = col.shape[0]
    pick = iota((n, n), 0) == iota((n, n), 1)
    return jnp.sum(jnp.where(pick, jnp.broadcast_to(col, (n, n)), 0.0), axis=0, keepdims=True)


def repeat_matrix(rows, period, times):
    shape = (rows, period * times)
    j = iota(shape, 1)
    hit = j == iota(shape, 0)
    for m in range(1, times):
        hit = hit | (j == iota(shape, 0) + m * period)
    return jnp.where(hit, 1.0, 0.0)


def hi_hi_lo(w, period):
    hi = w.astype(LOW).astype(F32)
    lane = iota(w.shape, 1)
    out = jnp.where(lane < 2 * period, hi, jnp.where(lane < 3 * period, w - hi, 0.0))
    return out.astype(LOW)


class Refs:
    def __init__(self, **refs):
        self.__dict__.update(refs)


def prepare_weights(r, chan):
    first = jnp.where(iota((8, 64), 0) == 1, jnp.broadcast_to(r.b_in[...], (8, 64)), 0.0)
    r.w_pad[0:32, :] = r.w_in[0:32, :]
    r.w_pad[32:40, :] = jnp.where(iota((8, 64), 0) == 0, jnp.broadcast_to(r.w_in[32:33, :], (8, 64)), first)
    r.w_pad[40:48, :] = jnp.zeros((8, 64), F32)
    r.k_in[...] = hi_hi_lo(dot_tn(r.w_pad[...], repeat_matrix(48, 48, 3), HIGHEST), 48)
    rep = repeat_matrix(64, 64, 3)
    for i in range(2):
        w = r.w_mid[i]
        r.k_mid[i] = hi_hi_lo(dot_full(w, rep), 64)
        r.k_back[i] = hi_hi_lo(dot_tn(w, rep, HIGHEST), 64)
    own = jnp.where(iota((CH, 128), 1) == iota((CH, 128), 0) + chan * CH, 1.0, 0.0)
    w_own = dot_nt(own, r.w_out[...], HIGHEST)
    r.k_out[...] = hi_hi_lo(dot_full(w_own, rep), 64)
    r.k_outback[...] = hi_hi_lo(dot_tn(w_own, repeat_matrix(CH, CH, 4), HIGHEST), CH)
    r.rate_col[...] = jnp.broadcast_to(to_column(r.rate[...], CH, chan * CH), (CH, 128))
    r.bias_col[0] = jnp.broadcast_to(to_column(r.b_mid[0:1, :], 64, 0), (64, 128))
    r.bias_col[1] = jnp.broadcast_to(to_column(r.b_mid[1:2, :], 64, 0), (64, 128))


def wide(block, times):
    return jnp.concatenate([block] * times, axis=1)


def fraction(seq, base):
    pos = seq * TB + base + iota((CH, CHUNK), 1)
    return pos.astype(F32) * (1.0 / L)


def net_forward(r, seq):
    per = CHUNK // 128

    def step(j, carry):
        base = pl.multiple_of(j * CHUNK, CHUNK)
        lanes = pl.ds(base, CHUNK)
        pos = seq * TB + base + iota((48, CHUNK), 1)
        row = iota((48, CHUNK), 0)
        phase = ((wide(r.bands[0], per) * pos + (wide(r.bands[1], per) + L // 2)) & (L - 1)) - L // 2
        phase = jnp.where(phase > L // 4, L // 2 - phase, phase)
        phase = jnp.where(phase < -(L // 4), -(L // 2) - phase, phase)
        wave = sin_small(phase.astype(F32) * (2.0 * math.pi / L))
        frac = pos.astype(F32) * (1.0 / L)
        hi, lo = split(jnp.where(row == 0, frac, jnp.where(row == 33, 1.0, wave)))
        r.feat[0:48, lanes] = hi
        r.feat[48:64, lanes] = jnp.zeros((16, CHUNK), LOW)
        r.feat[64:112, lanes] = lo
        r.feat[112:128, lanes] = jnp.zeros((16, CHUNK), LOW)
        z = low_dot(r.k_in[...], jnp.concatenate([hi, lo, hi], axis=0))
        for layer in range(3):
            s, c = sin_cos(z)
            r.der[layer, :, lanes] = c
            hi, lo = split(s)
            r.act[layer, 0:64, lanes] = hi
            r.act[layer, 64:128, lanes] = lo
            x = jnp.concatenate([hi, lo, hi], axis=0)
            if layer < 2:
                z = low_dot(r.k_mid[layer], x) + wide(r.bias_col[layer], per)
        raw = low_dot(r.k_out[...], x) * jnp.exp(-wide(r.rate_col[...], per) * frac[0:CH, :])
        for i in range(per):
            r.raw_all[seq * ABLK + j * per + i] = raw[:, 128 * i : 128 * i + 128]
        return carry

    lax.fori_loop(0, TB // CHUNK, step, 0)


def net_backward(r, seq):
    per = CHUNK // 128
    r.acc[...] = jnp.zeros_like(r.acc)
    r.acc_out[...] = jnp.zeros_like(r.acc_out)
    r.acc_bias[...] = jnp.zeros_like(r.acc_bias)
    r.acc_rate[...] = jnp.zeros_like(r.acc_rate)

    def lane_sum(x):
        total = x[:, 0:128]
        for i in range(1, per):
            total = total + x[:, 128 * i : 128 * i + 128]
        return total

    def step(j, carry):
        lanes = pl.ds(pl.multiple_of(j * CHUNK, CHUNK), CHUNK)
        start = seq * ABLK + j * per
        grad = jnp.concatenate([r.total[j * per + i] for i in range(per)], axis=1)
        raw = jnp.concatenate([r.raw_all[start + i] for i in range(per)], axis=1)
        frac = fraction(seq, j * CHUNK)
        r.acc_rate[...] -= lane_sum(grad * raw * frac)
        shaped = grad * jnp.exp(-wide(r.rate_col[...], per) * frac)
        hi = shaped.astype(LOW).astype(F32)
        lo = shaped - hi
        pair = jnp.concatenate([hi, lo], axis=0).astype(LOW)
        r.acc_out[...] += dot_nt(pair, r.act[2, :, lanes])
        d = low_dot(r.k_outback[...], jnp.concatenate([hi, lo, hi, jnp.zeros_like(hi)], axis=0).astype(LOW))
        for layer in (2, 1, 0):
            d = d * r.der[layer, :, lanes]
            hi, lo = split(d)
            pair = jnp.concatenate([hi, lo], axis=0)
            if layer:
                r.acc_bias[layer - 1] += lane_sum(d)
                r.acc[layer] += dot_nt(pair, r.act[layer - 1, :, lanes])
                d = low_dot(r.k_back[layer - 1], jnp.concatenate([hi, lo, hi], axis=0))
            else:
                r.acc[0] += dot_nt(pair, r.feat[:, lanes])
        return carry

    lax.fori_loop(0, TB // CHUNK, step, 0)


def fold_halves(x):
    n = x.shape[0] // 2
    total = x[0:n] + x[n:]
    return total + pltpu.roll(total, 64, 1)


def pack_shares(r):
    lane = iota((64, 128), 1)
    r.block[0] = jnp.where(lane < 64, fold_halves(r.acc[1]), fold_halves(r.acc[2]))
    block = fold_halves(r.acc[0])
    block = jnp.where(lane == 34, jnp.sum(r.acc_bias[0], axis=1, keepdims=True), block)
    r.block[1] = jnp.where(lane == 35, jnp.sum(r.acc_bias[1], axis=1, keepdims=True), block)
    lane = iota((CH, 128), 1)
    own = pltpu.roll(fold_halves(r.acc_out[...]), 48, 1)
    own = jnp.where(lane == 112, jnp.sum(r.acc_rate[...], axis=1, keepdims=True), own)
    own = jnp.where(lane == 113, r.skip_part[...], own)

    def place(s, carry):
        rows = pl.ds(pl.multiple_of(8 * s, 8), 8)
        r.share[s, :, 0:128] = r.block[0, rows, :]
        r.share[s, :, 128:256] = jnp.where(lane < 48, r.block[1, rows, :], own)
        return carry

    lax.fori_loop(0, NSEQ, place, 0)


def to_low(x):
    return x.astype(LOW)


def channel_rows(c):
    return pl.ds(c, A, stride=CH)


def forward_pair(r, x):
    tc, ts = r.turn[0], r.turn[1]
    g = low_dot(r.w1[...], x)
    parts = []
    for n in range(2):
        re, im = g[0:A, n * B : n * B + B], g[A:, n * B : n * B + B]
        parts.append(jnp.concatenate([to_low(re * tc + im * ts), to_low(im * tc - re * ts)], axis=1))
    f = low_dot(jnp.concatenate(parts, axis=0), r.fwd[...])
    return f[0:A], f[A:]


def inverse_pair(r, specs):
    tc, ts = r.turn[0], r.turn[1]
    s = jnp.concatenate([jnp.concatenate([to_low(re), to_low(im)], axis=1) for re, im in specs], axis=0)
    t = low_dot(s, r.inv[...])
    cols = []
    for n in range(2):
        re, im = t[n * A : n * A + A, 0:B], t[n * A : n * A + A, B:]
        cols.append(jnp.concatenate([to_low(re * tc - im * ts), to_low(re * ts + im * tc)], axis=0))
    y = low_dot(r.w1t[...], jnp.concatenate(cols, axis=1))
    return y[:, 0:B], y[:, B:]


BLK = 16
VMEM_MAIN = 56 << 20


def gate_products(r, n):
    def step(j, acc):
        part = pl.ds(j * BLK, BLK)
        rows = pl.ds(pl.multiple_of(j * (BLK * CH), BLK * CH), BLK * CH)
        m = r.val[n, part].astype(F32) * r.gin[n, part].astype(F32)
        g = r.cot[n, part].astype(F32) * r.gout[n, part].astype(F32)
        r.mixed[n, rows, :] = m.reshape(BLK * CH, B)
        r.inner[n, rows, :] = g.reshape(BLK * CH, B)
        return acc + jnp.sum(m * g, axis=0)

    return lax.fori_loop(0, A // BLK, step, jnp.zeros((CH, B), F32))


def spectra(r, p):
    cross = []
    for i in range(2):
        c = 2 * p + i
        rows = channel_rows(c)
        fm = forward_pair(r, jnp.concatenate([to_low(r.mixed[n, rows, :]) for n in range(2)], axis=1))
        fg = forward_pair(r, jnp.concatenate([to_low(r.inner[n, rows, :]) for n in range(2)], axis=1))
        re = im = None
        for n in range(2):
            r.f_mixed[c, n] = fm[n]
            r.f_inner[c, n] = fg[n]
            mr, mi = fm[n][:, 0:B], fm[n][:, B:]
            gr, gi = fg[n][:, 0:B], fg[n][:, B:]
            pr, pi = mr * gr + mi * gi, mr * gi - mi * gr
            re, im = (pr, pi) if re is None else (re + pr, im + pi)
        cross.append((re, im))
    ys = inverse_pair(r, cross)
    for i in range(2):
        r.gk[channel_rows(2 * p + i), :] = ys[i]


def normalize(r):
    def rows_of(j):
        return pl.ds(pl.multiple_of(j * (BLK * CH), BLK * CH), BLK * CH)

    def sums(j, carry):
        square, along = carry
        x = r.raw_all[pl.ds(j * BLK, BLK)]
        y = r.gk[rows_of(j), :].reshape(BLK, CH, B)
        return square + jnp.sum(x * x, axis=0), along + jnp.sum(x * y, axis=0)

    zero = jnp.zeros((CH, B), F32)
    square, along = lax.fori_loop(0, A // BLK, sums, (zero, zero))
    norm = jnp.sqrt(jnp.sum(square, axis=1, keepdims=True) + EPSILON)
    along = jnp.sum(along, axis=1, keepdims=True) * (1.0 / L)
    recip = jnp.broadcast_to(1.0 / norm, (CH, B))
    scale_gk = (recip * (1.0 / L))[None]
    scale_raw = jnp.broadcast_to(along / (norm * norm * norm), (CH, B))[None]

    def settle(j, carry):
        part = pl.ds(j * BLK, BLK)
        x = r.raw_all[part]
        r.grad_all[part] = r.gk[rows_of(j), :].reshape(BLK, CH, B) * scale_gk - x * scale_raw
        r.kern[rows_of(j), :] = (x * recip[None]).reshape(BLK * CH, B)
        return carry

    lax.fori_loop(0, A // BLK, settle, 0)


def filter_products(r, p):
    fk = forward_pair(r, jnp.concatenate([to_low(r.kern[channel_rows(2 * p + i), :]) for i in range(2)], axis=1))
    for i in range(2):
        c = 2 * p + i
        rows = channel_rows(c)
        kr, ki = fk[i][:, 0:B] * (1.0 / L), fk[i][:, B:] * (1.0 / L)
        specs = []
        for n in range(2):
            mr, mi = r.f_mixed[c, n, :, 0:B], r.f_mixed[c, n, :, B:]
            specs.append((mr * kr - mi * ki, mr * ki + mi * kr))
        ys = inverse_pair(r, specs)
        for n in range(2):
            r.conv[n, rows, :] = ys[n]
        specs = []
        for n in range(2):
            gr, gi = r.f_inner[c, n, :, 0:B], r.f_inner[c, n, :, B:]
            specs.append((gr * kr + gi * ki, gi * kr - gr * ki))
        ys = inverse_pair(r, specs)
        for n in range(2):
            r.back[n, rows, :] = ys[n]


def finish(r, n):
    gain = jnp.broadcast_to(to_column(r.skip[...], CH, 0), (CH, B))[None]

    def step(j, carry):
        part = pl.ds(j * BLK, BLK)
        rows = pl.ds(pl.multiple_of(j * (BLK * CH), BLK * CH), BLK * CH)
        shape = (BLK, CH, B)
        full = r.conv[n, rows, :].reshape(shape) + gain * r.mixed[n, rows, :].reshape(shape)
        r.o_gout[n, part] = to_low(r.cot[n, part].astype(F32) * full)
        full = r.back[n, rows, :].reshape(shape) + gain * r.inner[n, rows, :].reshape(shape)
        r.o_val[n, part] = to_low(full * r.gin[n, part].astype(F32))
        r.o_gin[n, part] = to_low(full * r.val[n, part].astype(F32))
        return carry

    lax.fori_loop(0, A // BLK, step, 0)


SMALL = ("bands", "w_in", "b_in", "w_mid", "b_mid", "w_out", "rate", "skip")
TABLES = ("w1", "w1t", "fwd", "inv", "turn")
LARGE = ("val", "gin", "cot", "gout")
OUTS = ("o_val", "o_gin", "o_gout", "second", "third", "g_skip")
BIG = (2, A, CH, B)
FULL = (2, A * CH, B)
SCRATCH = {
    "bands": ((2, 48, 128), jnp.int32),
    "w_in": ((33, 64), F32),
    "b_in": ((1, 64), F32),
    "w_mid": ((2, 64, 64), F32),
    "b_mid": ((2, 64), F32),
    "w_out": ((64, 128), F32),
    "rate": ((1, 128), F32),
    "skip": ((1, CH), F32),
    "w1": ((2 * A, A), LOW),
    "w1t": ((A, 2 * A), LOW),
    "fwd": ((2 * B, 2 * B), LOW),
    "inv": ((2 * B, 2 * B), LOW),
    "turn": ((2, A, B), F32),
    "val": (BIG, LOW),
    "gin": (BIG, LOW),
    "cot": (BIG, LOW),
    "gout": (BIG, LOW),
    "w_pad": ((48, 64), F32),
    "k_in": ((64, 144), LOW),
    "k_mid": ((2, 64, 192), LOW),
    "k_back": ((2, 64, 192), LOW),
    "k_out": ((CH, 192), LOW),
    "k_outback": ((64, 4 * CH), LOW),
    "rate_col": ((CH, 128), F32),
    "bias_col": ((2, 64, 128), F32),
    "feat": ((128, TB), LOW),
    "act": ((3, 128, TB), LOW),
    "der": ((3, 64, TB), F32),
    "raw_all": ((A, CH, B), F32),
    "grad_all": ((A, CH, B), F32),
    "total": ((ABLK, CH, B), F32),
    "half": ((2, 2, ABLK // 2, CH, B), F32),
    "side": ((2, 2, ABLK, CH, B), F32),
    "side_out": ((2, 2, ABLK, CH, B), F32),
    "pair": ((2, ABLK, CH, B), F32),
    "mixed": (FULL, F32),
    "inner": (FULL, F32),
    "f_mixed": ((CH, 2, A, 2 * B), F32),
    "f_inner": ((CH, 2, A, 2 * B), F32),
    "gk": ((A * CH, B), F32),
    "kern": ((A * CH, B), F32),
    "conv": (FULL, F32),
    "back": (FULL, F32),
    "acc": ((3, 128, 128), F32),
    "acc_out": ((16, 128), F32),
    "acc_bias": ((2, 64, 128), F32),
    "acc_rate": ((CH, 128), F32),
    "skip_part": ((CH, 1), F32),
    "block": ((2, 64, 128), F32),
    "share": ((NSEQ, 8, 256), F32),
    "first": ((NSEQ, 8, 256), F32),
}
N_LOCAL = len(SMALL) + len(TABLES) + len(LARGE)


def main_kernel(*refs):
    ins = refs[:N_LOCAL]
    outs = refs[N_LOCAL : N_LOCAL + len(OUTS)]
    names = list(SCRATCH)
    scratch = refs[N_LOCAL + len(OUTS) :]
    r = Refs(**dict(zip(OUTS, outs)), **dict(zip(names, scratch)))
    (load_sem, ag_send, ag_recv, rs_send, rs_recv, sem_b, recv_b, sem_c, recv_c, sem_d, recv_d) = scratch[len(names) :]
    chan, seq = lax.axis_index("chan"), lax.axis_index("seq")
    barrier = pltpu.get_barrier_semaphore()

    def signal(device):
        pl.semaphore_signal(barrier, inc=1, device_id=device, device_id_type=MESH)

    def hail_seq(d, carry):
        signal((chan, lax.rem(seq + d, NSEQ)))
        return carry

    def hail_chan(d, carry):
        signal((lax.rem(chan + d, NCHAN), seq))
        return carry

    loads = {}
    for i, name in enumerate(SMALL + TABLES + LARGE):
        loads[name] = pltpu.make_async_copy(ins[i], getattr(r, name), load_sem.at[i])
    for name in SMALL:
        loads[name].start()
    lax.fori_loop(1, NSEQ, hail_seq, 0)
    lax.fori_loop(1, NCHAN, hail_chan, 0)
    for name in LARGE + TABLES:
        loads[name].start()
    for name in SMALL:
        loads[name].wait()

    prepare_weights(r, chan)
    net_forward(r, seq)
    pl.semaphore_wait(barrier, NSEQ - 1 + NCHAN - 1)

    x, z = lax.div(seq, 2), lax.rem(seq, 2)
    xr, xl, xo = lax.rem(x + 1, 4), lax.rem(x + 3, 4), lax.rem(x + 2, 4)
    other = 1 - z
    to_z, to_r, to_l = (chan, 2 * x + other), (chan, 2 * xr + z), (chan, 2 * xl + z)
    HALF = ABLK // 2

    def gather(i, row, count, device):
        part = r.raw_all.at[pl.ds(row, count)]
        return pltpu.make_async_remote_copy(
            src_ref=part, dst_ref=part, send_sem=ag_send.at[i], recv_sem=ag_recv.at[i],
            device_id=device, device_id_type=MESH,
        )

    def row_of(xx, zz):
        return (2 * xx + zz) * ABLK

    ag = [gather(0, row_of(x, z), ABLK, to_z), gather(1, row_of(x, z), ABLK, to_r), gather(2, row_of(x, z), ABLK, to_l)]
    for copy in ag:
        copy.start()

    for name in LARGE:
        loads[name].wait()
    acc = gate_products(r, 0)
    acc = acc + gate_products(r, 1)
    r.skip_part[...] = jnp.sum(acc, axis=1, keepdims=True)

    ag[0].wait_recv()
    ag += [gather(3, row_of(x, other), ABLK, to_r), gather(4, row_of(x, other), ABLK, to_l)]
    ag[3].start()
    ag[4].start()
    ag[1].wait_recv()
    ag += [gather(5, row_of(xl, z), HALF, to_r)]
    ag[5].start()
    ag[2].wait_recv()
    ag += [gather(6, row_of(xr, z) + HALF, HALF, to_l)]
    ag[6].start()
    for name in TABLES:
        loads[name].wait()

    def loop(body, start, stop):
        def step(p, carry):
            body(r, p)
            return carry

        lax.fori_loop(start, stop, step, 0)

    loop(spectra, 0, 3)
    ag[3].wait_recv()
    ag += [gather(7, row_of(xl, other), HALF, to_r)]
    ag[7].start()
    ag[4].wait_recv()
    ag += [gather(8, row_of(xr, other) + HALF, HALF, to_l)]
    ag[8].start()
    loop(spectra, 3, 4)
    for i in (5, 6, 7, 8):
        ag[i].wait_recv()

    normalize(r)

    def send(i, src, dst, device):
        return pltpu.make_async_remote_copy(
            src_ref=src, dst_ref=dst, send_sem=rs_send.at[i], recv_sem=rs_recv.at[i],
            device_id=device, device_id_type=MESH,
        )

    zs = (other, z)
    rs = []
    for w in range(2):
        far = row_of(xo, zs[w])
        rs += [
            send(2 * w, r.grad_all.at[pl.ds(far, HALF)], r.half.at[w, 0], to_r),
            send(2 * w + 1, r.grad_all.at[pl.ds(far + HALF, HALF)], r.half.at[w, 1], to_l),
        ]
    for copy in rs:
        copy.start()

    def add_half(w):
        rs[2 * w].wait_recv()
        near = row_of(xr, zs[w])
        r.side_out[w, 0, 0:HALF] = r.grad_all[pl.ds(near, HALF)] + r.half[w, 0]
        r.side_out[w, 0, HALF:] = r.grad_all[pl.ds(near + HALF, HALF)]
        rs[2 * w + 1].wait_recv()
        near = row_of(xl, zs[w])
        r.side_out[w, 1, 0:HALF] = r.grad_all[pl.ds(near, HALF)]
        r.side_out[w, 1, HALF:] = r.grad_all[pl.ds(near + HALF, HALF)] + r.half[w, 1]
        for i, device in enumerate((to_r, to_l)):
            copy = send(4 + 2 * w + i, r.side_out.at[w, i], r.side.at[w, i], device)
            copy.start()
            rs.append(copy)

    def own_sum(w):
        rs[4 + 2 * w].wait_recv()
        rs[5 + 2 * w].wait_recv()
        return r.grad_all[pl.ds(row_of(x, zs[w]), ABLK)] + r.side[w, 0] + r.side[w, 1]

    loop(filter_products, 0, 1)
    add_half(0)
    loop(filter_products, 1, 2)
    add_half(1)
    loop(filter_products, 2, 4)
    r.pair[0] = own_sum(0)
    rs.append(send(8, r.pair.at[0], r.pair.at[1], to_z))
    rs[8].start()
    r.total[...] = own_sum(1)
    finish(r, 0)
    rs[8].wait_recv()
    r.total[...] += r.pair[1]
    for copy in ag + rs:
        copy.wait_send()

    net_backward(r, seq)
    pack_shares(r)

    def run(size, make):
        def start(d, carry):
            make(d).start()
            return carry

        def wait(d, carry):
            make(d).wait()
            return carry

        lax.fori_loop(1, size, start, 0)
        return lambda: lax.fori_loop(1, size, wait, 0)

    def seq_peer(d):
        return (chan, lax.rem(seq + d, NSEQ))

    def make_b(d):
        return pltpu.make_async_remote_copy(
            src_ref=r.share.at[lax.rem(seq + d, NSEQ)], dst_ref=r.first.at[d],
            send_sem=sem_b.at[d], recv_sem=recv_b.at[d], device_id=seq_peer(d), device_id_type=MESH,
        )

    def make_c(d):
        return pltpu.make_async_remote_copy(
            src_ref=r.second.at[chan], dst_ref=r.second.at[chan], send_sem=sem_c.at[d], recv_sem=recv_c.at[d],
            device_id=(lax.rem(chan + d, NCHAN), seq), device_id_type=MESH,
        )

    def make_d(d):
        return pltpu.make_async_remote_copy(
            src_ref=r.third.at[seq], dst_ref=r.third.at[seq], send_sem=sem_d.at[d], recv_sem=recv_d.at[d],
            device_id=seq_peer(d), device_id_type=MESH,
        )

    wait = run(NSEQ, make_b)
    finish(r, 1)
    wait()
    total = r.share[seq]
    for d in range(1, NSEQ):
        total = total + r.first[d]
    factor = 1.0 / math.sqrt(16 * L)
    total = total * factor
    r.second[chan] = total
    r.g_skip[...] = to_row(total[:, 241:242])
    run(NCHAN, make_c)()
    total = r.second[0]
    for c in range(1, NCHAN):
        total = total + r.second[c]
    r.third[seq] = total
    run(NSEQ, make_d)()


def write_kernel(
    i_val, i_gin, i_gout, second, third, skip,
    o_val, o_gin, o_gout, g_skip, g_in, g_bin, g_mid, g_bmid, g_out, g_rate, sems,
):
    copies = [
        pltpu.make_async_copy(src, dst, sems.at[i])
        for i, (src, dst) in enumerate(((i_val, o_val), (i_gin, o_gin), (i_gout, o_gout)))
    ]
    for copy in copies:
        copy.start()
    g_skip[...] = skip[...]
    hidden = third[...].reshape(64, 256)
    g_mid[0] = hidden[:, 0:64]
    g_mid[1] = pltpu.roll(hidden[:, 0:128], 64, 1)[:, 0:64]
    flat = jnp.transpose(hidden[:, 128:256])
    g_in[...] = flat[0:33, :]
    g_bin[...] = flat[33:34, :]
    g_bmid[...] = flat[34:36, :]
    own = jnp.transpose(second[...].reshape(128, 256)[:, 128:256])
    g_out[...] = own[48:112, :]
    g_rate[...] = own[112:113, :]
    for copy in copies:
        copy.wait()


def sds(shape, dtype=F32):
    return jax.ShapeDtypeStruct(shape, dtype)


VM = pl.BlockSpec(memory_space=pltpu.VMEM)
HB = pl.BlockSpec(memory_space=pl.ANY)
DMA = pltpu.SemaphoreType.DMA


def to_natural(x):
    return x.reshape(2, CH, A, B).transpose(0, 2, 1, 3)


def from_natural(x):
    return x.transpose(0, 2, 1, 3).reshape(2, CH, L)


def local(
    value, gate_in, gate_out, cotangent, skip_gain,
    weight_in, bias_in, weight_mid, bias_mid, weight_out, decay_rate,
):
    small = (
        row_constants(), weight_in.T, bias_in.reshape(1, 64), weight_mid, bias_mid, weight_out.T,
        decay_rate.reshape(1, 128), skip_gain.reshape(1, CH),
    )
    large = tuple(to_natural(x) for x in (value, gate_in, cotangent, gate_out))
    big = sds(BIG, LOW)
    o_val, o_gin, o_gout, second, third, g_skip = pl.pallas_call(
        main_kernel,
        out_shape=[big, big, big, sds((NCHAN, 8, 256)), sds((NSEQ, 8, 256)), sds((1, CH))],
        in_specs=[HB] * N_LOCAL,
        out_specs=[VM] * len(OUTS),
        scratch_shapes=[pltpu.VMEM(shape, dtype) for shape, dtype in SCRATCH.values()]
        + [
            DMA((N_LOCAL,)), DMA((9,)), DMA((9,)), DMA((9,)), DMA((9,)),
            DMA((NSEQ,)), DMA((NSEQ,)), DMA((NCHAN,)), DMA((NCHAN,)), DMA((NSEQ,)), DMA((NSEQ,)),
        ],
        compiler_params=pltpu.CompilerParams(
            collective_id=0, has_side_effects=True, vmem_limit_bytes=VMEM_MAIN
        ),
        name="hyena_backward",
    )(*small, *transform_tables(), *large)
    o_val, o_gin, o_gout, g_skip, g_in, g_bin, g_mid, g_bmid, g_out, g_rate = pl.pallas_call(
        write_kernel,
        out_shape=[
            big, big, big, sds((1, CH)), sds((33, 64)), sds((1, 64)), sds((2, 64, 64)), sds((2, 64)),
            sds((64, 128)), sds((1, 128)),
        ],
        in_specs=[HB] * 3 + [VM] * 3,
        out_specs=[HB] * 3 + [VM] * 7,
        scratch_shapes=[DMA((3,))],
        name="write_results",
    )(o_val, o_gin, o_gout, second, third, g_skip)
    return (
        from_natural(o_val), from_natural(o_gin), from_natural(o_gout), g_skip.reshape(CH),
        g_in.T, g_bin.reshape(64), g_mid, g_bmid, g_out.T, g_rate.reshape(128),
    )


def solution(mesh):
    return jax.shard_map(
        local,
        mesh=mesh,
        in_specs=(
            P("seq", "chan", None), P("seq", "chan", None), P("seq", "chan", None), P("seq", "chan", None),
            P("chan"), P(), P(), P(), P(), P(), P(),
        ),
        out_specs=(
            P("seq", "chan", None), P("seq", "chan", None), P("seq", "chan", None),
            P("chan"), P(), P(), P(), P(), P(), P(),
        ),
        check_vma=False,
    )
```

```python
import functools
import math

import jax
import jax.numpy as jnp
import numpy as np
from jax import lax
from jax.experimental import pallas as pl
from jax.experimental.pallas import tpu as pltpu
from jax.sharding import PartitionSpec as P

EPSILON = 1e-06
HIGHEST = lax.Precision.HIGHEST
L = 32768
A = 256
B = 128
CH = 8
NSEQ = 8
NCHAN = 16
ABLK = A // NSEQ
TB = L // NSEQ
CHUNK = 1024
LOW = jnp.bfloat16
F32 = jnp.float32
MESH = pl.DeviceIdType.MESH


def band_table(length, bands):
    highest = length / 4.0
    return np.array(
        [math.floor(highest ** (number / (bands - 1)) + 0.5) for number in range(bands)], np.int64
    )


def row_constants():
    freq = np.zeros((48, 128), np.int32)
    off = np.zeros((48, 128), np.int32)
    bands = band_table(L, 16)
    freq[1:17] = bands[:, None]
    off[1:17] = L // 4
    freq[17:33] = bands[:, None]
    return np.stack([freq, off])


def transform_tables():
    k = np.arange(A)[:, None]
    rows = 2.0 * np.pi * (((4 * k + 1) * np.arange(A)[None, :]) % 1024) / 1024.0
    w1 = np.concatenate([np.cos(rows), -np.sin(rows)], axis=0)
    turn = 2.0 * np.pi * (((4 * k + 1) * np.arange(B)[None, :]) % (4 * L)) / (4.0 * L)
    q = np.arange(B)
    cols = 2.0 * np.pi * ((q[:, None] * q[None, :]) % B) / B
    c, s = np.cos(cols), np.sin(cols)
    fwd = np.block([[c, -s], [s, c]])
    inv = np.block([[c, s], [-s, c]])
    low = np.dtype(LOW)
    return (
        w1.astype(low),
        w1.T.astype(low),
        fwd.astype(low),
        inv.astype(low),
        np.stack([np.cos(turn), np.sin(turn)]).astype(np.float32),
    )


def poly_fit():
    x = (np.cos(np.pi * (np.arange(64) + 0.5) / 64) + 1) / 2 * (np.pi / 2 * 1.002) ** 2
    r = np.sqrt(x)
    sin_c = np.polynomial.polynomial.polyfit(x, np.sin(r) / r, 5)
    cos_c = np.polynomial.polynomial.polyfit(x, np.cos(r), 6)
    return [float(v) for v in sin_c], [float(v) for v in cos_c]


SIN_C, COS_C = poly_fit()


def horner(x, coefs):
    acc = jnp.full_like(x, coefs[-1])
    for value in coefs[-2::-1]:
        acc = acc * x + value
    return acc


def sin_small(r):
    return r * horner(r * r, SIN_C)


def sin_cos(z):
    n = jnp.floor(z * (1.0 / math.pi) + 0.5)
    r = z - n * 3.140625
    r = r - n * 9.67653589793e-4
    half = n * 0.5
    sign = 1.0 - 4.0 * (half - jnp.floor(half))
    r2 = r * r
    return sign * (r * horner(r2, SIN_C)), sign * horner(r2, COS_C)


def dot_full(x, y):
    return jnp.dot(x, y, precision=HIGHEST, preferred_element_type=F32)


def dot_nt(x, y, precision=None):
    return lax.dot_general(x, y, (((1,), (1,)), ((), ())), precision=precision, preferred_element_type=F32)


def dot_tn(x, y, precision=None):
    return lax.dot_general(x, y, (((0,), (0,)), ((), ())), precision=precision, preferred_element_type=F32)


def low_dot(x, y):
    return jnp.dot(x, y, preferred_element_type=F32)


def split(x):
    hi = x.astype(LOW)
    return hi, (x - hi.astype(F32)).astype(LOW)


def iota(shape, dim):
    return lax.broadcasted_iota(jnp.int32, shape, dim)


def to_column(row, size, shift):
    n = row.shape[1]
    pick = iota((size, n), 0) + shift == iota((size, n), 1)
    return jnp.sum(jnp.where(pick, jnp.broadcast_to(row, (size, n)), 0.0), axis=1, keepdims=True)


def to_row(col):
    n = col.shape[0]
    pick = iota((n, n), 0) == iota((n, n), 1)
    return jnp.sum(jnp.where(pick, jnp.broadcast_to(col, (n, n)), 0.0), axis=0, keepdims=True)


def repeat_matrix(rows, period, times):
    shape = (rows, period * times)
    j = iota(shape, 1)
    hit = j == iota(shape, 0)
    for m in range(1, times):
        hit = hit | (j == iota(shape, 0) + m * period)
    return jnp.where(hit, 1.0, 0.0)


def hi_hi_lo(w, period):
    hi = w.astype(LOW).astype(F32)
    lane = iota(w.shape, 1)
    out = jnp.where(lane < 2 * period, hi, jnp.where(lane < 3 * period, w - hi, 0.0))
    return out.astype(LOW)


class Refs:
    def __init__(self, **refs):
        self.__dict__.update(refs)


def prepare_weights(r, chan):
    first = jnp.where(iota((8, 64), 0) == 1, jnp.broadcast_to(r.b_in[...], (8, 64)), 0.0)
    r.w_pad[0:32, :] = r.w_in[0:32, :]
    r.w_pad[32:40, :] = jnp.where(iota((8, 64), 0) == 0, jnp.broadcast_to(r.w_in[32:33, :], (8, 64)), first)
    r.w_pad[40:48, :] = jnp.zeros((8, 64), F32)
    r.k_in[...] = hi_hi_lo(dot_tn(r.w_pad[...], repeat_matrix(48, 48, 3), HIGHEST), 48)
    rep = repeat_matrix(64, 64, 3)
    for i in range(2):
        w = r.w_mid[i]
        r.k_mid[i] = hi_hi_lo(dot_full(w, rep), 64)
        r.k_back[i] = hi_hi_lo(dot_tn(w, rep, HIGHEST), 64)
    own = jnp.where(iota((CH, 128), 1) == iota((CH, 128), 0) + chan * CH, 1.0, 0.0)
    w_own = dot_nt(own, r.w_out[...], HIGHEST)
    r.k_out[...] = hi_hi_lo(dot_full(w_own, rep), 64)
    r.k_outback[...] = hi_hi_lo(dot_tn(w_own, repeat_matrix(CH, CH, 4), HIGHEST), CH)
    r.rate_col[...] = jnp.broadcast_to(to_column(r.rate[...], CH, chan * CH), (CH, 128))
    r.bias_col[0] = jnp.broadcast_to(to_column(r.b_mid[0:1, :], 64, 0), (64, 128))
    r.bias_col[1] = jnp.broadcast_to(to_column(r.b_mid[1:2, :], 64, 0), (64, 128))


def wide(block, times):
    return jnp.concatenate([block] * times, axis=1)


def fraction(seq, base):
    pos = seq * TB + base + iota((CH, CHUNK), 1)
    return pos.astype(F32) * (1.0 / L)


def net_forward(r, seq):
    per = CHUNK // 128

    def step(j, carry):
        base = pl.multiple_of(j * CHUNK, CHUNK)
        lanes = pl.ds(base, CHUNK)
        pos = seq * TB + base + iota((48, CHUNK), 1)
        row = iota((48, CHUNK), 0)
        phase = ((wide(r.bands[0], per) * pos + (wide(r.bands[1], per) + L // 2)) & (L - 1)) - L // 2
        phase = jnp.where(phase > L // 4, L // 2 - phase, phase)
        phase = jnp.where(phase < -(L // 4), -(L // 2) - phase, phase)
        wave = sin_small(phase.astype(F32) * (2.0 * math.pi / L))
        frac = pos.astype(F32) * (1.0 / L)
        hi, lo = split(jnp.where(row == 0, frac, jnp.where(row == 33, 1.0, wave)))
        r.feat[0:48, lanes] = hi
        r.feat[48:64, lanes] = jnp.zeros((16, CHUNK), LOW)
        r.feat[64:112, lanes] = lo
        r.feat[112:128, lanes] = jnp.zeros((16, CHUNK), LOW)
        z = low_dot(r.k_in[...], jnp.concatenate([hi, lo, hi], axis=0))
        for layer in range(3):
            s, c = sin_cos(z)
            r.der[layer, :, lanes] = c
            hi, lo = split(s)
            r.act[layer, 0:64, lanes] = hi
            r.act[layer, 64:128, lanes] = lo
            x = jnp.concatenate([hi, lo, hi], axis=0)
            if layer < 2:
                z = low_dot(r.k_mid[layer], x) + wide(r.bias_col[layer], per)
        raw = low_dot(r.k_out[...], x) * jnp.exp(-wide(r.rate_col[...], per) * frac[0:CH, :])
        for i in range(per):
            r.raw_all[seq * ABLK + j * per + i] = raw[:, 128 * i : 128 * i + 128]
        return carry

    lax.fori_loop(0, TB // CHUNK, step, 0)


def net_backward(r, seq):
    per = CHUNK // 128
    r.acc[...] = jnp.zeros_like(r.acc)
    r.acc_out[...] = jnp.zeros_like(r.acc_out)
    r.acc_bias[...] = jnp.zeros_like(r.acc_bias)
    r.acc_rate[...] = jnp.zeros_like(r.acc_rate)

    def lane_sum(x):
        total = x[:, 0:128]
        for i in range(1, per):
            total = total + x[:, 128 * i : 128 * i + 128]
        return total

    def step(j, carry):
        lanes = pl.ds(pl.multiple_of(j * CHUNK, CHUNK), CHUNK)
        start = seq * ABLK + j * per
        grad = jnp.concatenate([r.total[j * per + i] for i in range(per)], axis=1)
        raw = jnp.concatenate([r.raw_all[start + i] for i in range(per)], axis=1)
        frac = fraction(seq, j * CHUNK)
        r.acc_rate[...] -= lane_sum(grad * raw * frac)
        shaped = grad * jnp.exp(-wide(r.rate_col[...], per) * frac)
        hi = shaped.astype(LOW).astype(F32)
        lo = shaped - hi
        pair = jnp.concatenate([hi, lo], axis=0).astype(LOW)
        r.acc_out[...] += dot_nt(pair, r.act[2, :, lanes])
        d = low_dot(r.k_outback[...], jnp.concatenate([hi, lo, hi, jnp.zeros_like(hi)], axis=0).astype(LOW))
        for layer in (2, 1, 0):
            d = d * r.der[layer, :, lanes]
            hi, lo = split(d)
            pair = jnp.concatenate([hi, lo], axis=0)
            if layer:
                r.acc_bias[layer - 1] += lane_sum(d)
                r.acc[layer] += dot_nt(pair, r.act[layer - 1, :, lanes])
                d = low_dot(r.k_back[layer - 1], jnp.concatenate([hi, lo, hi], axis=0))
            else:
                r.acc[0] += dot_nt(pair, r.feat[:, lanes])
        return carry

    lax.fori_loop(0, TB // CHUNK, step, 0)


def fold_halves(x):
    n = x.shape[0] // 2
    total = x[0:n] + x[n:]
    return total + pltpu.roll(total, 64, 1)


def pack_shares(r):
    lane = iota((64, 128), 1)
    r.block[0] = jnp.where(lane < 64, fold_halves(r.acc[1]), fold_halves(r.acc[2]))
    block = fold_halves(r.acc[0])
    block = jnp.where(lane == 34, jnp.sum(r.acc_bias[0], axis=1, keepdims=True), block)
    r.block[1] = jnp.where(lane == 35, jnp.sum(r.acc_bias[1], axis=1, keepdims=True), block)
    lane = iota((CH, 128), 1)
    own = pltpu.roll(fold_halves(r.acc_out[...]), 48, 1)
    own = jnp.where(lane == 112, jnp.sum(r.acc_rate[...], axis=1, keepdims=True), own)
    own = jnp.where(lane == 113, r.skip_part[...], own)

    def place(s, carry):
        rows = pl.ds(pl.multiple_of(8 * s, 8), 8)
        r.share[s, :, 0:128] = r.block[0, rows, :]
        r.share[s, :, 128:256] = jnp.where(lane < 48, r.block[1, rows, :], own)
        return carry

    lax.fori_loop(0, NSEQ, place, 0)


def to_low(x):
    return x.astype(LOW)


def channel_rows(c):
    return pl.ds(c, A, stride=CH)


def forward_pair(r, x):
    tc, ts = r.turn[0], r.turn[1]
    g = low_dot(r.w1[...], x)
    parts = []
    for n in range(2):
        re, im = g[0:A, n * B : n * B + B], g[A:, n * B : n * B + B]
        parts.append(jnp.concatenate([to_low(re * tc + im * ts), to_low(im * tc - re * ts)], axis=1))
    f = low_dot(jnp.concatenate(parts, axis=0), r.fwd[...])
    return f[0:A], f[A:]


def inverse_pair(r, specs):
    tc, ts = r.turn[0], r.turn[1]
    s = jnp.concatenate([jnp.concatenate([to_low(re), to_low(im)], axis=1) for re, im in specs], axis=0)
    t = low_dot(s, r.inv[...])
    cols = []
    for n in range(2):
        re, im = t[n * A : n * A + A, 0:B], t[n * A : n * A + A, B:]
        cols.append(jnp.concatenate([to_low(re * tc - im * ts), to_low(re * ts + im * tc)], axis=0))
    y = low_dot(r.w1t[...], jnp.concatenate(cols, axis=1))
    return y[:, 0:B], y[:, B:]


BLK = 16
VMEM_MAIN = 56 << 20


def gate_products(r, n):
    def step(j, acc):
        part = pl.ds(j * BLK, BLK)
        rows = pl.ds(pl.multiple_of(j * (BLK * CH), BLK * CH), BLK * CH)
        m = r.val[n, part].astype(F32) * r.gin[n, part].astype(F32)
        g = r.cot[n, part].astype(F32) * r.gout[n, part].astype(F32)
        r.mixed[n, rows, :] = m.reshape(BLK * CH, B)
        r.inner[n, rows, :] = g.reshape(BLK * CH, B)
        return acc + jnp.sum(m * g, axis=0)

    return lax.fori_loop(0, A // BLK, step, jnp.zeros((CH, B), F32))


def spectra(r, p):
    cross = []
    for i in range(2):
        c = 2 * p + i
        rows = channel_rows(c)
        fm = forward_pair(r, jnp.concatenate([to_low(r.mixed[n, rows, :]) for n in range(2)], axis=1))
        fg = forward_pair(r, jnp.concatenate([to_low(r.inner[n, rows, :]) for n in range(2)], axis=1))
        re = im = None
        for n in range(2):
            r.f_mixed[c, n] = fm[n]
            r.f_inner[c, n] = fg[n]
            mr, mi = fm[n][:, 0:B], fm[n][:, B:]
            gr, gi = fg[n][:, 0:B], fg[n][:, B:]
            pr, pi = mr * gr + mi * gi, mr * gi - mi * gr
            re, im = (pr, pi) if re is None else (re + pr, im + pi)
        cross.append((re, im))
    ys = inverse_pair(r, cross)
    for i in range(2):
        r.gk[channel_rows(2 * p + i), :] = ys[i]


def normalize(r):
    def rows_of(j):
        return pl.ds(pl.multiple_of(j * (BLK * CH), BLK * CH), BLK * CH)

    def sums(j, carry):
        square, along = carry
        x = r.raw_all[pl.ds(j * BLK, BLK)]
        y = r.gk[rows_of(j), :].reshape(BLK, CH, B)
        return square + jnp.sum(x * x, axis=0), along + jnp.sum(x * y, axis=0)

    zero = jnp.zeros((CH, B), F32)
    square, along = lax.fori_loop(0, A // BLK, sums, (zero, zero))
    norm = jnp.sqrt(jnp.sum(square, axis=1, keepdims=True) + EPSILON)
    along = jnp.sum(along, axis=1, keepdims=True) * (1.0 / L)
    recip = jnp.broadcast_to(1.0 / norm, (CH, B))
    scale_gk = (recip * (1.0 / L))[None]
    scale_raw = jnp.broadcast_to(along / (norm * norm * norm), (CH, B))[None]

    def settle(j, carry):
        part = pl.ds(j * BLK, BLK)
        x = r.raw_all[part]
        r.grad_all[part] = r.gk[rows_of(j), :].reshape(BLK, CH, B) * scale_gk - x * scale_raw
        r.kern[rows_of(j), :] = (x * recip[None]).reshape(BLK * CH, B)
        return carry

    lax.fori_loop(0, A // BLK, settle, 0)


def filter_products(r, p):
    fk = forward_pair(r, jnp.concatenate([to_low(r.kern[channel_rows(2 * p + i), :]) for i in range(2)], axis=1))
    for i in range(2):
        c = 2 * p + i
        rows = channel_rows(c)
        kr, ki = fk[i][:, 0:B] * (1.0 / L), fk[i][:, B:] * (1.0 / L)
        specs = []
        for n in range(2):
            mr, mi = r.f_mixed[c, n, :, 0:B], r.f_mixed[c, n, :, B:]
            specs.append((mr * kr - mi * ki, mr * ki + mi * kr))
        ys = inverse_pair(r, specs)
        for n in range(2):
            r.conv[n, rows, :] = ys[n]
        specs = []
        for n in range(2):
            gr, gi = r.f_inner[c, n, :, 0:B], r.f_inner[c, n, :, B:]
            specs.append((gr * kr + gi * ki, gi * kr - gr * ki))
        ys = inverse_pair(r, specs)
        for n in range(2):
            r.back[n, rows, :] = ys[n]


def finish(r, n):
    gain = jnp.broadcast_to(to_column(r.skip[...], CH, 0), (CH, B))[None]

    def step(j, carry):
        part = pl.ds(j * BLK, BLK)
        rows = pl.ds(pl.multiple_of(j * (BLK * CH), BLK * CH), BLK * CH)
        shape = (BLK, CH, B)
        full = r.conv[n, rows, :].reshape(shape) + gain * r.mixed[n, rows, :].reshape(shape)
        r.o_gout[n, part] = to_low(r.cot[n, part].astype(F32) * full)
        full = r.back[n, rows, :].reshape(shape) + gain * r.inner[n, rows, :].reshape(shape)
        r.o_val[n, part] = to_low(full * r.gin[n, part].astype(F32))
        r.o_gin[n, part] = to_low(full * r.val[n, part].astype(F32))
        return carry

    lax.fori_loop(0, A // BLK, step, 0)


SMALL = ("bands", "w_in", "b_in", "w_mid", "b_mid", "w_out", "rate", "skip")
TABLES = ("w1", "w1t", "fwd", "inv", "turn")
LARGE = ("val", "gin", "cot", "gout")
OUTS = ("h_val", "h_gin", "h_gout", "second", "third", "g_skip")
BIG = (2, A, CH, B)
FULL = (2, A * CH, B)
SCRATCH = {
    "bands": ((2, 48, 128), jnp.int32),
    "w_in": ((33, 64), F32),
    "b_in": ((1, 64), F32),
    "w_mid": ((2, 64, 64), F32),
    "b_mid": ((2, 64), F32),
    "w_out": ((64, 128), F32),
    "rate": ((1, 128), F32),
    "skip": ((1, CH), F32),
    "w1": ((2 * A, A), LOW),
    "w1t": ((A, 2 * A), LOW),
    "fwd": ((2 * B, 2 * B), LOW),
    "inv": ((2 * B, 2 * B), LOW),
    "turn": ((2, A, B), F32),
    "val": (BIG, LOW),
    "gin": (BIG, LOW),
    "cot": (BIG, LOW),
    "gout": (BIG, LOW),
    "o_val": (BIG, LOW),
    "o_gin": (BIG, LOW),
    "o_gout": (BIG, LOW),
    "w_pad": ((48, 64), F32),
    "k_in": ((64, 144), LOW),
    "k_mid": ((2, 64, 192), LOW),
    "k_back": ((2, 64, 192), LOW),
    "k_out": ((CH, 192), LOW),
    "k_outback": ((64, 4 * CH), LOW),
    "rate_col": ((CH, 128), F32),
    "bias_col": ((2, 64, 128), F32),
    "feat": ((128, TB), LOW),
    "act": ((3, 128, TB), LOW),
    "der": ((3, 64, TB), F32),
    "raw_all": ((A, CH, B), F32),
    "grad_all": ((A, CH, B), F32),
    "total": ((ABLK, CH, B), F32),
    "half": ((2, 2, ABLK // 2, CH, B), F32),
    "side": ((2, 2, ABLK, CH, B), F32),
    "side_out": ((2, 2, ABLK, CH, B), F32),
    "pair": ((2, ABLK, CH, B), F32),
    "mixed": (FULL, F32),
    "inner": (FULL, F32),
    "f_mixed": ((CH, 2, A, 2 * B), F32),
    "f_inner": ((CH, 2, A, 2 * B), F32),
    "gk": ((A * CH, B), F32),
    "kern": ((A * CH, B), F32),
    "conv": (FULL, F32),
    "back": (FULL, F32),
    "acc": ((3, 128, 128), F32),
    "acc_out": ((16, 128), F32),
    "acc_bias": ((2, 64, 128), F32),
    "acc_rate": ((CH, 128), F32),
    "skip_part": ((CH, 1), F32),
    "block": ((2, 64, 128), F32),
    "share": ((NSEQ, 8, 256), F32),
    "first": ((NSEQ, 8, 256), F32),
}
N_LOCAL = len(SMALL) + len(TABLES) + len(LARGE)


def main_kernel(*refs):
    ins = refs[:N_LOCAL]
    outs = refs[N_LOCAL : N_LOCAL + len(OUTS)]
    names = list(SCRATCH)
    scratch = refs[N_LOCAL + len(OUTS) :]
    r = Refs(**dict(zip(OUTS, outs)), **dict(zip(names, scratch)))
    (load_sem, out_sem, ag_send, ag_recv, rs_send, rs_recv, sem_b, recv_b, sem_c, recv_c, sem_d, recv_d) = scratch[len(names) :]
    chan, seq = lax.axis_index("chan"), lax.axis_index("seq")
    barrier = pltpu.get_barrier_semaphore()

    def signal(device):
        pl.semaphore_signal(barrier, inc=1, device_id=device, device_id_type=MESH)

    def hail_seq(d, carry):
        signal((chan, lax.rem(seq + d, NSEQ)))
        return carry

    def hail_chan(d, carry):
        signal((lax.rem(chan + d, NCHAN), seq))
        return carry

    loads = {}
    for i, name in enumerate(SMALL + TABLES + LARGE):
        loads[name] = pltpu.make_async_copy(ins[i], getattr(r, name), load_sem.at[i])
    for name in SMALL:
        loads[name].start()
    lax.fori_loop(1, NSEQ, hail_seq, 0)
    lax.fori_loop(1, NCHAN, hail_chan, 0)
    for name in LARGE + TABLES:
        loads[name].start()
    for name in SMALL:
        loads[name].wait()

    prepare_weights(r, chan)
    net_forward(r, seq)
    pl.semaphore_wait(barrier, NSEQ - 1 + NCHAN - 1)

    x, z = lax.div(seq, 2), lax.rem(seq, 2)
    xr, xl, xo = lax.rem(x + 1, 4), lax.rem(x + 3, 4), lax.rem(x + 2, 4)
    other = 1 - z
    to_z, to_r, to_l = (chan, 2 * x + other), (chan, 2 * xr + z), (chan, 2 * xl + z)
    HALF = ABLK // 2

    def gather(i, row, count, device):
        part = r.raw_all.at[pl.ds(row, count)]
        return pltpu.make_async_remote_copy(
            src_ref=part, dst_ref=part, send_sem=ag_send.at[i], recv_sem=ag_recv.at[i],
            device_id=device, device_id_type=MESH,
        )

    def row_of(xx, zz):
        return (2 * xx + zz) * ABLK

    ag = [gather(0, row_of(x, z), ABLK, to_z), gather(1, row_of(x, z), ABLK, to_r), gather(2, row_of(x, z), ABLK, to_l)]
    for copy in ag:
        copy.start()

    for name in LARGE:
        loads[name].wait()
    acc = gate_products(r, 0)
    acc = acc + gate_products(r, 1)
    r.skip_part[...] = jnp.sum(acc, axis=1, keepdims=True)

    ag[0].wait_recv()
    ag += [gather(3, row_of(x, other), ABLK, to_r), gather(4, row_of(x, other), ABLK, to_l)]
    ag[3].start()
    ag[4].start()
    ag[1].wait_recv()
    ag += [gather(5, row_of(xl, z), HALF, to_r)]
    ag[5].start()
    ag[2].wait_recv()
    ag += [gather(6, row_of(xr, z) + HALF, HALF, to_l)]
    ag[6].start()
    for name in TABLES:
        loads[name].wait()

    def loop(body, start, stop):
        def step(p, carry):
            body(r, p)
            return carry

        lax.fori_loop(start, stop, step, 0)

    loop(spectra, 0, 3)
    ag[3].wait_recv()
    ag += [gather(7, row_of(xl, other), HALF, to_r)]
    ag[7].start()
    ag[4].wait_recv()
    ag += [gather(8, row_of(xr, other) + HALF, HALF, to_l)]
    ag[8].start()
    loop(spectra, 3, 4)
    for i in (5, 6, 7, 8):
        ag[i].wait_recv()

    normalize(r)

    def send(i, src, dst, device):
        return pltpu.make_async_remote_copy(
            src_ref=src, dst_ref=dst, send_sem=rs_send.at[i], recv_sem=rs_recv.at[i],
            device_id=device, device_id_type=MESH,
        )

    zs = (other, z)
    rs = []
    for w in range(2):
        far = row_of(xo, zs[w])
        rs += [
            send(2 * w, r.grad_all.at[pl.ds(far, HALF)], r.half.at[w, 0], to_r),
            send(2 * w + 1, r.grad_all.at[pl.ds(far + HALF, HALF)], r.half.at[w, 1], to_l),
        ]
    for copy in rs:
        copy.start()

    def add_half(w):
        rs[2 * w].wait_recv()
        near = row_of(xr, zs[w])
        r.side_out[w, 0, 0:HALF] = r.grad_all[pl.ds(near, HALF)] + r.half[w, 0]
        r.side_out[w, 0, HALF:] = r.grad_all[pl.ds(near + HALF, HALF)]
        rs[2 * w + 1].wait_recv()
        near = row_of(xl, zs[w])
        r.side_out[w, 1, 0:HALF] = r.grad_all[pl.ds(near, HALF)]
        r.side_out[w, 1, HALF:] = r.grad_all[pl.ds(near + HALF, HALF)] + r.half[w, 1]
        for i, device in enumerate((to_r, to_l)):
            copy = send(4 + 2 * w + i, r.side_out.at[w, i], r.side.at[w, i], device)
            copy.start()
            rs.append(copy)

    def own_sum(w):
        rs[4 + 2 * w].wait_recv()
        rs[5 + 2 * w].wait_recv()
        return r.grad_all[pl.ds(row_of(x, zs[w]), ABLK)] + r.side[w, 0] + r.side[w, 1]

    loop(filter_products, 0, 1)
    add_half(0)
    loop(filter_products, 1, 2)
    add_half(1)
    loop(filter_products, 2, 4)
    r.pair[0] = own_sum(0)
    rs.append(send(8, r.pair.at[0], r.pair.at[1], to_z))
    rs[8].start()
    r.total[...] = own_sum(1)
    finish(r, 0)
    results = []

    def leave(n):
        for i, (src, dst) in enumerate(((r.o_val, r.h_val), (r.o_gin, r.h_gin), (r.o_gout, r.h_gout))):
            copy = pltpu.make_async_copy(src.at[n], dst.at[n], out_sem.at[3 * n + i])
            copy.start()
            results.append(copy)

    leave(0)
    rs[8].wait_recv()
    r.total[...] += r.pair[1]
    for copy in ag + rs:
        copy.wait_send()

    net_backward(r, seq)
    pack_shares(r)

    def run(size, make):
        def start(d, carry):
            make(d).start()
            return carry

        def wait(d, carry):
            make(d).wait()
            return carry

        lax.fori_loop(1, size, start, 0)
        return lambda: lax.fori_loop(1, size, wait, 0)

    def seq_peer(d):
        return (chan, lax.rem(seq + d, NSEQ))

    def make_b(d):
        return pltpu.make_async_remote_copy(
            src_ref=r.share.at[lax.rem(seq + d, NSEQ)], dst_ref=r.first.at[d],
            send_sem=sem_b.at[d], recv_sem=recv_b.at[d], device_id=seq_peer(d), device_id_type=MESH,
        )

    def make_c(d):
        return pltpu.make_async_remote_copy(
            src_ref=r.second.at[chan], dst_ref=r.second.at[chan], send_sem=sem_c.at[d], recv_sem=recv_c.at[d],
            device_id=(lax.rem(chan + d, NCHAN), seq), device_id_type=MESH,
        )

    def make_d(d):
        return pltpu.make_async_remote_copy(
            src_ref=r.third.at[seq], dst_ref=r.third.at[seq], send_sem=sem_d.at[d], recv_sem=recv_d.at[d],
            device_id=seq_peer(d), device_id_type=MESH,
        )

    wait = run(NSEQ, make_b)
    finish(r, 1)
    leave(1)
    wait()
    total = r.share[seq]
    for d in range(1, NSEQ):
        total = total + r.first[d]
    factor = 1.0 / math.sqrt(16 * L)
    total = total * factor
    r.second[chan] = total
    r.g_skip[...] = to_row(total[:, 241:242])
    run(NCHAN, make_c)()
    total = r.second[0]
    for c in range(1, NCHAN):
        total = total + r.second[c]
    r.third[seq] = total
    run(NSEQ, make_d)()
    for copy in results:
        copy.wait()


def write_kernel(
    i_val, i_gin, i_gout, i_second, i_third, skip,
    o_val, o_gin, o_gout, g_skip, g_in, g_bin, g_mid, g_bmid, g_out, g_rate,
    stage, second, third, in_sem, out_sem, small_sem,
):
    loads, stores = [], []
    for i, (src, dst) in enumerate(((i_val, o_val), (i_gin, o_gin), (i_gout, o_gout))):
        for n in range(2):
            loads.append(pltpu.make_async_copy(src.at[n], stage.at[i, n], in_sem.at[2 * i + n]))
            stores.append(pltpu.make_async_copy(stage.at[i, n], dst.at[n], out_sem.at[2 * i + n]))
    small = [
        pltpu.make_async_copy(i_second, second, small_sem.at[0]),
        pltpu.make_async_copy(i_third, third, small_sem.at[1]),
    ]
    for copy in small + loads:
        copy.start()
    g_skip[...] = skip[...]
    for load, store in zip(loads, stores):
        load.wait()
        store.start()
    for copy in small:
        copy.wait()
    hidden = third[...].reshape(64, 256)
    g_mid[0] = hidden[:, 0:64]
    g_mid[1] = pltpu.roll(hidden[:, 0:128], 64, 1)[:, 0:64]
    flat = jnp.transpose(hidden[:, 128:256])
    g_in[...] = flat[0:33, :]
    g_bin[...] = flat[33:34, :]
    g_bmid[...] = flat[34:36, :]
    own = jnp.transpose(second[...].reshape(128, 256)[:, 128:256])
    g_out[...] = own[48:112, :]
    g_rate[...] = own[112:113, :]
    for copy in stores:
        copy.wait()


def sds(shape, dtype=F32):
    return jax.ShapeDtypeStruct(shape, dtype)


VM = pl.BlockSpec(memory_space=pltpu.VMEM)
HB = pl.BlockSpec(memory_space=pltpu.HBM)
DMA = pltpu.SemaphoreType.DMA


def to_natural(x):
    return x.reshape(2, CH, A, B).transpose(0, 2, 1, 3)


def from_natural(x):
    return x.transpose(0, 2, 1, 3).reshape(2, CH, L)


def local(
    value, gate_in, gate_out, cotangent, skip_gain,
    weight_in, bias_in, weight_mid, bias_mid, weight_out, decay_rate,
):
    small = (
        row_constants(), weight_in.T, bias_in.reshape(1, 64), weight_mid, bias_mid, weight_out.T,
        decay_rate.reshape(1, 128), skip_gain.reshape(1, CH),
    )
    large = tuple(to_natural(x) for x in (value, gate_in, cotangent, gate_out))
    big = sds(BIG, LOW)
    o_val, o_gin, o_gout, second, third, g_skip = pl.pallas_call(
        main_kernel,
        out_shape=[big, big, big, sds((NCHAN, 8, 256)), sds((NSEQ, 8, 256)), sds((1, CH))],
        in_specs=[HB] * N_LOCAL,
        out_specs=[HB] * 3 + [VM] * 3,
        scratch_shapes=[pltpu.VMEM(shape, dtype) for shape, dtype in SCRATCH.values()]
        + [
            DMA((N_LOCAL,)), DMA((6,)), DMA((9,)), DMA((9,)), DMA((9,)), DMA((9,)),
            DMA((NSEQ,)), DMA((NSEQ,)), DMA((NCHAN,)), DMA((NCHAN,)), DMA((NSEQ,)), DMA((NSEQ,)),
        ],
        compiler_params=pltpu.CompilerParams(
            collective_id=0, has_side_effects=True, vmem_limit_bytes=VMEM_MAIN
        ),
        name="hyena_backward",
    )(*small, *transform_tables(), *large)
    o_val, o_gin, o_gout, g_skip, g_in, g_bin, g_mid, g_bmid, g_out, g_rate = pl.pallas_call(
        write_kernel,
        out_shape=[
            big, big, big, sds((1, CH)), sds((33, 64)), sds((1, 64)), sds((2, 64, 64)), sds((2, 64)),
            sds((64, 128)), sds((1, 128)),
        ],
        in_specs=[HB] * 5 + [VM],
        out_specs=[HB] * 3 + [VM] * 7,
        scratch_shapes=[
            pltpu.VMEM((3,) + BIG, LOW), pltpu.VMEM((NCHAN, 8, 256), F32), pltpu.VMEM((NSEQ, 8, 256), F32),
            DMA((6,)), DMA((6,)), DMA((2,)),
        ],
        compiler_params=pltpu.CompilerParams(vmem_limit_bytes=VMEM_MAIN),
        name="write_results",
    )(o_val, o_gin, o_gout, second, third, g_skip)
    return (
        from_natural(o_val), from_natural(o_gin), from_natural(o_gout), g_skip.reshape(CH),
        g_in.T, g_bin.reshape(64), g_mid, g_bmid, g_out.T, g_rate.reshape(128),
    )


def solution(mesh):
    return jax.shard_map(
        local,
        mesh=mesh,
        in_specs=(
            P("seq", "chan", None), P("seq", "chan", None), P("seq", "chan", None), P("seq", "chan", None),
            P("chan"), P(), P(), P(), P(), P(), P(),
        ),
        out_specs=(
            P("seq", "chan", None), P("seq", "chan", None), P("seq", "chan", None),
            P("chan"), P(), P(), P(), P(), P(), P(),
        ),
        check_vma=False,
    )
```

```python
import functools
import math

import jax
import jax.numpy as jnp
import numpy as np
from jax import lax
from jax.experimental import pallas as pl
from jax.experimental.pallas import tpu as pltpu
from jax.sharding import PartitionSpec as P

EPSILON = 1e-06
HIGHEST = lax.Precision.HIGHEST
L = 32768
A = 256
B = 128
CH = 8
NSEQ = 8
NCHAN = 16
ABLK = A // NSEQ
TB = L // NSEQ
CHUNK = 1024
LOW = jnp.bfloat16
F32 = jnp.float32
MESH = pl.DeviceIdType.MESH


def band_table(length, bands):
    highest = length / 4.0
    return np.array(
        [math.floor(highest ** (number / (bands - 1)) + 0.5) for number in range(bands)], np.int64
    )


def row_constants():
    freq = np.zeros((48, 128), np.int32)
    off = np.zeros((48, 128), np.int32)
    bands = band_table(L, 16)
    freq[1:17] = bands[:, None]
    off[1:17] = L // 4
    freq[17:33] = bands[:, None]
    return np.stack([freq, off])


def transform_tables():
    k = np.arange(A)[:, None]
    rows = 2.0 * np.pi * (((4 * k + 1) * np.arange(A)[None, :]) % 1024) / 1024.0
    w1 = np.concatenate([np.cos(rows), -np.sin(rows)], axis=0)
    turn = 2.0 * np.pi * (((4 * k + 1) * np.arange(B)[None, :]) % (4 * L)) / (4.0 * L)
    q = np.arange(B)
    cols = 2.0 * np.pi * ((q[:, None] * q[None, :]) % B) / B
    c, s = np.cos(cols), np.sin(cols)
    fwd = np.block([[c, -s], [s, c]])
    inv = np.block([[c, s], [-s, c]])
    low = np.dtype(LOW)
    return (
        w1.astype(low),
        w1.T.astype(low),
        fwd.astype(low),
        inv.astype(low),
        np.stack([np.cos(turn), np.sin(turn)]).astype(np.float32),
    )


def poly_fit():
    x = (np.cos(np.pi * (np.arange(64) + 0.5) / 64) + 1) / 2 * (np.pi / 2 * 1.002) ** 2
    r = np.sqrt(x)
    sin_c = np.polynomial.polynomial.polyfit(x, np.sin(r) / r, 5)
    cos_c = np.polynomial.polynomial.polyfit(x, np.cos(r), 6)
    return [float(v) for v in sin_c], [float(v) for v in cos_c]


SIN_C, COS_C = poly_fit()


def horner(x, coefs):
    acc = jnp.full_like(x, coefs[-1])
    for value in coefs[-2::-1]:
        acc = acc * x + value
    return acc


def sin_small(r):
    return r * horner(r * r, SIN_C)


def sin_cos(z):
    n = jnp.floor(z * (1.0 / math.pi) + 0.5)
    r = z - n * 3.140625
    r = r - n * 9.67653589793e-4
    half = n * 0.5
    sign = 1.0 - 4.0 * (half - jnp.floor(half))
    r2 = r * r
    return sign * (r * horner(r2, SIN_C)), sign * horner(r2, COS_C)


def dot_full(x, y):
    return jnp.dot(x, y, precision=HIGHEST, preferred_element_type=F32)


def dot_nt(x, y, precision=None):
    return lax.dot_general(x, y, (((1,), (1,)), ((), ())), precision=precision, preferred_element_type=F32)


def dot_tn(x, y, precision=None):
    return lax.dot_general(x, y, (((0,), (0,)), ((), ())), precision=precision, preferred_element_type=F32)


def low_dot(x, y):
    return jnp.dot(x, y, preferred_element_type=F32)


def split(x):
    hi = x.astype(LOW)
    return hi, (x - hi.astype(F32)).astype(LOW)


def iota(shape, dim):
    return lax.broadcasted_iota(jnp.int32, shape, dim)


def to_column(row, size, shift):
    n = row.shape[1]
    pick = iota((size, n), 0) + shift == iota((size, n), 1)
    return jnp.sum(jnp.where(pick, jnp.broadcast_to(row, (size, n)), 0.0), axis=1, keepdims=True)


def to_row(col):
    n = col.shape[0]
    pick = iota((n, n), 0) == iota((n, n), 1)
    return jnp.sum(jnp.where(pick, jnp.broadcast_to(col, (n, n)), 0.0), axis=0, keepdims=True)


def repeat_matrix(rows, period, times):
    shape = (rows, period * times)
    j = iota(shape, 1)
    hit = j == iota(shape, 0)
    for m in range(1, times):
        hit = hit | (j == iota(shape, 0) + m * period)
    return jnp.where(hit, 1.0, 0.0)


def hi_hi_lo(w, period):
    hi = w.astype(LOW).astype(F32)
    lane = iota(w.shape, 1)
    out = jnp.where(lane < 2 * period, hi, jnp.where(lane < 3 * period, w - hi, 0.0))
    return out.astype(LOW)


class Refs:
    def __init__(self, **refs):
        self.__dict__.update(refs)


def prepare_weights(r, chan):
    first = jnp.where(iota((8, 64), 0) == 1, jnp.broadcast_to(r.b_in[...], (8, 64)), 0.0)
    r.w_pad[0:32, :] = r.w_in[0:32, :]
    r.w_pad[32:40, :] = jnp.where(iota((8, 64), 0) == 0, jnp.broadcast_to(r.w_in[32:33, :], (8, 64)), first)
    r.w_pad[40:48, :] = jnp.zeros((8, 64), F32)
    r.k_in[...] = hi_hi_lo(dot_tn(r.w_pad[...], repeat_matrix(48, 48, 3), HIGHEST), 48)
    rep = repeat_matrix(64, 64, 3)
    for i in range(2):
        w = r.w_mid[i]
        r.k_mid[i] = hi_hi_lo(dot_full(w, rep), 64)
        r.k_back[i] = hi_hi_lo(dot_tn(w, rep, HIGHEST), 64)
    own = jnp.where(iota((CH, 128), 1) == iota((CH, 128), 0) + chan * CH, 1.0, 0.0)
    w_own = dot_nt(own, r.w_out[...], HIGHEST)
    r.k_out[...] = hi_hi_lo(dot_full(w_own, rep), 64)
    r.k_outback[...] = hi_hi_lo(dot_tn(w_own, repeat_matrix(CH, CH, 4), HIGHEST), CH)
    r.rate_col[...] = jnp.broadcast_to(to_column(r.rate[...], CH, chan * CH), (CH, 128))
    r.bias_col[0] = jnp.broadcast_to(to_column(r.b_mid[0:1, :], 64, 0), (64, 128))
    r.bias_col[1] = jnp.broadcast_to(to_column(r.b_mid[1:2, :], 64, 0), (64, 128))


def wide(block, times):
    return jnp.concatenate([block] * times, axis=1)


def fraction(seq, base):
    pos = seq * TB + base + iota((CH, CHUNK), 1)
    return pos.astype(F32) * (1.0 / L)


def net_forward(r, seq, send):
    per = CHUNK // 128

    def step(j, carry):
        base = pl.multiple_of(j * CHUNK, CHUNK)
        lanes = pl.ds(base, CHUNK)
        pos = seq * TB + base + iota((48, CHUNK), 1)
        row = iota((48, CHUNK), 0)
        phase = ((wide(r.bands[0], per) * pos + (wide(r.bands[1], per) + L // 2)) & (L - 1)) - L // 2
        phase = jnp.where(phase > L // 4, L // 2 - phase, phase)
        phase = jnp.where(phase < -(L // 4), -(L // 2) - phase, phase)
        wave = sin_small(phase.astype(F32) * (2.0 * math.pi / L))
        frac = pos.astype(F32) * (1.0 / L)
        hi, lo = split(jnp.where(row == 0, frac, jnp.where(row == 33, 1.0, wave)))
        r.feat[0:48, lanes] = hi
        r.feat[48:64, lanes] = jnp.zeros((16, CHUNK), LOW)
        r.feat[64:112, lanes] = lo
        r.feat[112:128, lanes] = jnp.zeros((16, CHUNK), LOW)
        z = low_dot(r.k_in[...], jnp.concatenate([hi, lo, hi], axis=0))
        for layer in range(3):
            s, c = sin_cos(z)
            r.der[layer, :, lanes] = c
            hi, lo = split(s)
            r.act[layer, 0:64, lanes] = hi
            r.act[layer, 64:128, lanes] = lo
            x = jnp.concatenate([hi, lo, hi], axis=0)
            if layer < 2:
                z = low_dot(r.k_mid[layer], x) + wide(r.bias_col[layer], per)
        raw = low_dot(r.k_out[...], x) * jnp.exp(-wide(r.rate_col[...], per) * frac[0:CH, :])
        for i in range(per):
            r.raw_all[seq * ABLK + j * per + i] = raw[:, 128 * i : 128 * i + 128]
        send(j)
        return carry

    lax.fori_loop(0, TB // CHUNK, step, 0)


def net_backward(r, seq, scale_gk, scale_raw):
    per = CHUNK // 128
    r.acc[...] = jnp.zeros_like(r.acc)
    r.acc_out[...] = jnp.zeros_like(r.acc_out)
    r.acc_bias[...] = jnp.zeros_like(r.acc_bias)
    r.acc_rate[...] = jnp.zeros_like(r.acc_rate)

    def lane_sum(x):
        total = x[:, 0:128]
        for i in range(1, per):
            total = total + x[:, 128 * i : 128 * i + 128]
        return total

    def step(j, carry):
        lanes = pl.ds(pl.multiple_of(j * CHUNK, CHUNK), CHUNK)
        start = seq * ABLK + j * per
        grad = jnp.concatenate([r.total[pl.ds(j * per + i, CH, stride=ABLK), :] for i in range(per)], axis=1)
        raw = jnp.concatenate([r.raw_all[start + i] for i in range(per)], axis=1)
        grad = grad * wide(scale_gk, per) - raw * wide(scale_raw, per)
        frac = fraction(seq, j * CHUNK)
        r.acc_rate[...] -= lane_sum(grad * raw * frac)
        shaped = grad * jnp.exp(-wide(r.rate_col[...], per) * frac)
        hi = shaped.astype(LOW).astype(F32)
        lo = shaped - hi
        pair = jnp.concatenate([hi, lo], axis=0).astype(LOW)
        r.acc_out[...] += dot_nt(pair, r.act[2, :, lanes])
        d = low_dot(r.k_outback[...], jnp.concatenate([hi, lo, hi, jnp.zeros_like(hi)], axis=0).astype(LOW))
        for layer in (2, 1, 0):
            d = d * r.der[layer, :, lanes]
            hi, lo = split(d)
            pair = jnp.concatenate([hi, lo], axis=0)
            if layer:
                r.acc_bias[layer - 1] += lane_sum(d)
                r.acc[layer] += dot_nt(pair, r.act[layer - 1, :, lanes])
                d = low_dot(r.k_back[layer - 1], jnp.concatenate([hi, lo, hi], axis=0))
            else:
                r.acc[0] += dot_nt(pair, r.feat[:, lanes])
        return carry

    lax.fori_loop(0, TB // CHUNK, step, 0)


def fold_halves(x):
    n = x.shape[0] // 2
    total = x[0:n] + x[n:]
    return total + pltpu.roll(total, 64, 1)


def pack_shares(r):
    lane = iota((64, 128), 1)
    r.block[0] = jnp.where(lane < 64, fold_halves(r.acc[1]), fold_halves(r.acc[2]))
    block = fold_halves(r.acc[0])
    block = jnp.where(lane == 34, jnp.sum(r.acc_bias[0], axis=1, keepdims=True), block)
    r.block[1] = jnp.where(lane == 35, jnp.sum(r.acc_bias[1], axis=1, keepdims=True), block)
    lane = iota((CH, 128), 1)
    own = pltpu.roll(fold_halves(r.acc_out[...]), 48, 1)
    own = jnp.where(lane == 112, jnp.sum(r.acc_rate[...], axis=1, keepdims=True), own)
    own = jnp.where(lane == 113, r.skip_part[...], own)

    def place(s, carry):
        rows = pl.ds(pl.multiple_of(8 * s, 8), 8)
        r.share[s, :, 0:128] = r.block[0, rows, :]
        r.share[s, :, 128:256] = jnp.where(lane < 48, r.block[1, rows, :], own)
        return carry

    lax.fori_loop(0, NSEQ, place, 0)


def to_low(x):
    return x.astype(LOW)


def channel_rows(c):
    return pl.ds(c, A, stride=CH)


def forward_pair(r, x):
    tc, ts = r.turn[0], r.turn[1]
    g = low_dot(r.w1[...], x)
    parts = []
    for n in range(2):
        re, im = g[0:A, n * B : n * B + B], g[A:, n * B : n * B + B]
        parts.append(jnp.concatenate([to_low(re * tc + im * ts), to_low(im * tc - re * ts)], axis=1))
    f = low_dot(jnp.concatenate(parts, axis=0), r.fwd[...])
    return f[0:A], f[A:]


def inverse_pair(r, specs):
    tc, ts = r.turn[0], r.turn[1]
    s = jnp.concatenate([jnp.concatenate([to_low(re), to_low(im)], axis=1) for re, im in specs], axis=0)
    t = low_dot(s, r.inv[...])
    cols = []
    for n in range(2):
        re, im = t[n * A : n * A + A, 0:B], t[n * A : n * A + A, B:]
        cols.append(jnp.concatenate([to_low(re * tc - im * ts), to_low(re * ts + im * tc)], axis=0))
    y = low_dot(r.w1t[...], jnp.concatenate(cols, axis=1))
    return y[:, 0:B], y[:, B:]


BLK = 16
VMEM_MAIN = 56 << 20


def gate_products(r, n):
    def step(j, acc):
        part = pl.ds(j * BLK, BLK)
        rows = pl.ds(pl.multiple_of(j * (BLK * CH), BLK * CH), BLK * CH)
        m = r.val[n, part].astype(F32) * r.gin[n, part].astype(F32)
        g = r.cot[n, part].astype(F32) * r.gout[n, part].astype(F32)
        r.mixed[n, rows, :] = m.reshape(BLK * CH, B)
        r.inner[n, rows, :] = g.reshape(BLK * CH, B)
        return acc + jnp.sum(m * g, axis=0)

    return lax.fori_loop(0, A // BLK, step, jnp.zeros((CH, B), F32))


def spectra(r, p):
    cross = []
    for i in range(2):
        c = 2 * p + i
        rows = channel_rows(c)
        fm = forward_pair(r, jnp.concatenate([to_low(r.mixed[n, rows, :]) for n in range(2)], axis=1))
        fg = forward_pair(r, jnp.concatenate([to_low(r.inner[n, rows, :]) for n in range(2)], axis=1))
        re = im = None
        for n in range(2):
            r.f_mixed[c, n] = fm[n]
            r.f_inner[c, n] = fg[n]
            mr, mi = fm[n][:, 0:B], fm[n][:, B:]
            gr, gi = fg[n][:, 0:B], fg[n][:, B:]
            pr, pi = mr * gr + mi * gi, mr * gi - mi * gr
            re, im = (pr, pi) if re is None else (re + pr, im + pi)
        cross.append((re, im))
    ys = inverse_pair(r, cross)
    for i in range(2):
        r.gk[2 * p + i] = ys[i]


def filter_products(r, p):
    kernels = []
    for i in range(2):
        c = 2 * p + i
        x = r.raw_flat[channel_rows(c), :]
        square = jnp.sum(x * x, axis=0, keepdims=True)
        r.stat[0, pl.ds(c, 1), :] = square
        r.stat[1, pl.ds(c, 1), :] = jnp.sum(x * r.gk[c], axis=0, keepdims=True)
        norm = jnp.sqrt(jnp.sum(square, axis=1, keepdims=True) + EPSILON)
        kernels.append(to_low(x / norm))
    fk = forward_pair(r, jnp.concatenate(kernels, axis=1))
    for i in range(2):
        c = 2 * p + i
        rows = channel_rows(c)
        kr, ki = fk[i][:, 0:B] * (1.0 / L), fk[i][:, B:] * (1.0 / L)
        specs = []
        for n in range(2):
            mr, mi = r.f_mixed[c, n, :, 0:B], r.f_mixed[c, n, :, B:]
            specs.append((mr * kr - mi * ki, mr * ki + mi * kr))
        ys = inverse_pair(r, specs)
        for n in range(2):
            r.conv[n, rows, :] = ys[n]
        specs = []
        for n in range(2):
            gr, gi = r.f_inner[c, n, :, 0:B], r.f_inner[c, n, :, B:]
            specs.append((gr * kr + gi * ki, gi * kr - gr * ki))
        ys = inverse_pair(r, specs)
        for n in range(2):
            r.back[n, rows, :] = ys[n]


def finish(r, n):
    gain = jnp.broadcast_to(to_column(r.skip[...], CH, 0), (CH, B))[None]

    def step(j, carry):
        part = pl.ds(j * BLK, BLK)
        rows = pl.ds(pl.multiple_of(j * (BLK * CH), BLK * CH), BLK * CH)
        shape = (BLK, CH, B)
        full = r.conv[n, rows, :].reshape(shape) + gain * r.mixed[n, rows, :].reshape(shape)
        r.o_gout[n, part] = to_low(r.cot[n, part].astype(F32) * full)
        full = r.back[n, rows, :].reshape(shape) + gain * r.inner[n, rows, :].reshape(shape)
        r.o_val[n, part] = to_low(full * r.gin[n, part].astype(F32))
        r.o_gin[n, part] = to_low(full * r.val[n, part].astype(F32))
        return carry

    lax.fori_loop(0, A // BLK, step, 0)


SMALL = ("bands", "w_in", "b_in", "w_mid", "b_mid", "w_out", "rate", "skip")
TABLES = ("w1", "w1t", "fwd", "inv", "turn")
LARGE = ("val", "gin", "cot", "gout")
OUTS = ("h_val", "h_gin", "h_gout", "second", "third", "g_skip")
BIG = (2, A, CH, B)
FULL = (2, A * CH, B)
SCRATCH = {
    "bands": ((2, 48, 128), jnp.int32),
    "w_in": ((33, 64), F32),
    "b_in": ((1, 64), F32),
    "w_mid": ((2, 64, 64), F32),
    "b_mid": ((2, 64), F32),
    "w_out": ((64, 128), F32),
    "rate": ((1, 128), F32),
    "skip": ((1, CH), F32),
    "w1": ((2 * A, A), LOW),
    "w1t": ((A, 2 * A), LOW),
    "fwd": ((2 * B, 2 * B), LOW),
    "inv": ((2 * B, 2 * B), LOW),
    "turn": ((2, A, B), F32),
    "val": (BIG, LOW),
    "gin": (BIG, LOW),
    "cot": (BIG, LOW),
    "gout": (BIG, LOW),
    "o_val": (BIG, LOW),
    "o_gin": (BIG, LOW),
    "o_gout": (BIG, LOW),
    "w_pad": ((48, 64), F32),
    "k_in": ((64, 144), LOW),
    "k_mid": ((2, 64, 192), LOW),
    "k_back": ((2, 64, 192), LOW),
    "k_out": ((CH, 192), LOW),
    "k_outback": ((64, 4 * CH), LOW),
    "rate_col": ((CH, 128), F32),
    "bias_col": ((2, 64, 128), F32),
    "feat": ((128, TB), LOW),
    "act": ((3, 128, TB), LOW),
    "der": ((3, 64, TB), F32),
    "raw_all": ((A, CH, B), F32),
    "total": ((CH * ABLK, B), F32),
    "half": ((CH // 2, 2, 2, 2, ABLK // 2, B), F32),
    "side_out": ((CH // 2, 2, 2, 2, ABLK, B), F32),
    "side": ((CH // 2, 5, 2, ABLK, B), F32),
    "stat": ((2, CH, B), F32),
    "along": ((NSEQ, CH, B), F32),
    "mixed": (FULL, F32),
    "inner": (FULL, F32),
    "f_mixed": ((CH, 2, A, 2 * B), F32),
    "f_inner": ((CH, 2, A, 2 * B), F32),
    "gk": ((CH, A, B), F32),
    "conv": (FULL, F32),
    "back": (FULL, F32),
    "acc": ((3, 128, 128), F32),
    "acc_out": ((16, 128), F32),
    "acc_bias": ((2, 64, 128), F32),
    "acc_rate": ((CH, 128), F32),
    "skip_part": ((CH, 1), F32),
    "block": ((2, 64, 128), F32),
    "share": ((NSEQ, 8, 256), F32),
    "first": ((NSEQ, 8, 256), F32),
}
N_LOCAL = len(SMALL) + len(TABLES) + len(LARGE)


def main_kernel(*refs):
    ins = refs[:N_LOCAL]
    outs = refs[N_LOCAL : N_LOCAL + len(OUTS)]
    names = list(SCRATCH)
    scratch = refs[N_LOCAL + len(OUTS) :]
    r = Refs(**dict(zip(OUTS, outs)), **dict(zip(names, scratch)))
    (load_sem, out_sem, ag_send, ag_recv, relay_send, relay_recv, half_send, half_recv, rs_send, rs_recv,
     sem_a, recv_a, sem_b, recv_b, sem_c, recv_c, sem_d, recv_d) = scratch[len(names) :]
    r.raw_flat = r.raw_all.reshape(A * CH, B)
    chan, seq = lax.axis_index("chan"), lax.axis_index("seq")
    barrier = pltpu.get_barrier_semaphore()

    def signal(device):
        pl.semaphore_signal(barrier, inc=1, device_id=device, device_id_type=MESH)

    def hail_seq(d, carry):
        signal((chan, lax.rem(seq + d, NSEQ)))
        return carry

    def hail_chan(d, carry):
        signal((lax.rem(chan + d, NCHAN), seq))
        return carry

    loads = {}
    for i, name in enumerate(SMALL + TABLES + LARGE):
        loads[name] = pltpu.make_async_copy(ins[i], getattr(r, name), load_sem.at[i])
    for name in SMALL:
        loads[name].start()
    lax.fori_loop(1, NSEQ, hail_seq, 0)
    lax.fori_loop(1, NCHAN, hail_chan, 0)
    for name in LARGE + TABLES:
        loads[name].start()
    for name in SMALL:
        loads[name].wait()

    x, z = lax.div(seq, 2), lax.rem(seq, 2)
    xr, xl, xo = lax.rem(x + 1, 4), lax.rem(x + 3, 4), lax.rem(x + 2, 4)
    other = 1 - z
    near = (
        (chan, 2 * x + other), (chan, 2 * xr + z), (chan, 2 * xr + other), (chan, 2 * xl + z), (chan, 2 * xl + other)
    )
    to_r, to_l = near[1], near[3]
    half = ABLK // 2
    piece = CHUNK // 128
    n_piece = ABLK // piece

    def row_of(xx, zz):
        return (2 * xx + zz) * ABLK

    def gather(i, j):
        part = r.raw_all.at[pl.ds(row_of(x, z) + j * piece, piece)]
        return pltpu.make_async_remote_copy(
            src_ref=part, dst_ref=part, send_sem=ag_send.at[i, j], recv_sem=ag_recv.at[i, j],
            device_id=near[i], device_id_type=MESH,
        )

    def send_chunk(j):
        for i in range(5):
            gather(i, j).start()

    def relay(i):
        row = row_of(xl if i < 2 else xr, (z, other)[i % 2]) + (0 if i < 2 else half)
        part = r.raw_all.at[pl.ds(row, half)]
        return pltpu.make_async_remote_copy(
            src_ref=part, dst_ref=part, send_sem=relay_send.at[i], recv_sem=relay_recv.at[i],
            device_id=to_r if i < 2 else to_l, device_id_type=MESH,
        )

    def arrived(i, start, stop):
        def step(j, carry):
            gather(i, j).wait_recv()
            return carry

        lax.fori_loop(start, stop, step, 0)

    zs = (other, z)

    def rows_at(p, row, count):
        return r.gk.at[pl.ds(2 * p, 2), pl.ds(pl.multiple_of(row, half), count)]

    def far_half(p, w, h):
        return pltpu.make_async_remote_copy(
            src_ref=rows_at(p, row_of(xo, zs[w]) + h * half, half), dst_ref=r.half.at[p, w, h],
            send_sem=half_send.at[p, 2 * w + h], recv_sem=half_recv.at[p, 2 * w + h],
            device_id=(to_r, to_l)[h], device_id_type=MESH,
        )

    def near_block(p, i):
        w = i % 2
        src = rows_at(p, row_of(x, other), ABLK) if i == 0 else r.side_out.at[p, w, (i - 1) // 2]
        return pltpu.make_async_remote_copy(
            src_ref=src, dst_ref=r.side.at[p, i], send_sem=rs_send.at[p, i], recv_sem=rs_recv.at[p, i],
            device_id=near[i], device_id_type=MESH,
        )

    def scatter_far(p):
        for w in range(2):
            for h in range(2):
                far_half(p, w, h).start()
        near_block(p, 0).start()

    def scatter_near(p):
        for w in range(2):
            for h in range(2):
                far_half(p, w, h).wait_recv()
                row = row_of((xr, xl)[h], zs[w])
                for i in range(2):
                    mine = r.gk[2 * p + i, pl.ds(pl.multiple_of(row, half), half), :]
                    rest = r.gk[2 * p + i, pl.ds(pl.multiple_of(row + half, half), half), :]
                    extra = r.half[p, w, h, i]
                    r.side_out[p, w, h, i, 0:half, :] = mine + extra if h == 0 else mine
                    r.side_out[p, w, h, i, half:, :] = rest if h == 0 else rest + extra
        for i in range(1, 5):
            near_block(p, i).start()

    prepare_weights(r, chan)
    pl.semaphore_wait(barrier, NSEQ - 1 + NCHAN - 1)
    net_forward(r, seq, send_chunk)

    for name in LARGE:
        loads[name].wait()
    acc = gate_products(r, 0)
    acc = acc + gate_products(r, 1)
    r.skip_part[...] = jnp.sum(acc, axis=1, keepdims=True)
    for name in TABLES:
        loads[name].wait()
    for i in range(2):
        arrived(1 + i, 0, n_piece // 2)
        relay(i).start()

    spectra(r, 0)
    scatter_far(0)
    for i in range(2):
        arrived(3 + i, n_piece // 2, n_piece)
        relay(2 + i).start()

    def pair_step(p, carry):
        spectra(r, p)
        scatter_far(p)
        scatter_near(p - 1)
        return carry

    lax.fori_loop(1, CH // 2, pair_step, 0)
    arrived(0, 0, n_piece)
    for i in range(2):
        arrived(1 + i, n_piece // 2, n_piece)
        arrived(3 + i, 0, n_piece // 2)
    for i in range(4):
        relay(i).wait_recv()

    filter_products(r, 0)
    scatter_near(CH // 2 - 1)

    def product_step(p, carry):
        filter_products(r, p)
        return carry

    lax.fori_loop(1, CH // 2, product_step, 0)

    def run(size, make):
        def start(d, carry):
            make(d).start()
            return carry

        def wait(d, carry):
            make(d).wait()
            return carry

        lax.fori_loop(1, size, start, 0)
        return lambda: lax.fori_loop(1, size, wait, 0)

    def seq_peer(d):
        return (chan, lax.rem(seq + d, NSEQ))

    def make_a(d):
        return pltpu.make_async_remote_copy(
            src_ref=r.stat.at[1], dst_ref=r.along.at[d],
            send_sem=sem_a.at[d], recv_sem=recv_a.at[d], device_id=seq_peer(d), device_id_type=MESH,
        )

    wait_along = run(NSEQ, make_a)
    results = []

    def leave(n):
        for i, (src, dst) in enumerate(((r.o_val, r.h_val), (r.o_gin, r.h_gin), (r.o_gout, r.h_gout))):
            copy = pltpu.make_async_copy(src.at[n], dst.at[n], out_sem.at[3 * n + i])
            copy.start()
            results.append(copy)

    finish(r, 0)
    leave(0)

    def settle(p, carry):
        for i in range(5):
            near_block(p, i).wait_recv()
        row = pl.multiple_of(row_of(x, z), ABLK)
        for i in range(2):
            c = 2 * p + i
            total = r.gk[c, pl.ds(row, ABLK), :]
            for k in range(5):
                total = total + r.side[p, k, i]
            r.total[pl.ds(pl.multiple_of(c * ABLK, ABLK), ABLK), :] = total
        return carry

    lax.fori_loop(0, CH // 2, settle, 0)
    wait_along()
    along = r.stat[1]
    for d in range(1, NSEQ):
        along = along + r.along[d]
    along = jnp.sum(along, axis=1, keepdims=True) * (1.0 / L)
    norm = jnp.sqrt(jnp.sum(r.stat[0], axis=1, keepdims=True) + EPSILON)
    scale_gk = jnp.broadcast_to((1.0 / L) / norm, (CH, B))
    scale_raw = jnp.broadcast_to(along / (norm * norm * norm), (CH, B))

    def sent(j, carry):
        for i in range(5):
            gather(i, j).wait_send()
            near_block(j, i).wait_send()
        for i in range(4):
            far_half(j, i // 2, i % 2).wait_send()
        return carry

    net_backward(r, seq, scale_gk, scale_raw)
    pack_shares(r)

    def make_b(d):
        return pltpu.make_async_remote_copy(
            src_ref=r.share.at[lax.rem(seq + d, NSEQ)], dst_ref=r.first.at[d],
            send_sem=sem_b.at[d], recv_sem=recv_b.at[d], device_id=seq_peer(d), device_id_type=MESH,
        )

    def make_c(d):
        return pltpu.make_async_remote_copy(
            src_ref=r.second.at[chan], dst_ref=r.second.at[chan], send_sem=sem_c.at[d], recv_sem=recv_c.at[d],
            device_id=(lax.rem(chan + d, NCHAN), seq), device_id_type=MESH,
        )

    def make_d(d):
        return pltpu.make_async_remote_copy(
            src_ref=r.third.at[seq], dst_ref=r.third.at[seq], send_sem=sem_d.at[d], recv_sem=recv_d.at[d],
            device_id=seq_peer(d), device_id_type=MESH,
        )

    wait = run(NSEQ, make_b)
    finish(r, 1)
    leave(1)
    wait()
    total = r.share[seq]
    for d in range(1, NSEQ):
        total = total + r.first[d]
    factor = 1.0 / math.sqrt(16 * L)
    total = total * factor
    r.second[chan] = total
    r.g_skip[...] = to_row(total[:, 241:242])
    run(NCHAN, make_c)()
    total = r.second[0]
    for c in range(1, NCHAN):
        total = total + r.second[c]
    r.third[seq] = total
    run(NSEQ, make_d)()
    lax.fori_loop(0, CH // 2, sent, 0)
    for i in range(4):
        relay(i).wait_send()
    for copy in results:
        copy.wait()


def write_kernel(
    i_val, i_gin, i_gout, i_second, i_third, skip,
    o_val, o_gin, o_gout, o_skip, o_in, o_bin, o_mid, o_bmid, o_out, o_rate,
    stage, second, third, g_skip, g_in, g_bin, g_mid, g_bmid, g_out, g_rate, in_sem, out_sem, small_sem,
):
    loads, stores = [], []
    for i, (src, dst) in enumerate(((i_val, o_val), (i_gin, o_gin), (i_gout, o_gout))):
        for n in range(2):
            loads.append(pltpu.make_async_copy(src.at[n], stage.at[i, n], in_sem.at[2 * i + n]))
            stores.append(pltpu.make_async_copy(stage.at[i, n], dst.at[n], out_sem.at[2 * i + n]))
    small = [
        pltpu.make_async_copy(i_second, second, small_sem.at[0]),
        pltpu.make_async_copy(i_third, third, small_sem.at[1]),
        pltpu.make_async_copy(skip, g_skip, small_sem.at[2]),
    ]
    for copy in small + loads:
        copy.start()
    for load, store in zip(loads, stores):
        load.wait()
        store.start()
    for copy in small:
        copy.wait()
    hidden = third[...].reshape(64, 256)
    g_mid[0] = hidden[:, 0:64]
    g_mid[1] = pltpu.roll(hidden[:, 0:128], 64, 1)[:, 0:64]
    flat = jnp.transpose(hidden[:, 128:256])
    g_in[...] = flat[0:33, :]
    g_bin[...] = flat[33:34, :]
    g_bmid[...] = flat[34:36, :]
    own = jnp.transpose(second[...].reshape(128, 256)[:, 128:256])
    g_out[...] = own[48:112, :]
    g_rate[...] = own[112:113, :]
    pairs = (
        (g_skip, o_skip), (g_in, o_in), (g_bin, o_bin), (g_mid, o_mid), (g_bmid, o_bmid), (g_out, o_out),
        (g_rate, o_rate),
    )
    for i, (src, dst) in enumerate(pairs):
        copy = pltpu.make_async_copy(src, dst, small_sem.at[3 + i])
        copy.start()
        stores.append(copy)
    for copy in stores:
        copy.wait()


def sds(shape, dtype=F32):
    return jax.ShapeDtypeStruct(shape, dtype)


VM = pl.BlockSpec(memory_space=pltpu.VMEM)
HB = pl.BlockSpec(memory_space=pltpu.HBM)
DMA = pltpu.SemaphoreType.DMA


def to_natural(x):
    return x.reshape(2, CH, A, B).transpose(0, 2, 1, 3)


def from_natural(x):
    return x.transpose(0, 2, 1, 3).reshape(2, CH, L)


def local(
    value, gate_in, gate_out, cotangent, skip_gain,
    weight_in, bias_in, weight_mid, bias_mid, weight_out, decay_rate,
):
    small = (
        row_constants(), weight_in.T, bias_in.reshape(1, 64), weight_mid, bias_mid, weight_out.T,
        decay_rate.reshape(1, 128), skip_gain.reshape(1, CH),
    )
    large = tuple(to_natural(x) for x in (value, gate_in, cotangent, gate_out))
    big = sds(BIG, LOW)
    o_val, o_gin, o_gout, second, third, g_skip = pl.pallas_call(
        main_kernel,
        out_shape=[big, big, big, sds((NCHAN, 8, 256)), sds((NSEQ, 8, 256)), sds((1, CH))],
        in_specs=[HB] * N_LOCAL,
        out_specs=[HB] * 3 + [VM] * 3,
        scratch_shapes=[pltpu.VMEM(shape, dtype) for shape, dtype in SCRATCH.values()]
        + [
            DMA((N_LOCAL,)), DMA((6,)), DMA((5, 4)), DMA((5, 4)), DMA((4,)), DMA((4,)),
            DMA((4, 4)), DMA((4, 4)), DMA((4, 5)), DMA((4, 5)), DMA((NSEQ,)), DMA((NSEQ,)),
            DMA((NSEQ,)), DMA((NSEQ,)), DMA((NCHAN,)), DMA((NCHAN,)), DMA((NSEQ,)), DMA((NSEQ,)),
        ],
        compiler_params=pltpu.CompilerParams(
            collective_id=0, has_side_effects=True, vmem_limit_bytes=VMEM_MAIN
        ),
        name="hyena_backward",
    )(*small, *transform_tables(), *large)
    o_val, o_gin, o_gout, g_skip, g_in, g_bin, g_mid, g_bmid, g_out, g_rate = pl.pallas_call(
        write_kernel,
        out_shape=[
            big, big, big, sds((1, CH)), sds((33, 64)), sds((1, 64)), sds((2, 64, 64)), sds((2, 64)),
            sds((64, 128)), sds((1, 128)),
        ],
        in_specs=[HB] * 6,
        out_specs=[HB] * 10,
        scratch_shapes=[
            pltpu.VMEM((3,) + BIG, LOW), pltpu.VMEM((NCHAN, 8, 256), F32), pltpu.VMEM((NSEQ, 8, 256), F32),
            pltpu.VMEM((1, CH), F32), pltpu.VMEM((33, 64), F32), pltpu.VMEM((1, 64), F32),
            pltpu.VMEM((2, 64, 64), F32), pltpu.VMEM((2, 64), F32), pltpu.VMEM((64, 128), F32),
            pltpu.VMEM((1, 128), F32),
            DMA((6,)), DMA((6,)), DMA((10,)),
        ],
        compiler_params=pltpu.CompilerParams(vmem_limit_bytes=VMEM_MAIN),
        name="write_results",
    )(o_val, o_gin, o_gout, second, third, g_skip)
    return (
        from_natural(o_val), from_natural(o_gin), from_natural(o_gout), g_skip.reshape(CH),
        g_in.T, g_bin.reshape(64), g_mid, g_bmid, g_out.T, g_rate.reshape(128),
    )


def solution(mesh):
    return jax.shard_map(
        local,
        mesh=mesh,
        in_specs=(
            P("seq", "chan", None), P("seq", "chan", None), P("seq", "chan", None), P("seq", "chan", None),
            P("chan"), P(), P(), P(), P(), P(), P(),
        ),
        out_specs=(
            P("seq", "chan", None), P("seq", "chan", None), P("seq", "chan", None),
            P("chan"), P(), P(), P(), P(), P(), P(),
        ),
        check_vma=False,
    )
```

```python
import functools
import math

import jax
import jax.numpy as jnp
import numpy as np
from jax import lax
from jax.experimental import pallas as pl
from jax.experimental.pallas import tpu as pltpu
from jax.sharding import PartitionSpec as P

EPSILON = 1e-06
HIGHEST = lax.Precision.HIGHEST
L = 32768
A = 256
B = 128
CH = 8
NSEQ = 8
NCHAN = 16
ABLK = A // NSEQ
TB = L // NSEQ
CHUNK = 1024
LOW = jnp.bfloat16
F32 = jnp.float32
MESH = pl.DeviceIdType.MESH


def band_table(length, bands):
    highest = length / 4.0
    return np.array(
        [math.floor(highest ** (number / (bands - 1)) + 0.5) for number in range(bands)], np.int64
    )


def row_constants():
    freq = np.zeros((48, 128), np.int32)
    off = np.zeros((48, 128), np.int32)
    bands = band_table(L, 16)
    freq[1:17] = bands[:, None]
    off[1:17] = L // 4
    freq[17:33] = bands[:, None]
    return np.stack([freq, off])


def transform_tables():
    k = np.arange(A)[:, None]
    rows = 2.0 * np.pi * (((4 * k + 1) * np.arange(A)[None, :]) % 1024) / 1024.0
    w1 = np.concatenate([np.cos(rows), -np.sin(rows)], axis=0)
    turn = 2.0 * np.pi * (((4 * k + 1) * np.arange(B)[None, :]) % (4 * L)) / (4.0 * L)
    q = np.arange(B)
    cols = 2.0 * np.pi * ((q[:, None] * q[None, :]) % B) / B
    c, s = np.cos(cols), np.sin(cols)
    fwd = np.block([[c, -s], [s, c]])
    inv = np.block([[c, s], [-s, c]])
    low = np.dtype(LOW)
    return (
        w1.astype(low),
        w1.T.astype(low),
        fwd.astype(low),
        inv.astype(low),
        np.stack([np.cos(turn), np.sin(turn)]).astype(np.float32),
    )


def poly_fit():
    x = (np.cos(np.pi * (np.arange(64) + 0.5) / 64) + 1) / 2 * (np.pi / 2 * 1.002) ** 2
    r = np.sqrt(x)
    sin_c = np.polynomial.polynomial.polyfit(x, np.sin(r) / r, 4)
    cos_c = np.polynomial.polynomial.polyfit(x, np.cos(r), 5)
    return [float(v) for v in sin_c], [float(v) for v in cos_c]


SIN_C, COS_C = poly_fit()


def horner(x, coefs):
    acc = jnp.full_like(x, coefs[-1])
    for value in coefs[-2::-1]:
        acc = acc * x + value
    return acc


def sin_small(r):
    return r * horner(r * r, SIN_C)


def sin_cos(z):
    n = jnp.floor(z * (1.0 / math.pi) + 0.5)
    r = z - n * 3.140625
    r = r - n * 9.67653589793e-4
    half = n * 0.5
    sign = 1.0 - 4.0 * (half - jnp.floor(half))
    r2 = r * r
    return sign * (r * horner(r2, SIN_C)), sign * horner(r2, COS_C)


def dot_full(x, y):
    return jnp.dot(x, y, precision=HIGHEST, preferred_element_type=F32)


def dot_nt(x, y, precision=None):
    return lax.dot_general(x, y, (((1,), (1,)), ((), ())), precision=precision, preferred_element_type=F32)


def dot_tn(x, y, precision=None):
    return lax.dot_general(x, y, (((0,), (0,)), ((), ())), precision=precision, preferred_element_type=F32)


def low_dot(x, y):
    return jnp.dot(x, y, preferred_element_type=F32)


def split(x):
    hi = x.astype(LOW)
    return hi, (x - hi.astype(F32)).astype(LOW)


def iota(shape, dim):
    return lax.broadcasted_iota(jnp.int32, shape, dim)


def to_column(row, size, shift):
    n = row.shape[1]
    pick = iota((size, n), 0) + shift == iota((size, n), 1)
    return jnp.sum(jnp.where(pick, jnp.broadcast_to(row, (size, n)), 0.0), axis=1, keepdims=True)


def to_row(col):
    n = col.shape[0]
    pick = iota((n, n), 0) == iota((n, n), 1)
    return jnp.sum(jnp.where(pick, jnp.broadcast_to(col, (n, n)), 0.0), axis=0, keepdims=True)


def repeat_matrix(rows, period, times):
    shape = (rows, period * times)
    j = iota(shape, 1)
    hit = j == iota(shape, 0)
    for m in range(1, times):
        hit = hit | (j == iota(shape, 0) + m * period)
    return jnp.where(hit, 1.0, 0.0)


def hi_hi_lo(w, period):
    hi = w.astype(LOW).astype(F32)
    lane = iota(w.shape, 1)
    out = jnp.where(lane < 2 * period, hi, jnp.where(lane < 3 * period, w - hi, 0.0))
    return out.astype(LOW)


class Refs:
    def __init__(self, **refs):
        self.__dict__.update(refs)


def prepare_weights(r, chan):
    first = jnp.where(iota((8, 64), 0) == 1, jnp.broadcast_to(r.b_in[...], (8, 64)), 0.0)
    r.w_pad[0:32, :] = r.w_in[0:32, :]
    r.w_pad[32:40, :] = jnp.where(iota((8, 64), 0) == 0, jnp.broadcast_to(r.w_in[32:33, :], (8, 64)), first)
    r.w_pad[40:48, :] = jnp.zeros((8, 64), F32)
    r.k_in[...] = hi_hi_lo(dot_tn(r.w_pad[...], repeat_matrix(48, 48, 3), HIGHEST), 48)
    rep = repeat_matrix(64, 64, 3)
    for i in range(2):
        w = r.w_mid[i]
        r.k_mid[i] = hi_hi_lo(dot_full(w, rep), 64)
        r.k_back[i] = hi_hi_lo(dot_tn(w, rep, HIGHEST), 64)
    own = jnp.where(iota((CH, 128), 1) == iota((CH, 128), 0) + chan * CH, 1.0, 0.0)
    w_own = dot_nt(own, r.w_out[...], HIGHEST)
    r.k_out[...] = hi_hi_lo(dot_full(w_own, rep), 64)
    r.k_outback[...] = hi_hi_lo(dot_tn(w_own, repeat_matrix(CH, CH, 4), HIGHEST), CH)
    r.rate_col[...] = jnp.broadcast_to(to_column(r.rate[...], CH, chan * CH), (CH, 128))
    r.bias_col[0] = jnp.broadcast_to(to_column(r.b_mid[0:1, :], 64, 0), (64, 128))
    r.bias_col[1] = jnp.broadcast_to(to_column(r.b_mid[1:2, :], 64, 0), (64, 128))


def wide(block, times):
    return jnp.concatenate([block] * times, axis=1)


def fraction(seq, base):
    pos = seq * TB + base + iota((CH, CHUNK), 1)
    return pos.astype(F32) * (1.0 / L)


def net_forward(r, seq, send):
    per = CHUNK // 128

    def step(j, carry):
        base = pl.multiple_of(j * CHUNK, CHUNK)
        lanes = pl.ds(base, CHUNK)
        pos = seq * TB + base + iota((48, CHUNK), 1)
        row = iota((48, CHUNK), 0)
        phase = ((wide(r.bands[0], per) * pos + (wide(r.bands[1], per) + L // 2)) & (L - 1)) - L // 2
        phase = jnp.where(phase > L // 4, L // 2 - phase, phase)
        phase = jnp.where(phase < -(L // 4), -(L // 2) - phase, phase)
        wave = sin_small(phase.astype(F32) * (2.0 * math.pi / L))
        frac = pos.astype(F32) * (1.0 / L)
        hi, lo = split(jnp.where(row == 0, frac, jnp.where(row == 33, 1.0, wave)))
        r.feat[0:48, lanes] = hi
        r.feat[48:64, lanes] = jnp.zeros((16, CHUNK), LOW)
        r.feat[64:112, lanes] = lo
        r.feat[112:128, lanes] = jnp.zeros((16, CHUNK), LOW)
        z = low_dot(r.k_in[...], jnp.concatenate([hi, lo, hi], axis=0))
        for layer in range(3):
            s, c = sin_cos(z)
            r.der[layer, :, lanes] = c
            hi, lo = split(s)
            r.act[layer, 0:64, lanes] = hi
            r.act[layer, 64:128, lanes] = lo
            x = jnp.concatenate([hi, lo, hi], axis=0)
            if layer < 2:
                z = low_dot(r.k_mid[layer], x) + wide(r.bias_col[layer], per)
        raw = low_dot(r.k_out[...], x) * jnp.exp(-wide(r.rate_col[...], per) * frac[0:CH, :])
        for i in range(per):
            r.raw_all[seq * ABLK + j * per + i] = raw[:, 128 * i : 128 * i + 128]
        send(j)
        return carry

    lax.fori_loop(0, TB // CHUNK, step, 0)


def net_backward(r, seq, scale_gk, scale_raw):
    per = CHUNK // 128
    r.acc[...] = jnp.zeros_like(r.acc)
    r.acc_out[...] = jnp.zeros_like(r.acc_out)
    r.acc_bias[...] = jnp.zeros_like(r.acc_bias)
    r.acc_rate[...] = jnp.zeros_like(r.acc_rate)

    def lane_sum(x):
        total = x[:, 0:128]
        for i in range(1, per):
            total = total + x[:, 128 * i : 128 * i + 128]
        return total

    def step(j, carry):
        lanes = pl.ds(pl.multiple_of(j * CHUNK, CHUNK), CHUNK)
        start = seq * ABLK + j * per
        grad = jnp.concatenate([r.total[pl.ds(j * per + i, CH, stride=ABLK), :] for i in range(per)], axis=1)
        raw = jnp.concatenate([r.raw_all[start + i] for i in range(per)], axis=1)
        grad = grad * wide(scale_gk, per) - raw * wide(scale_raw, per)
        frac = fraction(seq, j * CHUNK)
        r.acc_rate[...] -= lane_sum(grad * raw * frac)
        shaped = grad * jnp.exp(-wide(r.rate_col[...], per) * frac)
        hi = shaped.astype(LOW).astype(F32)
        lo = shaped - hi
        pair = jnp.concatenate([hi, lo], axis=0).astype(LOW)
        r.acc_out[...] += dot_nt(pair, r.act[2, :, lanes])
        d = low_dot(r.k_outback[...], jnp.concatenate([hi, lo, hi, jnp.zeros_like(hi)], axis=0).astype(LOW))
        for layer in (2, 1, 0):
            d = d * r.der[layer, :, lanes]
            hi, lo = split(d)
            pair = jnp.concatenate([hi, lo], axis=0)
            if layer:
                r.acc_bias[layer - 1] += lane_sum(d)
                r.acc[layer] += dot_nt(pair, r.act[layer - 1, :, lanes])
                d = low_dot(r.k_back[layer - 1], jnp.concatenate([hi, lo, hi], axis=0))
            else:
                r.acc[0] += dot_nt(pair, r.feat[:, lanes])
        return carry

    lax.fori_loop(0, TB // CHUNK, step, 0)


def fold_halves(x):
    n = x.shape[0] // 2
    total = x[0:n] + x[n:]
    return total + pltpu.roll(total, 64, 1)


def pack_shares(r):
    lane = iota((64, 128), 1)
    r.block[0] = jnp.where(lane < 64, fold_halves(r.acc[1]), fold_halves(r.acc[2]))
    block = fold_halves(r.acc[0])
    block = jnp.where(lane == 34, jnp.sum(r.acc_bias[0], axis=1, keepdims=True), block)
    r.block[1] = jnp.where(lane == 35, jnp.sum(r.acc_bias[1], axis=1, keepdims=True), block)
    lane = iota((CH, 128), 1)
    own = pltpu.roll(fold_halves(r.acc_out[...]), 48, 1)
    own = jnp.where(lane == 112, jnp.sum(r.acc_rate[...], axis=1, keepdims=True), own)
    own = jnp.where(lane == 113, r.skip_part[...], own)

    def place(s, carry):
        rows = pl.ds(pl.multiple_of(8 * s, 8), 8)
        r.share[s, :, 0:128] = r.block[0, rows, :]
        r.share[s, :, 128:256] = jnp.where(lane < 48, r.block[1, rows, :], own)
        return carry

    lax.fori_loop(0, NSEQ, place, 0)


def to_low(x):
    return x.astype(LOW)


def channel_rows(c):
    return pl.ds(c, A, stride=CH)


def forward_pair(r, x):
    tc, ts = r.turn[0], r.turn[1]
    g = low_dot(r.w1[...], x)
    parts = []
    for n in range(2):
        re, im = g[0:A, n * B : n * B + B], g[A:, n * B : n * B + B]
        parts.append(jnp.concatenate([to_low(re * tc + im * ts), to_low(im * tc - re * ts)], axis=1))
    f = low_dot(jnp.concatenate(parts, axis=0), r.fwd[...])
    return f[0:A], f[A:]


def inverse_pair(r, specs):
    tc, ts = r.turn[0], r.turn[1]
    s = jnp.concatenate([jnp.concatenate([to_low(re), to_low(im)], axis=1) for re, im in specs], axis=0)
    t = low_dot(s, r.inv[...])
    cols = []
    for n in range(2):
        re, im = t[n * A : n * A + A, 0:B], t[n * A : n * A + A, B:]
        cols.append(jnp.concatenate([to_low(re * tc - im * ts), to_low(re * ts + im * tc)], axis=0))
    y = low_dot(r.w1t[...], jnp.concatenate(cols, axis=1))
    return y[:, 0:B], y[:, B:]


BLK = 16
VMEM_MAIN = 56 << 20


def gate_products(r, n):
    def step(j, acc):
        part = pl.ds(j * BLK, BLK)
        rows = pl.ds(pl.multiple_of(j * (BLK * CH), BLK * CH), BLK * CH)
        m = r.val[n, part].astype(F32) * r.gin[n, part].astype(F32)
        g = r.cot[n, part].astype(F32) * r.gout[n, part].astype(F32)
        r.mixed[n, rows, :] = m.reshape(BLK * CH, B)
        r.inner[n, rows, :] = g.reshape(BLK * CH, B)
        return acc + jnp.sum(m * g, axis=0)

    return lax.fori_loop(0, A // BLK, step, jnp.zeros((CH, B), F32))


def spectra(r, p):
    cross = []
    for i in range(2):
        c = 2 * p + i
        rows = channel_rows(c)
        fm = forward_pair(r, jnp.concatenate([to_low(r.mixed[n, rows, :]) for n in range(2)], axis=1))
        fg = forward_pair(r, jnp.concatenate([to_low(r.inner[n, rows, :]) for n in range(2)], axis=1))
        re = im = None
        for n in range(2):
            r.f_mixed[c, n] = fm[n]
            r.f_inner[c, n] = fg[n]
            mr, mi = fm[n][:, 0:B], fm[n][:, B:]
            gr, gi = fg[n][:, 0:B], fg[n][:, B:]
            pr, pi = mr * gr + mi * gi, mr * gi - mi * gr
            re, im = (pr, pi) if re is None else (re + pr, im + pi)
        cross.append((re, im))
    ys = inverse_pair(r, cross)
    for i in range(2):
        r.gk[2 * p + i] = ys[i]


def channel_stats(r, c):
    x = r.raw_flat[channel_rows(c), :]
    r.stat[0, pl.ds(c, 1), :] = jnp.sum(x * x, axis=0, keepdims=True)
    r.stat[1, pl.ds(c, 1), :] = jnp.sum(x * r.gk[c], axis=0, keepdims=True)


def filter_products(r, p):
    kernels = []
    for i in range(2):
        c = 2 * p + i
        square = jnp.sum(r.stat[0, pl.ds(c, 1), :], axis=1, keepdims=True)
        kernels.append(to_low(r.raw_flat[channel_rows(c), :] * (1.0 / jnp.sqrt(square + EPSILON))))
    fk = forward_pair(r, jnp.concatenate(kernels, axis=1))
    for i in range(2):
        c = 2 * p + i
        rows = channel_rows(c)
        kr, ki = fk[i][:, 0:B] * (1.0 / L), fk[i][:, B:] * (1.0 / L)
        specs = []
        for n in range(2):
            mr, mi = r.f_mixed[c, n, :, 0:B], r.f_mixed[c, n, :, B:]
            specs.append((mr * kr - mi * ki, mr * ki + mi * kr))
        ys = inverse_pair(r, specs)
        for n in range(2):
            r.conv[n, rows, :] = ys[n]
        specs = []
        for n in range(2):
            gr, gi = r.f_inner[c, n, :, 0:B], r.f_inner[c, n, :, B:]
            specs.append((gr * kr + gi * ki, gi * kr - gr * ki))
        ys = inverse_pair(r, specs)
        for n in range(2):
            r.back[n, rows, :] = ys[n]


def finish(r, n):
    gain = jnp.broadcast_to(to_column(r.skip[...], CH, 0), (CH, B))[None]

    def step(j, carry):
        part = pl.ds(j * BLK, BLK)
        rows = pl.ds(pl.multiple_of(j * (BLK * CH), BLK * CH), BLK * CH)
        shape = (BLK, CH, B)
        full = r.conv[n, rows, :].reshape(shape) + gain * r.mixed[n, rows, :].reshape(shape)
        r.o_gout[n, part] = to_low(r.cot[n, part].astype(F32) * full)
        full = r.back[n, rows, :].reshape(shape) + gain * r.inner[n, rows, :].reshape(shape)
        r.o_val[n, part] = to_low(full * r.gin[n, part].astype(F32))
        r.o_gin[n, part] = to_low(full * r.val[n, part].astype(F32))
        return carry

    lax.fori_loop(0, A // BLK, step, 0)


SMALL = ("bands", "w_in", "b_in", "w_mid", "b_mid", "w_out", "rate", "skip")
TABLES = ("w1", "w1t", "fwd", "inv", "turn")
LARGE = ("val", "gin", "cot", "gout")
OUTS = ("h_val", "h_gin", "h_gout", "own", "third", "g_skip")
BIG = (2, A, CH, B)
FULL = (2, A * CH, B)
SCRATCH = {
    "bands": ((2, 48, 128), jnp.int32),
    "w_in": ((33, 64), F32),
    "b_in": ((1, 64), F32),
    "w_mid": ((2, 64, 64), F32),
    "b_mid": ((2, 64), F32),
    "w_out": ((64, 128), F32),
    "rate": ((1, 128), F32),
    "skip": ((1, CH), F32),
    "w1": ((2 * A, A), LOW),
    "w1t": ((A, 2 * A), LOW),
    "fwd": ((2 * B, 2 * B), LOW),
    "inv": ((2 * B, 2 * B), LOW),
    "turn": ((2, A, B), F32),
    "val": (BIG, LOW),
    "gin": (BIG, LOW),
    "cot": (BIG, LOW),
    "gout": (BIG, LOW),
    "o_val": (BIG, LOW),
    "o_gin": (BIG, LOW),
    "o_gout": (BIG, LOW),
    "w_pad": ((48, 64), F32),
    "k_in": ((64, 144), LOW),
    "k_mid": ((2, 64, 192), LOW),
    "k_back": ((2, 64, 192), LOW),
    "k_out": ((CH, 192), LOW),
    "k_outback": ((64, 4 * CH), LOW),
    "rate_col": ((CH, 128), F32),
    "bias_col": ((2, 64, 128), F32),
    "feat": ((128, TB), LOW),
    "act": ((3, 128, TB), LOW),
    "der": ((3, 64, TB), F32),
    "raw_all": ((A, CH, B), F32),
    "total": ((CH * ABLK, B), F32),
    "half": ((CH // 2, 2, 2, 2, ABLK // 2, B), F32),
    "side_out": ((CH // 2, 2, 2, 2, ABLK, B), F32),
    "side": ((CH // 2, 5, 2, ABLK, B), F32),
    "stat": ((2, CH, B), F32),
    "along": ((NSEQ, CH, B), F32),
    "mixed": (FULL, F32),
    "inner": (FULL, F32),
    "f_mixed": ((CH, 2, A, 2 * B), F32),
    "f_inner": ((CH, 2, A, 2 * B), F32),
    "gk": ((CH, A, B), F32),
    "conv": (FULL, F32),
    "back": (FULL, F32),
    "acc": ((3, 128, 128), F32),
    "acc_out": ((16, 128), F32),
    "acc_bias": ((2, 64, 128), F32),
    "acc_rate": ((CH, 128), F32),
    "skip_part": ((CH, 1), F32),
    "block": ((2, 64, 128), F32),
    "share": ((NSEQ, 8, 256), F32),
    "first": ((NSEQ, 8, 256), F32),
    "second": ((16, 8, 256), F32),
}
N_LOCAL = len(SMALL) + len(TABLES) + len(LARGE)


def main_kernel(*refs):
    ins = refs[:N_LOCAL]
    outs = refs[N_LOCAL : N_LOCAL + len(OUTS)]
    names = list(SCRATCH)
    scratch = refs[N_LOCAL + len(OUTS) :]
    r = Refs(**dict(zip(OUTS, outs)), **dict(zip(names, scratch)))
    (load_sem, out_sem, ag_send, ag_recv, relay_send, relay_recv, half_send, half_recv, rs_send, rs_recv,
     sem_a, recv_a, sem_b, recv_b, sem_c, recv_c, sem_d, recv_d) = scratch[len(names) :]
    r.raw_flat = r.raw_all.reshape(A * CH, B)
    chan, seq = lax.axis_index("chan"), lax.axis_index("seq")
    barrier = pltpu.get_barrier_semaphore()

    def signal(device):
        pl.semaphore_signal(barrier, inc=1, device_id=device, device_id_type=MESH)

    x, z = lax.div(seq, 2), lax.rem(seq, 2)
    yz, core = lax.div(chan, 2), lax.rem(chan, 2)
    first_id, second_id = 2 * x + core, 2 * yz + z

    def seq_peer(d):
        return (chan, lax.rem(seq + d, NSEQ))

    def first_peer(d):
        to = lax.rem(first_id + d, 8)
        return (2 * yz + lax.rem(to, 2), 2 * lax.div(to, 2) + z)

    def second_peer(d):
        to = lax.rem(second_id + d, 16)
        return (2 * lax.div(to, 2) + core, 2 * x + lax.rem(to, 2))

    def hail(d, carry):
        signal(seq_peer(d))
        signal(first_peer(d))
        return carry

    def hail_second(d, carry):
        signal(second_peer(d))
        return carry

    loads = {}
    for i, name in enumerate(SMALL + TABLES + LARGE):
        loads[name] = pltpu.make_async_copy(ins[i], getattr(r, name), load_sem.at[i])
    for name in SMALL:
        loads[name].start()
    lax.fori_loop(1, 8, hail, 0)
    lax.fori_loop(1, 16, hail_second, 0)
    for name in LARGE + TABLES:
        loads[name].start()
    for name in SMALL:
        loads[name].wait()

    xr, xl, xo = lax.rem(x + 1, 4), lax.rem(x + 3, 4), lax.rem(x + 2, 4)
    other = 1 - z
    near = (
        (chan, 2 * x + other), (chan, 2 * xr + z), (chan, 2 * xr + other), (chan, 2 * xl + z), (chan, 2 * xl + other)
    )
    to_r, to_l = near[1], near[3]
    half = ABLK // 2
    piece = CHUNK // 128
    n_piece = ABLK // piece

    def row_of(xx, zz):
        return (2 * xx + zz) * ABLK

    def gather(i, j):
        part = r.raw_all.at[pl.ds(row_of(x, z) + j * piece, piece)]
        return pltpu.make_async_remote_copy(
            src_ref=part, dst_ref=part, send_sem=ag_send.at[i, j], recv_sem=ag_recv.at[i, j],
            device_id=near[i], device_id_type=MESH,
        )

    def send_chunk(j):
        for i in range(5):
            gather(i, j).start()

    def relay(i):
        row = row_of(xl if i < 2 else xr, (z, other)[i % 2]) + (0 if i < 2 else half)
        part = r.raw_all.at[pl.ds(row, half)]
        return pltpu.make_async_remote_copy(
            src_ref=part, dst_ref=part, send_sem=relay_send.at[i], recv_sem=relay_recv.at[i],
            device_id=to_r if i < 2 else to_l, device_id_type=MESH,
        )

    def arrived(i, start, stop):
        def step(j, carry):
            gather(i, j).wait_recv()
            return carry

        lax.fori_loop(start, stop, step, 0)

    zs = (other, z)

    def rows_at(p, row, count):
        return r.gk.at[pl.ds(2 * p, 2), pl.ds(pl.multiple_of(row, half), count)]

    def far_half(p, w, h):
        return pltpu.make_async_remote_copy(
            src_ref=rows_at(p, row_of(xo, zs[w]) + h * half, half), dst_ref=r.half.at[p, w, h],
            send_sem=half_send.at[p, 2 * w + h], recv_sem=half_recv.at[p, 2 * w + h],
            device_id=(to_r, to_l)[h], device_id_type=MESH,
        )

    def near_block(p, i):
        w = i % 2
        src = rows_at(p, row_of(x, other), ABLK) if i == 0 else r.side_out.at[p, w, (i - 1) // 2]
        return pltpu.make_async_remote_copy(
            src_ref=src, dst_ref=r.side.at[p, i], send_sem=rs_send.at[p, i], recv_sem=rs_recv.at[p, i],
            device_id=near[i], device_id_type=MESH,
        )

    def scatter_far(p):
        for w in range(2):
            for h in range(2):
                far_half(p, w, h).start()
        near_block(p, 0).start()

    def scatter_near(p):
        for w in range(2):
            for h in range(2):
                far_half(p, w, h).wait_recv()
                row = row_of((xr, xl)[h], zs[w])
                for i in range(2):
                    mine = r.gk[2 * p + i, pl.ds(pl.multiple_of(row, half), half), :]
                    rest = r.gk[2 * p + i, pl.ds(pl.multiple_of(row + half, half), half), :]
                    extra = r.half[p, w, h, i]
                    r.side_out[p, w, h, i, 0:half, :] = mine + extra if h == 0 else mine
                    r.side_out[p, w, h, i, half:, :] = rest if h == 0 else rest + extra
        for i in range(1, 5):
            near_block(p, i).start()

    prepare_weights(r, chan)
    pl.semaphore_wait(barrier, 7 + 7 + 15)
    net_forward(r, seq, send_chunk)

    for name in LARGE:
        loads[name].wait()
    acc = gate_products(r, 0)
    acc = acc + gate_products(r, 1)
    r.skip_part[...] = jnp.sum(acc, axis=1, keepdims=True)
    for name in TABLES:
        loads[name].wait()
    for i in range(2):
        arrived(1 + i, 0, n_piece // 2)
        relay(i).start()

    spectra(r, 0)
    scatter_far(0)
    for i in range(2):
        arrived(3 + i, n_piece // 2, n_piece)
        relay(2 + i).start()

    spectra(r, 1)
    scatter_far(1)

    def pair_step(p, carry):
        spectra(r, p)
        scatter_far(p)
        scatter_near(p - 2)
        return carry

    lax.fori_loop(2, CH // 2, pair_step, 0)
    arrived(0, 0, n_piece)
    for i in range(2):
        arrived(1 + i, n_piece // 2, n_piece)
        arrived(3 + i, 0, n_piece // 2)
    for i in range(4):
        relay(i).wait_recv()

    def stats_step(c, carry):
        channel_stats(r, c)
        return carry

    lax.fori_loop(0, CH, stats_step, 0)

    def run(size, make):
        def start(d, carry):
            make(d).start()
            return carry

        def wait(d, carry):
            make(d).wait()
            return carry

        lax.fori_loop(1, size, start, 0)
        return lambda: lax.fori_loop(1, size, wait, 0)

    def make_a(d):
        return pltpu.make_async_remote_copy(
            src_ref=r.stat.at[1], dst_ref=r.along.at[d],
            send_sem=sem_a.at[d], recv_sem=recv_a.at[d], device_id=seq_peer(d), device_id_type=MESH,
        )

    wait_along = run(NSEQ, make_a)

    def product_step(p, carry):
        filter_products(r, p)
        scatter_near(p + CH // 2 - 2)
        return carry

    lax.fori_loop(0, 2, product_step, 0)

    def last_step(p, carry):
        filter_products(r, p)
        return carry

    lax.fori_loop(2, CH // 2, last_step, 0)
    results = []

    def leave(n):
        for i, (src, dst) in enumerate(((r.o_val, r.h_val), (r.o_gin, r.h_gin), (r.o_gout, r.h_gout))):
            copy = pltpu.make_async_copy(src.at[n], dst.at[n], out_sem.at[3 * n + i])
            copy.start()
            results.append(copy)

    finish(r, 0)
    leave(0)

    def settle(p, carry):
        for i in range(5):
            near_block(p, i).wait_recv()
        row = pl.multiple_of(row_of(x, z), ABLK)
        for i in range(2):
            c = 2 * p + i
            total = r.gk[c, pl.ds(row, ABLK), :]
            for k in range(5):
                total = total + r.side[p, k, i]
            r.total[pl.ds(pl.multiple_of(c * ABLK, ABLK), ABLK), :] = total
        return carry

    lax.fori_loop(0, CH // 2, settle, 0)
    wait_along()
    along = r.stat[1]
    for d in range(1, NSEQ):
        along = along + r.along[d]
    along = jnp.sum(along, axis=1, keepdims=True) * (1.0 / L)
    norm = jnp.sqrt(jnp.sum(r.stat[0], axis=1, keepdims=True) + EPSILON)
    scale_gk = jnp.broadcast_to((1.0 / L) / norm, (CH, B))
    scale_raw = jnp.broadcast_to(along / (norm * norm * norm), (CH, B))

    def sent(j, carry):
        for i in range(5):
            gather(i, j).wait_send()
            near_block(j, i).wait_send()
        for i in range(4):
            far_half(j, i // 2, i % 2).wait_send()
        return carry

    net_backward(r, seq, scale_gk, scale_raw)
    pack_shares(r)

    def make_b(d):
        return pltpu.make_async_remote_copy(
            src_ref=r.share.at[lax.rem(first_id + d, 8)], dst_ref=r.first.at[d],
            send_sem=sem_b.at[d], recv_sem=recv_b.at[d], device_id=first_peer(d), device_id_type=MESH,
        )

    def make_c(d):
        return pltpu.make_async_remote_copy(
            src_ref=r.second.at[second_id], dst_ref=r.second.at[second_id],
            send_sem=sem_c.at[d], recv_sem=recv_c.at[d], device_id=second_peer(d), device_id_type=MESH,
        )

    def make_d(d):
        return pltpu.make_async_remote_copy(
            src_ref=r.third.at[first_id], dst_ref=r.third.at[first_id],
            send_sem=sem_d.at[d], recv_sem=recv_d.at[d], device_id=first_peer(d), device_id_type=MESH,
        )

    wait = run(8, make_b)
    finish(r, 1)
    leave(1)
    wait()
    same = r.share[first_id]
    for d in range(2, 8, 2):
        same = same + r.first[d]
    both = same
    for d in range(1, 8, 2):
        both = both + r.first[d]
    factor = 1.0 / math.sqrt(16 * L)
    r.second[second_id] = jnp.where(iota((8, 256), 1) < 176, both, same) * factor
    run(16, make_c)()
    total = r.second[0]
    for c in range(1, 16):
        total = total + r.second[c]
    r.third[first_id] = total
    for c in range(8):
        r.own[c, core] = r.second[2 * c, :, 128:256] + r.second[2 * c + 1, :, 128:256]
    wait = run(8, make_d)
    part = r.own.at[:, core]
    swap = pltpu.make_async_remote_copy(
        src_ref=part, dst_ref=part, send_sem=sem_d.at[0], recv_sem=recv_d.at[0],
        device_id=(2 * yz + 1 - core, seq), device_id_type=MESH,
    )
    swap.start()
    r.g_skip[...] = to_row(r.own[yz, core][:, 113:114])
    wait()
    swap.wait()
    lax.fori_loop(0, CH // 2, sent, 0)
    for i in range(4):
        relay(i).wait_send()
    for copy in results:
        copy.wait()


def write_kernel(
    i_val, i_gin, i_gout, i_second, i_third, skip,
    o_val, o_gin, o_gout, o_skip, o_in, o_bin, o_mid, o_bmid, o_out, o_rate,
    stage, second, third, g_skip, g_in, g_bin, g_mid, g_bmid, g_out, g_rate, in_sem, out_sem, small_sem,
):
    loads, stores = [], []
    for i, (src, dst) in enumerate(((i_val, o_val), (i_gin, o_gin), (i_gout, o_gout))):
        for n in range(2):
            loads.append(pltpu.make_async_copy(src.at[n], stage.at[i, n], in_sem.at[2 * i + n]))
            stores.append(pltpu.make_async_copy(stage.at[i, n], dst.at[n], out_sem.at[2 * i + n]))
    small = [
        pltpu.make_async_copy(i_second, second, small_sem.at[0]),
        pltpu.make_async_copy(i_third, third, small_sem.at[1]),
        pltpu.make_async_copy(skip, g_skip, small_sem.at[2]),
    ]
    for copy in small + loads:
        copy.start()
    for load, store in zip(loads, stores):
        load.wait()
        store.start()
    for copy in small:
        copy.wait()
    hidden = third[...].reshape(64, 256)
    g_mid[0] = hidden[:, 0:64]
    g_mid[1] = pltpu.roll(hidden[:, 0:128], 64, 1)[:, 0:64]
    flat = jnp.transpose(hidden[:, 128:256])
    g_in[...] = flat[0:33, :]
    g_bin[...] = flat[33:34, :]
    g_bmid[...] = flat[34:36, :]
    own = jnp.transpose(second[...].reshape(128, 128))
    g_out[...] = own[48:112, :]
    g_rate[...] = own[112:113, :]
    pairs = (
        (g_skip, o_skip), (g_in, o_in), (g_bin, o_bin), (g_mid, o_mid), (g_bmid, o_bmid), (g_out, o_out),
        (g_rate, o_rate),
    )
    for i, (src, dst) in enumerate(pairs):
        copy = pltpu.make_async_copy(src, dst, small_sem.at[3 + i])
        copy.start()
        stores.append(copy)
    for copy in stores:
        copy.wait()


def sds(shape, dtype=F32):
    return jax.ShapeDtypeStruct(shape, dtype)


VM = pl.BlockSpec(memory_space=pltpu.VMEM)
HB = pl.BlockSpec(memory_space=pltpu.HBM)
DMA = pltpu.SemaphoreType.DMA


def to_natural(x):
    return x.reshape(2, CH, A, B).transpose(0, 2, 1, 3)


def from_natural(x):
    return x.transpose(0, 2, 1, 3).reshape(2, CH, L)


def local(
    value, gate_in, gate_out, cotangent, skip_gain,
    weight_in, bias_in, weight_mid, bias_mid, weight_out, decay_rate,
):
    small = (
        row_constants(), weight_in.T, bias_in.reshape(1, 64), weight_mid, bias_mid, weight_out.T,
        decay_rate.reshape(1, 128), skip_gain.reshape(1, CH),
    )
    large = tuple(to_natural(x) for x in (value, gate_in, cotangent, gate_out))
    big = sds(BIG, LOW)
    o_val, o_gin, o_gout, own, third, g_skip = pl.pallas_call(
        main_kernel,
        out_shape=[big, big, big, sds((8, 2, 8, 128)), sds((NSEQ, 8, 256)), sds((1, CH))],
        in_specs=[HB] * N_LOCAL,
        out_specs=[HB] * 3 + [VM] * 3,
        scratch_shapes=[pltpu.VMEM(shape, dtype) for shape, dtype in SCRATCH.values()]
        + [
            DMA((N_LOCAL,)), DMA((6,)), DMA((5, 4)), DMA((5, 4)), DMA((4,)), DMA((4,)),
            DMA((4, 4)), DMA((4, 4)), DMA((4, 5)), DMA((4, 5)), DMA((NSEQ,)), DMA((NSEQ,)),
            DMA((NSEQ,)), DMA((NSEQ,)), DMA((NCHAN,)), DMA((NCHAN,)), DMA((NSEQ,)), DMA((NSEQ,)),
        ],
        compiler_params=pltpu.CompilerParams(
            collective_id=0, has_side_effects=True, vmem_limit_bytes=VMEM_MAIN
        ),
        name="hyena_backward",
    )(*small, *transform_tables(), *large)
    o_val, o_gin, o_gout, g_skip, g_in, g_bin, g_mid, g_bmid, g_out, g_rate = pl.pallas_call(
        write_kernel,
        out_shape=[
            big, big, big, sds((1, CH)), sds((33, 64)), sds((1, 64)), sds((2, 64, 64)), sds((2, 64)),
            sds((64, 128)), sds((1, 128)),
        ],
        in_specs=[HB] * 6,
        out_specs=[HB] * 10,
        scratch_shapes=[
            pltpu.VMEM((3,) + BIG, LOW), pltpu.VMEM((8, 2, 8, 128), F32), pltpu.VMEM((NSEQ, 8, 256), F32),
            pltpu.VMEM((1, CH), F32), pltpu.VMEM((33, 64), F32), pltpu.VMEM((1, 64), F32),
            pltpu.VMEM((2, 64, 64), F32), pltpu.VMEM((2, 64), F32), pltpu.VMEM((64, 128), F32),
            pltpu.VMEM((1, 128), F32),
            DMA((6,)), DMA((6,)), DMA((10,)),
        ],
        compiler_params=pltpu.CompilerParams(vmem_limit_bytes=VMEM_MAIN),
        name="write_results",
    )(o_val, o_gin, o_gout, own, third, g_skip)
    return (
        from_natural(o_val), from_natural(o_gin), from_natural(o_gout), g_skip.reshape(CH),
        g_in.T, g_bin.reshape(64), g_mid, g_bmid, g_out.T, g_rate.reshape(128),
    )


def solution(mesh):
    return jax.shard_map(
        local,
        mesh=mesh,
        in_specs=(
            P("seq", "chan", None), P("seq", "chan", None), P("seq", "chan", None), P("seq", "chan", None),
            P("chan"), P(), P(), P(), P(), P(), P(),
        ),
        out_specs=(
            P("seq", "chan", None), P("seq", "chan", None), P("seq", "chan", None),
            P("chan"), P(), P(), P(), P(), P(), P(),
        ),
        check_vma=False,
    )
```

```python
import functools
import math

import jax
import jax.numpy as jnp
import numpy as np
from jax import lax
from jax.experimental import pallas as pl
from jax.experimental.pallas import tpu as pltpu
from jax.sharding import PartitionSpec as P

EPSILON = 1e-06
HIGHEST = lax.Precision.HIGHEST
L = 32768
A = 256
B = 128
CH = 8
NSEQ = 8
NCHAN = 16
ABLK = A // NSEQ
TB = L // NSEQ
CHUNK = 1024
LOW = jnp.bfloat16
F32 = jnp.float32
MESH = pl.DeviceIdType.MESH


def band_table(length, bands):
    highest = length / 4.0
    return np.array(
        [math.floor(highest ** (number / (bands - 1)) + 0.5) for number in range(bands)], np.int64
    )


def row_constants():
    freq = np.zeros((48, 128), np.int32)
    off = np.zeros((48, 128), np.int32)
    bands = band_table(L, 16)
    freq[1:17] = bands[:, None]
    off[1:17] = L // 4
    freq[17:33] = bands[:, None]
    return np.stack([freq, off])


def transform_tables():
    k = np.arange(A)[:, None]
    rows = 2.0 * np.pi * (((4 * k + 1) * np.arange(A)[None, :]) % 1024) / 1024.0
    w1 = np.concatenate([np.cos(rows), -np.sin(rows)], axis=0)
    turn = 2.0 * np.pi * (((4 * k + 1) * np.arange(B)[None, :]) % (4 * L)) / (4.0 * L)
    q = np.arange(B)
    cols = 2.0 * np.pi * ((q[:, None] * q[None, :]) % B) / B
    c, s = np.cos(cols), np.sin(cols)
    fwd = np.block([[c, -s], [s, c]])
    inv = np.block([[c, s], [-s, c]])
    low = np.dtype(LOW)
    return (
        w1.astype(low),
        w1.T.astype(low),
        fwd.astype(low),
        inv.astype(low),
        np.stack([np.cos(turn), np.sin(turn)]).astype(np.float32),
    )


def poly_fit():
    x = (np.cos(np.pi * (np.arange(64) + 0.5) / 64) + 1) / 2 * (np.pi / 2 * 1.002) ** 2
    r = np.sqrt(x)
    sin_c = np.polynomial.polynomial.polyfit(x, np.sin(r) / r, 4)
    cos_c = np.polynomial.polynomial.polyfit(x, np.cos(r), 5)
    return [float(v) for v in sin_c], [float(v) for v in cos_c]


SIN_C, COS_C = poly_fit()


def horner(x, coefs):
    acc = jnp.full_like(x, coefs[-1])
    for value in coefs[-2::-1]:
        acc = acc * x + value
    return acc


def sin_small(r):
    return r * horner(r * r, SIN_C)


def sin_cos(z):
    n = jnp.floor(z * (1.0 / math.pi) + 0.5)
    r = z - n * 3.140625
    r = r - n * 9.67653589793e-4
    half = n * 0.5
    sign = 1.0 - 4.0 * (half - jnp.floor(half))
    r2 = r * r
    return sign * (r * horner(r2, SIN_C)), sign * horner(r2, COS_C)


def dot_full(x, y):
    return jnp.dot(x, y, precision=HIGHEST, preferred_element_type=F32)


def dot_nt(x, y, precision=None):
    return lax.dot_general(x, y, (((1,), (1,)), ((), ())), precision=precision, preferred_element_type=F32)


def dot_tn(x, y, precision=None):
    return lax.dot_general(x, y, (((0,), (0,)), ((), ())), precision=precision, preferred_element_type=F32)


def low_dot(x, y):
    return jnp.dot(x, y, preferred_element_type=F32)


def split(x):
    hi = x.astype(LOW)
    return hi, (x - hi.astype(F32)).astype(LOW)


def iota(shape, dim):
    return lax.broadcasted_iota(jnp.int32, shape, dim)


def to_column(row, size, shift):
    n = row.shape[1]
    pick = iota((size, n), 0) + shift == iota((size, n), 1)
    return jnp.sum(jnp.where(pick, jnp.broadcast_to(row, (size, n)), 0.0), axis=1, keepdims=True)


def to_row(col):
    n = col.shape[0]
    pick = iota((n, n), 0) == iota((n, n), 1)
    return jnp.sum(jnp.where(pick, jnp.broadcast_to(col, (n, n)), 0.0), axis=0, keepdims=True)


def repeat_matrix(rows, period, times):
    shape = (rows, period * times)
    j = iota(shape, 1)
    hit = j == iota(shape, 0)
    for m in range(1, times):
        hit = hit | (j == iota(shape, 0) + m * period)
    return jnp.where(hit, 1.0, 0.0)


def hi_hi_lo(w, period):
    hi = w.astype(LOW).astype(F32)
    lane = iota(w.shape, 1)
    out = jnp.where(lane < 2 * period, hi, jnp.where(lane < 3 * period, w - hi, 0.0))
    return out.astype(LOW)


class Refs:
    def __init__(self, **refs):
        self.__dict__.update(refs)


def prepare_weights(r, chan, other):
    first = jnp.where(iota((8, 64), 0) == 1, jnp.broadcast_to(r.b_in[...], (8, 64)), 0.0)
    r.w_pad[0:32, :] = r.w_in[0:32, :]
    r.w_pad[32:40, :] = jnp.where(iota((8, 64), 0) == 0, jnp.broadcast_to(r.w_in[32:33, :], (8, 64)), first)
    r.w_pad[40:48, :] = jnp.zeros((8, 64), F32)
    r.k_in[...] = hi_hi_lo(dot_tn(r.w_pad[...], repeat_matrix(48, 48, 3), HIGHEST), 48)
    rep = repeat_matrix(64, 64, 3)
    for i in range(2):
        w = r.w_mid[i]
        r.k_mid[i] = hi_hi_lo(dot_full(w, rep), 64)
        r.k_back[i] = hi_hi_lo(dot_tn(w, rep, HIGHEST), 64)
    row = iota((2 * CH, 128), 0)
    channel = jnp.where(row < CH, row + chan * CH, row - CH + other * CH)
    pick = jnp.where(iota((2 * CH, 128), 1) == channel, 1.0, 0.0)
    w_own = dot_nt(pick, r.w_out[...], HIGHEST)
    r.k_out[...] = hi_hi_lo(dot_full(w_own, rep), 64)
    r.k_outback[...] = hi_hi_lo(dot_tn(w_own, repeat_matrix(2 * CH, 2 * CH, 3), HIGHEST), 2 * CH)
    rates = jnp.sum(jnp.where(pick > 0.5, jnp.broadcast_to(r.rate[...], (2 * CH, 128)), 0.0), axis=1, keepdims=True)
    r.rate_col[...] = jnp.broadcast_to(rates, (2 * CH, 128))
    r.bias_col[0] = jnp.broadcast_to(to_column(r.b_mid[0:1, :], 64, 0), (64, 128))
    r.bias_col[1] = jnp.broadcast_to(to_column(r.b_mid[1:2, :], 64, 0), (64, 128))


def wide(block, times):
    return jnp.concatenate([block] * times, axis=1)


def fraction(base):
    pos = base + iota((2 * CH, CHUNK), 1)
    return pos.astype(F32) * (1.0 / L)


def net_forward(r, seq, core, send):
    per = CHUNK // 128

    def step(j, carry):
        base = pl.multiple_of(j * CHUNK, CHUNK)
        lanes = pl.ds(base, CHUNK)
        pos = seq * TB + (2 * core + j) * CHUNK + iota((48, CHUNK), 1)
        row = iota((48, CHUNK), 0)
        phase = ((wide(r.bands[0], per) * pos + (wide(r.bands[1], per) + L // 2)) & (L - 1)) - L // 2
        phase = jnp.where(phase > L // 4, L // 2 - phase, phase)
        phase = jnp.where(phase < -(L // 4), -(L // 2) - phase, phase)
        wave = sin_small(phase.astype(F32) * (2.0 * math.pi / L))
        frac = pos.astype(F32) * (1.0 / L)
        hi, lo = split(jnp.where(row == 0, frac, jnp.where(row == 33, 1.0, wave)))
        r.feat[0:48, lanes] = hi
        r.feat[48:64, lanes] = jnp.zeros((16, CHUNK), LOW)
        r.feat[64:112, lanes] = lo
        r.feat[112:128, lanes] = jnp.zeros((16, CHUNK), LOW)
        z = low_dot(r.k_in[...], jnp.concatenate([hi, lo, hi], axis=0))
        for layer in range(3):
            s, c = sin_cos(z)
            r.der[layer, :, lanes] = c
            hi, lo = split(s)
            r.act[layer, 0:64, lanes] = hi
            r.act[layer, 64:128, lanes] = lo
            x = jnp.concatenate([hi, lo, hi], axis=0)
            if layer < 2:
                z = low_dot(r.k_mid[layer], x) + wide(r.bias_col[layer], per)
        raw = low_dot(r.k_out[...], x) * jnp.exp(-wide(r.rate_col[...], per) * frac[0 : 2 * CH, :])
        for i in range(per):
            r.raw_all[seq * ABLK + (2 * core + j) * per + i] = raw[0:CH, 128 * i : 128 * i + 128]
            r.raw_other[j * per + i] = raw[CH:, 128 * i : 128 * i + 128]
        send(j)
        return carry

    lax.fori_loop(0, TB // CHUNK // 2, step, 0)


def net_backward(r, seq, core):
    per = CHUNK // 128
    r.acc[...] = jnp.zeros_like(r.acc)
    r.acc_out[...] = jnp.zeros_like(r.acc_out)
    r.acc_bias[...] = jnp.zeros_like(r.acc_bias)
    r.acc_rate[...] = jnp.zeros_like(r.acc_rate)

    def lane_sum(x):
        total = x[:, 0:128]
        for i in range(1, per):
            total = total + x[:, 128 * i : 128 * i + 128]
        return total

    def step(j, carry):
        lanes = pl.ds(pl.multiple_of(j * CHUNK, CHUNK), CHUNK)
        start = (2 * core + j) * per

        def rows(mine, first, others, second):
            return jnp.concatenate(
                [jnp.concatenate([mine[first + i], others[second + i]], axis=0) for i in range(per)], axis=1
            )

        grad = rows(r.grad_own, start, r.grad_other, j * per)
        raw = rows(r.raw_all, seq * ABLK + start, r.raw_other, j * per)
        frac = fraction(seq * TB + (2 * core + j) * CHUNK)
        r.acc_rate[...] -= lane_sum(grad * raw * frac)
        shaped = grad * jnp.exp(-wide(r.rate_col[...], per) * frac)
        hi = shaped.astype(LOW).astype(F32)
        lo = shaped - hi
        pair = jnp.concatenate([hi, lo], axis=0).astype(LOW)
        r.acc_out[...] += dot_nt(pair, r.act[2, :, lanes])
        d = low_dot(r.k_outback[...], jnp.concatenate([hi, lo, hi], axis=0).astype(LOW))
        for layer in (2, 1, 0):
            d = d * r.der[layer, :, lanes]
            hi, lo = split(d)
            pair = jnp.concatenate([hi, lo], axis=0)
            if layer:
                r.acc_bias[layer - 1] += lane_sum(d)
                r.acc[layer] += dot_nt(pair, r.act[layer - 1, :, lanes])
                d = low_dot(r.k_back[layer - 1], jnp.concatenate([hi, lo, hi], axis=0))
            else:
                r.acc[0] += dot_nt(pair, r.feat[:, lanes])
        return carry

    lax.fori_loop(0, TB // CHUNK // 2, step, 0)


def fold_halves(x):
    n = x.shape[0] // 2
    total = x[0:n] + x[n:]
    return total + pltpu.roll(total, 64, 1)


def pack_shares(r, core):
    lane = iota((64, 128), 1)
    r.block[0] = jnp.where(lane < 64, fold_halves(r.acc[1]), fold_halves(r.acc[2]))
    block = fold_halves(r.acc[0])
    block = jnp.where(lane == 34, jnp.sum(r.acc_bias[0], axis=1, keepdims=True), block)
    r.block[1] = jnp.where(lane == 35, jnp.sum(r.acc_bias[1], axis=1, keepdims=True), block)
    lane = iota((2 * CH, 128), 1)
    own = pltpu.roll(fold_halves(r.acc_out[...]), 48, 1)
    own = jnp.where(lane == 112, jnp.sum(r.acc_rate[...], axis=1, keepdims=True), own)
    own = jnp.where(lane > 112, 0.0, own)
    lane = iota((CH, 128), 1)
    theirs = own[CH:]
    own = jnp.where(lane == 113, r.skip_part[...], own[0:CH])

    def place(s, carry):
        rows = pl.ds(pl.multiple_of(8 * s, 8), 8)
        r.share[s, :, 0:128] = r.block[0, rows, :]
        apart = jnp.where(lax.rem(s, 2) == core, own, theirs)
        r.share[s, :, 128:256] = jnp.where(lane < 48, r.block[1, rows, :], apart)
        return carry

    lax.fori_loop(0, NSEQ, place, 0)


def to_low(x):
    return x.astype(LOW)


def channel_rows(c):
    return pl.ds(c, A, stride=CH)


def forward_pair(r, x):
    tc, ts = r.turn[0], r.turn[1]
    g = low_dot(r.w1[...], x)
    parts = []
    for n in range(2):
        re, im = g[0:A, n * B : n * B + B], g[A:, n * B : n * B + B]
        parts.append(jnp.concatenate([to_low(re * tc + im * ts), to_low(im * tc - re * ts)], axis=1))
    f = low_dot(jnp.concatenate(parts, axis=0), r.fwd[...])
    return f[0:A], f[A:]


def inverse_pair(r, specs):
    tc, ts = r.turn[0], r.turn[1]
    s = jnp.concatenate([jnp.concatenate([to_low(re), to_low(im)], axis=1) for re, im in specs], axis=0)
    t = low_dot(s, r.inv[...])
    cols = []
    for n in range(2):
        re, im = t[n * A : n * A + A, 0:B], t[n * A : n * A + A, B:]
        cols.append(jnp.concatenate([to_low(re * tc - im * ts), to_low(re * ts + im * tc)], axis=0))
    y = low_dot(r.w1t[...], jnp.concatenate(cols, axis=1))
    return y[:, 0:B], y[:, B:]


BLK = 16
VMEM_MAIN = 56 << 20


def gate_products(r, n):
    def step(j, acc):
        part = pl.ds(j * BLK, BLK)
        rows = pl.ds(pl.multiple_of(j * (BLK * CH), BLK * CH), BLK * CH)
        m = r.val[n, part].astype(F32) * r.gin[n, part].astype(F32)
        g = r.cot[n, part].astype(F32) * r.gout[n, part].astype(F32)
        r.mixed[n, rows, :] = m.reshape(BLK * CH, B)
        r.inner[n, rows, :] = g.reshape(BLK * CH, B)
        return acc + jnp.sum(m * g, axis=0)

    return lax.fori_loop(0, A // BLK, step, jnp.zeros((CH, B), F32))


def spectra(r, p):
    cross = []
    for i in range(2):
        c = 2 * p + i
        rows = channel_rows(c)
        fm = forward_pair(r, jnp.concatenate([to_low(r.mixed[n, rows, :]) for n in range(2)], axis=1))
        fg = forward_pair(r, jnp.concatenate([to_low(r.inner[n, rows, :]) for n in range(2)], axis=1))
        re = im = None
        for n in range(2):
            r.f_mixed[c, n] = fm[n]
            r.f_inner[c, n] = fg[n]
            mr, mi = fm[n][:, 0:B], fm[n][:, B:]
            gr, gi = fg[n][:, 0:B], fg[n][:, B:]
            pr, pi = mr * gr + mi * gi, mr * gi - mi * gr
            re, im = (pr, pi) if re is None else (re + pr, im + pi)
        cross.append((re, im))
    ys = inverse_pair(r, cross)
    for i in range(2):
        r.gk[2 * p + i] = ys[i]


def channel_stats(r, c):
    x = r.raw_flat[channel_rows(c), :]
    r.stat[0, pl.ds(c, 1), :] = jnp.sum(x * x, axis=0, keepdims=True)
    r.stat[1, pl.ds(c, 1), :] = jnp.sum(x * r.gk[c], axis=0, keepdims=True)


def filter_products(r, p):
    kernels = []
    for i in range(2):
        c = 2 * p + i
        square = jnp.sum(r.stat[0, pl.ds(c, 1), :], axis=1, keepdims=True)
        kernels.append(to_low(r.raw_flat[channel_rows(c), :] * (1.0 / jnp.sqrt(square + EPSILON))))
    fk = forward_pair(r, jnp.concatenate(kernels, axis=1))
    for i in range(2):
        c = 2 * p + i
        rows = channel_rows(c)
        kr, ki = fk[i][:, 0:B] * (1.0 / L), fk[i][:, B:] * (1.0 / L)
        specs = []
        for n in range(2):
            mr, mi = r.f_mixed[c, n, :, 0:B], r.f_mixed[c, n, :, B:]
            specs.append((mr * kr - mi * ki, mr * ki + mi * kr))
        ys = inverse_pair(r, specs)
        for n in range(2):
            r.conv[n, rows, :] = ys[n]
        specs = []
        for n in range(2):
            gr, gi = r.f_inner[c, n, :, 0:B], r.f_inner[c, n, :, B:]
            specs.append((gr * kr + gi * ki, gi * kr - gr * ki))
        ys = inverse_pair(r, specs)
        for n in range(2):
            r.back[n, rows, :] = ys[n]


def finish(r, n):
    gain = jnp.broadcast_to(to_column(r.skip[...], CH, 0), (CH, B))[None]

    def step(j, carry):
        part = pl.ds(j * BLK, BLK)
        rows = pl.ds(pl.multiple_of(j * (BLK * CH), BLK * CH), BLK * CH)
        shape = (BLK, CH, B)
        full = r.conv[n, rows, :].reshape(shape) + gain * r.mixed[n, rows, :].reshape(shape)
        r.o_gout[n, part] = to_low(r.cot[n, part].astype(F32) * full)
        full = r.back[n, rows, :].reshape(shape) + gain * r.inner[n, rows, :].reshape(shape)
        r.o_val[n, part] = to_low(full * r.gin[n, part].astype(F32))
        r.o_gin[n, part] = to_low(full * r.val[n, part].astype(F32))
        return carry

    lax.fori_loop(0, A // BLK, step, 0)


SMALL = ("bands", "w_in", "b_in", "w_mid", "b_mid", "w_out", "rate", "skip")
TABLES = ("w1", "w1t", "fwd", "inv", "turn")
LARGE = ("val", "gin", "cot", "gout")
OUTS = ("h_val", "h_gin", "h_gout", "own", "third", "g_skip")
BIG = (2, A, CH, B)
FULL = (2, A * CH, B)
SCRATCH = {
    "bands": ((2, 48, 128), jnp.int32),
    "w_in": ((33, 64), F32),
    "b_in": ((1, 64), F32),
    "w_mid": ((2, 64, 64), F32),
    "b_mid": ((2, 64), F32),
    "w_out": ((64, 128), F32),
    "rate": ((1, 128), F32),
    "skip": ((1, CH), F32),
    "w1": ((2 * A, A), LOW),
    "w1t": ((A, 2 * A), LOW),
    "fwd": ((2 * B, 2 * B), LOW),
    "inv": ((2 * B, 2 * B), LOW),
    "turn": ((2, A, B), F32),
    "val": (BIG, LOW),
    "gin": (BIG, LOW),
    "cot": (BIG, LOW),
    "gout": (BIG, LOW),
    "o_val": (BIG, LOW),
    "o_gin": (BIG, LOW),
    "o_gout": (BIG, LOW),
    "w_pad": ((48, 64), F32),
    "k_in": ((64, 144), LOW),
    "k_mid": ((2, 64, 192), LOW),
    "k_back": ((2, 64, 192), LOW),
    "k_out": ((2 * CH, 192), LOW),
    "k_outback": ((64, 6 * CH), LOW),
    "rate_col": ((2 * CH, 128), F32),
    "bias_col": ((2, 64, 128), F32),
    "feat": ((128, TB // 2), LOW),
    "act": ((3, 128, TB // 2), LOW),
    "der": ((3, 64, TB // 2), F32),
    "raw_all": ((A, CH, B), F32),
    "raw_other": ((ABLK // 2, CH, B), F32),
    "grad_own": ((ABLK, CH, B), F32),
    "grad_other": ((ABLK // 2, CH, B), F32),
    "total": ((CH * ABLK, B), F32),
    "half": ((CH // 2, 2, 2, 2, ABLK // 2, B), F32),
    "side_out": ((CH // 2, 2, 2, 2, ABLK, B), F32),
    "side": ((CH // 2, 5, 2, ABLK, B), F32),
    "stat": ((2, CH, B), F32),
    "along": ((NSEQ, CH, B), F32),
    "mixed": (FULL, F32),
    "inner": (FULL, F32),
    "f_mixed": ((CH, 2, A, 2 * B), F32),
    "f_inner": ((CH, 2, A, 2 * B), F32),
    "gk": ((CH, A, B), F32),
    "conv": (FULL, F32),
    "back": (FULL, F32),
    "acc": ((3, 128, 128), F32),
    "acc_out": ((4 * CH, 128), F32),
    "acc_bias": ((2, 64, 128), F32),
    "acc_rate": ((2 * CH, 128), F32),
    "skip_part": ((CH, 1), F32),
    "block": ((2, 64, 128), F32),
    "share": ((NSEQ, 8, 256), F32),
    "first": ((NSEQ, 8, 256), F32),
    "second": ((16, 8, 256), F32),
}
N_LOCAL = len(SMALL) + len(TABLES) + len(LARGE)


def main_kernel(*refs):
    ins = refs[:N_LOCAL]
    outs = refs[N_LOCAL : N_LOCAL + len(OUTS)]
    names = list(SCRATCH)
    scratch = refs[N_LOCAL + len(OUTS) :]
    r = Refs(**dict(zip(OUTS, outs)), **dict(zip(names, scratch)))
    (load_sem, out_sem, ag_send, ag_recv, cross_send, relay_send, relay_recv, half_send, half_recv, rs_send, rs_recv,
     sem_a, recv_a, sem_b, recv_b, sem_c, recv_c, sem_d, recv_d) = scratch[len(names) :]
    r.raw_flat = r.raw_all.reshape(A * CH, B)
    chan, seq = lax.axis_index("chan"), lax.axis_index("seq")
    barrier = pltpu.get_barrier_semaphore()

    def signal(device):
        pl.semaphore_signal(barrier, inc=1, device_id=device, device_id_type=MESH)

    x, z = lax.div(seq, 2), lax.rem(seq, 2)
    yz, core = lax.div(chan, 2), lax.rem(chan, 2)
    first_id, second_id = 2 * x + core, 2 * yz + z

    xr, xl, xo = lax.rem(x + 1, 4), lax.rem(x + 3, 4), lax.rem(x + 2, 4)
    other = 1 - z
    near_seq = (2 * x + other, 2 * xr + z, 2 * xr + other, 2 * xl + z, 2 * xl + other)
    near = tuple((chan, to) for to in near_seq)
    across = tuple((2 * yz + 1 - core, to) for to in near_seq + (seq,))
    to_r, to_l = near[1], near[3]

    def seq_peer(d):
        return (chan, lax.rem(seq + d, NSEQ))

    def first_peer(d):
        to = lax.rem(first_id + d, 8)
        return (2 * yz + lax.rem(to, 2), 2 * lax.div(to, 2) + z)

    def second_peer(d):
        to = lax.rem(second_id + d, 16)
        return (2 * lax.div(to, 2) + core, 2 * x + lax.rem(to, 2))

    def hail(d, carry):
        signal(seq_peer(d))
        signal(first_peer(d))
        return carry

    def hail_second(d, carry):
        signal(second_peer(d))
        return carry

    loads = {}
    for i, name in enumerate(SMALL + TABLES + LARGE):
        loads[name] = pltpu.make_async_copy(ins[i], getattr(r, name), load_sem.at[i])
    for name in SMALL:
        loads[name].start()
    lax.fori_loop(1, 8, hail, 0)
    lax.fori_loop(1, 16, hail_second, 0)
    for i in range(5):
        signal(across[i])
    for name in LARGE + TABLES:
        loads[name].start()
    for name in SMALL:
        loads[name].wait()

    half = ABLK // 2
    piece = CHUNK // 128
    n_piece = ABLK // piece

    def row_of(xx, zz):
        return (2 * xx + zz) * ABLK

    def gather(i, j):
        part = r.raw_all.at[pl.ds(row_of(x, z) + j * piece, piece)]
        return pltpu.make_async_remote_copy(
            src_ref=part, dst_ref=part, send_sem=ag_send.at[i, j], recv_sem=ag_recv.at[i, j],
            device_id=near[i], device_id_type=MESH,
        )

    def cross(i, j):
        return pltpu.make_async_remote_copy(
            src_ref=r.raw_other.at[pl.ds(j * piece, piece)],
            dst_ref=r.raw_all.at[pl.ds(row_of(x, z) + (2 * core + j) * piece, piece)],
            send_sem=cross_send.at[i, j], recv_sem=ag_recv.at[i, 2 * core + j],
            device_id=across[i], device_id_type=MESH,
        )

    def send_chunk(j):
        for i in range(5):
            gather(i, 2 * core + j).start()
        for i in range(6):
            cross(i, j).start()

    def relay(i):
        row = row_of(xl if i < 2 else xr, (z, other)[i % 2]) + (0 if i < 2 else half)
        part = r.raw_all.at[pl.ds(row, half)]
        return pltpu.make_async_remote_copy(
            src_ref=part, dst_ref=part, send_sem=relay_send.at[i], recv_sem=relay_recv.at[i],
            device_id=to_r if i < 2 else to_l, device_id_type=MESH,
        )

    def own_half(j):
        part = r.raw_all.at[pl.ds(row_of(x, z) + (2 * (1 - core) + j) * piece, piece)]
        return pltpu.make_async_remote_copy(
            src_ref=part, dst_ref=part, send_sem=cross_send.at[5, j], recv_sem=ag_recv.at[5, 2 * (1 - core) + j],
            device_id=across[5], device_id_type=MESH,
        )

    def arrived(i, start, stop):
        def step(j, carry):
            gather(i, j).wait_recv()
            return carry

        lax.fori_loop(start, stop, step, 0)

    zs = (other, z)

    def rows_at(p, row, count):
        return r.gk.at[pl.ds(2 * p, 2), pl.ds(pl.multiple_of(row, half), count)]

    def far_half(p, w, h):
        return pltpu.make_async_remote_copy(
            src_ref=rows_at(p, row_of(xo, zs[w]) + h * half, half), dst_ref=r.half.at[p, w, h],
            send_sem=half_send.at[p, 2 * w + h], recv_sem=half_recv.at[p, 2 * w + h],
            device_id=(to_r, to_l)[h], device_id_type=MESH,
        )

    def near_block(p, i):
        w = i % 2
        src = rows_at(p, row_of(x, other), ABLK) if i == 0 else r.side_out.at[p, w, (i - 1) // 2]
        return pltpu.make_async_remote_copy(
            src_ref=src, dst_ref=r.side.at[p, i], send_sem=rs_send.at[p, i], recv_sem=rs_recv.at[p, i],
            device_id=near[i], device_id_type=MESH,
        )

    def scatter_far(p):
        for w in range(2):
            for h in range(2):
                far_half(p, w, h).start()
        near_block(p, 0).start()

    def scatter_near(p):
        for w in range(2):
            for h in range(2):
                far_half(p, w, h).wait_recv()
                row = row_of((xr, xl)[h], zs[w])
                for i in range(2):
                    mine = r.gk[2 * p + i, pl.ds(pl.multiple_of(row, half), half), :]
                    rest = r.gk[2 * p + i, pl.ds(pl.multiple_of(row + half, half), half), :]
                    extra = r.half[p, w, h, i]
                    r.side_out[p, w, h, i, 0:half, :] = mine + extra if h == 0 else mine
                    r.side_out[p, w, h, i, half:, :] = rest if h == 0 else rest + extra
        for i in range(1, 5):
            near_block(p, i).start()

    prepare_weights(r, chan, 2 * yz + 1 - core)
    pl.semaphore_wait(barrier, 7 + 7 + 15 + 5)
    net_forward(r, seq, core, send_chunk)

    for name in LARGE:
        loads[name].wait()
    acc = gate_products(r, 0)
    acc = acc + gate_products(r, 1)
    r.skip_part[...] = jnp.sum(acc, axis=1, keepdims=True)
    for name in TABLES:
        loads[name].wait()
    for i in range(2):
        arrived(1 + i, 0, n_piece // 2)
        relay(i).start()

    spectra(r, 0)
    scatter_far(0)
    for i in range(2):
        arrived(3 + i, n_piece // 2, n_piece)
        relay(2 + i).start()

    spectra(r, 1)
    scatter_far(1)

    def pair_step(p, carry):
        spectra(r, p)
        scatter_far(p)
        scatter_near(p - 2)
        return carry

    lax.fori_loop(2, CH // 2, pair_step, 0)
    arrived(0, 0, n_piece)
    for j in range(2):
        own_half(j).wait_recv()
    for i in range(2):
        arrived(1 + i, n_piece // 2, n_piece)
        arrived(3 + i, 0, n_piece // 2)
    for i in range(4):
        relay(i).wait_recv()

    def stats_step(c, carry):
        channel_stats(r, c)
        return carry

    lax.fori_loop(0, CH, stats_step, 0)

    def run(size, make):
        def start(d, carry):
            make(d).start()
            return carry

        def wait(d, carry):
            make(d).wait()
            return carry

        lax.fori_loop(1, size, start, 0)
        return lambda: lax.fori_loop(1, size, wait, 0)

    def make_a(d):
        return pltpu.make_async_remote_copy(
            src_ref=r.stat.at[1], dst_ref=r.along.at[d],
            send_sem=sem_a.at[d], recv_sem=recv_a.at[d], device_id=seq_peer(d), device_id_type=MESH,
        )

    wait_along = run(NSEQ, make_a)

    def product_step(p, carry):
        filter_products(r, p)
        scatter_near(p + CH // 2 - 2)
        return carry

    lax.fori_loop(0, 2, product_step, 0)

    def last_step(p, carry):
        filter_products(r, p)
        return carry

    lax.fori_loop(2, CH // 2, last_step, 0)
    results = []

    def leave(n):
        for i, (src, dst) in enumerate(((r.o_val, r.h_val), (r.o_gin, r.h_gin), (r.o_gout, r.h_gout))):
            copy = pltpu.make_async_copy(src.at[n], dst.at[n], out_sem.at[3 * n + i])
            copy.start()
            results.append(copy)

    finish(r, 0)
    leave(0)

    def settle(p, carry):
        for i in range(5):
            near_block(p, i).wait_recv()
        row = pl.multiple_of(row_of(x, z), ABLK)
        for i in range(2):
            c = 2 * p + i
            total = r.gk[c, pl.ds(row, ABLK), :]
            for k in range(5):
                total = total + r.side[p, k, i]
            r.total[pl.ds(pl.multiple_of(c * ABLK, ABLK), ABLK), :] = total
        return carry

    lax.fori_loop(0, CH // 2, settle, 0)
    wait_along()
    along = r.stat[1]
    for d in range(1, NSEQ):
        along = along + r.along[d]
    along = jnp.sum(along, axis=1, keepdims=True) * (1.0 / L)
    norm = jnp.sqrt(jnp.sum(r.stat[0], axis=1, keepdims=True) + EPSILON)
    scale_gk = jnp.broadcast_to((1.0 / L) / norm, (CH, B))
    scale_raw = jnp.broadcast_to(along / (norm * norm * norm), (CH, B))

    def gradient(half_id):
        def step(i, carry):
            row = half_id * half + i
            total = r.total[pl.ds(row, CH, stride=ABLK), :]
            r.grad_own[row] = total * scale_gk - r.raw_all[row_of(x, z) + row] * scale_raw
            return carry

        lax.fori_loop(0, half, step, 0, unroll=4)

    gradient(1 - core)
    hand = pltpu.make_async_remote_copy(
        src_ref=r.grad_own.at[pl.ds((1 - core) * half, half)], dst_ref=r.grad_other,
        send_sem=sem_a.at[0], recv_sem=recv_a.at[0], device_id=across[5], device_id_type=MESH,
    )
    hand.start()
    gradient(core)
    hand.wait()

    def sent(j, carry):
        for i in range(5):
            near_block(j, i).wait_send()
        for i in range(4):
            far_half(j, i // 2, i % 2).wait_send()
        return carry

    def sent_raw(j, carry):
        for i in range(5):
            gather(i, 2 * core + j).wait_send()
        for i in range(6):
            cross(i, j).wait_send()
        return carry

    net_backward(r, seq, core)
    pack_shares(r, core)

    def make_b(d):
        return pltpu.make_async_remote_copy(
            src_ref=r.share.at[lax.rem(first_id + d, 8)], dst_ref=r.first.at[d],
            send_sem=sem_b.at[d], recv_sem=recv_b.at[d], device_id=first_peer(d), device_id_type=MESH,
        )

    def make_c(d):
        return pltpu.make_async_remote_copy(
            src_ref=r.second.at[second_id], dst_ref=r.second.at[second_id],
            send_sem=sem_c.at[d], recv_sem=recv_c.at[d], device_id=second_peer(d), device_id_type=MESH,
        )

    def make_d(d):
        return pltpu.make_async_remote_copy(
            src_ref=r.third.at[first_id], dst_ref=r.third.at[first_id],
            send_sem=sem_d.at[d], recv_sem=recv_d.at[d], device_id=first_peer(d), device_id_type=MESH,
        )

    wait = run(8, make_b)
    finish(r, 1)
    leave(1)
    wait()
    both = r.share[first_id]
    for d in range(1, 8):
        both = both + r.first[d]
    factor = 1.0 / math.sqrt(16 * L)
    r.second[second_id] = both * factor
    run(16, make_c)()
    total = r.second[0]
    for c in range(1, 16):
        total = total + r.second[c]
    r.third[first_id] = total
    for c in range(8):
        r.own[c, core] = r.second[2 * c, :, 128:256] + r.second[2 * c + 1, :, 128:256]
    wait = run(8, make_d)
    part = r.own.at[:, core]
    swap = pltpu.make_async_remote_copy(
        src_ref=part, dst_ref=part, send_sem=sem_d.at[0], recv_sem=recv_d.at[0],
        device_id=(2 * yz + 1 - core, seq), device_id_type=MESH,
    )
    swap.start()
    r.g_skip[...] = to_row(r.own[yz, core][:, 113:114])
    wait()
    swap.wait()
    lax.fori_loop(0, CH // 2, sent, 0)
    lax.fori_loop(0, 2, sent_raw, 0)
    for i in range(4):
        relay(i).wait_send()
    for copy in results:
        copy.wait()


def write_kernel(
    i_val, i_gin, i_gout, i_second, i_third, skip,
    o_val, o_gin, o_gout, o_skip, o_in, o_bin, o_mid, o_bmid, o_out, o_rate,
    stage, second, third, g_skip, g_in, g_bin, g_mid, g_bmid, g_out, g_rate, in_sem, out_sem, small_sem,
):
    loads, stores = [], []
    for i, (src, dst) in enumerate(((i_val, o_val), (i_gin, o_gin), (i_gout, o_gout))):
        for q in range(4):
            part = (q // 2, pl.ds(q % 2 * (A // 2), A // 2))
            loads.append(pltpu.make_async_copy(src.at[part], stage.at[(i,) + part], in_sem.at[4 * i + q]))
            stores.append(pltpu.make_async_copy(stage.at[(i,) + part], dst.at[part], out_sem.at[4 * i + q]))
    small = [
        pltpu.make_async_copy(i_second, second, small_sem.at[0]),
        pltpu.make_async_copy(i_third, third, small_sem.at[1]),
        pltpu.make_async_copy(skip, g_skip, small_sem.at[2]),
    ]
    for copy in small + loads:
        copy.start()
    for load, store in zip(loads, stores):
        load.wait()
        store.start()
    for copy in small:
        copy.wait()
    hidden = third[...].reshape(64, 256)
    g_mid[0] = hidden[:, 0:64]
    g_mid[1] = pltpu.roll(hidden[:, 0:128], 64, 1)[:, 0:64]
    flat = jnp.transpose(hidden[:, 128:256])
    g_in[...] = flat[0:33, :]
    g_bin[...] = flat[33:34, :]
    g_bmid[...] = flat[34:36, :]
    own = jnp.transpose(second[...].reshape(128, 128))
    g_out[...] = own[48:112, :]
    g_rate[...] = own[112:113, :]
    pairs = (
        (g_skip, o_skip), (g_in, o_in), (g_bin, o_bin), (g_mid, o_mid), (g_bmid, o_bmid), (g_out, o_out),
        (g_rate, o_rate),
    )
    for i, (src, dst) in enumerate(pairs):
        copy = pltpu.make_async_copy(src, dst, small_sem.at[3 + i])
        copy.start()
        stores.append(copy)
    for copy in stores:
        copy.wait()


def sds(shape, dtype=F32):
    return jax.ShapeDtypeStruct(shape, dtype)


VM = pl.BlockSpec(memory_space=pltpu.VMEM)
HB = pl.BlockSpec(memory_space=pltpu.HBM)
DMA = pltpu.SemaphoreType.DMA


def to_natural(x):
    return x.reshape(2, CH, A, B).transpose(0, 2, 1, 3)


def from_natural(x):
    return x.transpose(0, 2, 1, 3).reshape(2, CH, L)


def local(
    value, gate_in, gate_out, cotangent, skip_gain,
    weight_in, bias_in, weight_mid, bias_mid, weight_out, decay_rate,
):
    small = (
        row_constants(), weight_in.T, bias_in.reshape(1, 64), weight_mid, bias_mid, weight_out.T,
        decay_rate.reshape(1, 128), skip_gain.reshape(1, CH),
    )
    large = tuple(to_natural(x) for x in (value, gate_in, cotangent, gate_out))
    big = sds(BIG, LOW)
    o_val, o_gin, o_gout, own, third, g_skip = pl.pallas_call(
        main_kernel,
        out_shape=[big, big, big, sds((8, 2, 8, 128)), sds((NSEQ, 8, 256)), sds((1, CH))],
        in_specs=[HB] * N_LOCAL,
        out_specs=[HB] * 3 + [VM] * 3,
        scratch_shapes=[pltpu.VMEM(shape, dtype) for shape, dtype in SCRATCH.values()]
        + [
            DMA((N_LOCAL,)), DMA((6,)), DMA((5, 4)), DMA((6, 4)), DMA((6, 2)), DMA((4,)), DMA((4,)),
            DMA((4, 4)), DMA((4, 4)), DMA((4, 5)), DMA((4, 5)), DMA((NSEQ,)), DMA((NSEQ,)),
            DMA((NSEQ,)), DMA((NSEQ,)), DMA((NCHAN,)), DMA((NCHAN,)), DMA((NSEQ,)), DMA((NSEQ,)),
        ],
        compiler_params=pltpu.CompilerParams(
            collective_id=0, has_side_effects=True, vmem_limit_bytes=VMEM_MAIN
        ),
        name="hyena_backward",
    )(*small, *transform_tables(), *large)
    o_val, o_gin, o_gout, g_skip, g_in, g_bin, g_mid, g_bmid, g_out, g_rate = pl.pallas_call(
        write_kernel,
        out_shape=[
            big, big, big, sds((1, CH)), sds((33, 64)), sds((1, 64)), sds((2, 64, 64)), sds((2, 64)),
            sds((64, 128)), sds((1, 128)),
        ],
        in_specs=[HB] * 6,
        out_specs=[HB] * 10,
        scratch_shapes=[
            pltpu.VMEM((3,) + BIG, LOW), pltpu.VMEM((8, 2, 8, 128), F32), pltpu.VMEM((NSEQ, 8, 256), F32),
            pltpu.VMEM((1, CH), F32), pltpu.VMEM((33, 64), F32), pltpu.VMEM((1, 64), F32),
            pltpu.VMEM((2, 64, 64), F32), pltpu.VMEM((2, 64), F32), pltpu.VMEM((64, 128), F32),
            pltpu.VMEM((1, 128), F32),
            DMA((12,)), DMA((12,)), DMA((10,)),
        ],
        compiler_params=pltpu.CompilerParams(vmem_limit_bytes=VMEM_MAIN),
        name="write_results",
    )(o_val, o_gin, o_gout, own, third, g_skip)
    return (
        from_natural(o_val), from_natural(o_gin), from_natural(o_gout), g_skip.reshape(CH),
        g_in.T, g_bin.reshape(64), g_mid, g_bmid, g_out.T, g_rate.reshape(128),
    )


def solution(mesh):
    return jax.shard_map(
        local,
        mesh=mesh,
        in_specs=(
            P("seq", "chan", None), P("seq", "chan", None), P("seq", "chan", None), P("seq", "chan", None),
            P("chan"), P(), P(), P(), P(), P(), P(),
        ),
        out_specs=(
            P("seq", "chan", None), P("seq", "chan", None), P("seq", "chan", None),
            P("chan"), P(), P(), P(), P(), P(), P(),
        ),
        check_vma=False,
    )
```

```python
import functools
import math

import jax
import jax.numpy as jnp
import numpy as np
from jax import lax
from jax.experimental import pallas as pl
from jax.experimental.pallas import tpu as pltpu
from jax.sharding import PartitionSpec as P

EPSILON = 1e-06
HIGHEST = lax.Precision.HIGHEST
L = 32768
A = 256
B = 128
CH = 8
NSEQ = 8
NCHAN = 16
ABLK = A // NSEQ
TB = L // NSEQ
CHUNK = 1024
LOW = jnp.bfloat16
F32 = jnp.float32
MESH = pl.DeviceIdType.MESH


def band_table(length, bands):
    highest = length / 4.0
    return np.array(
        [math.floor(highest ** (number / (bands - 1)) + 0.5) for number in range(bands)], np.int64
    )


def row_constants():
    freq = np.zeros((48, 128), np.int32)
    off = np.zeros((48, 128), np.int32)
    bands = band_table(L, 16)
    freq[1:17] = bands[:, None]
    off[1:17] = L // 4
    freq[17:33] = bands[:, None]
    return np.stack([freq, off])


def transform_tables():
    k = np.arange(A)[:, None]
    rows = 2.0 * np.pi * (((4 * k + 1) * np.arange(A)[None, :]) % 1024) / 1024.0
    w1 = np.concatenate([np.cos(rows), -np.sin(rows)], axis=0)
    turn = 2.0 * np.pi * (((4 * k + 1) * np.arange(B)[None, :]) % (4 * L)) / (4.0 * L)
    q = np.arange(B)
    cols = 2.0 * np.pi * ((q[:, None] * q[None, :]) % B) / B
    c, s = np.cos(cols), np.sin(cols)
    fwd = np.block([[c, -s], [s, c]])
    inv = np.block([[c, s], [-s, c]])
    low = np.dtype(LOW)
    return (
        w1.astype(low),
        w1.T.astype(low),
        fwd.astype(low),
        inv.astype(low),
        np.stack([np.cos(turn), np.sin(turn)]).astype(np.float32),
    )


def poly_fit():
    x = (np.cos(np.pi * (np.arange(64) + 0.5) / 64) + 1) / 2 * (np.pi / 2 * 1.002) ** 2
    r = np.sqrt(x)
    sin_c = np.polynomial.polynomial.polyfit(x, np.sin(r) / r, 4)
    cos_c = np.polynomial.polynomial.polyfit(x, np.cos(r), 5)
    return [float(v) for v in sin_c], [float(v) for v in cos_c]


SIN_C, COS_C = poly_fit()


def horner(x, coefs):
    acc = jnp.full_like(x, coefs[-1])
    for value in coefs[-2::-1]:
        acc = acc * x + value
    return acc


def sin_small(r):
    return r * horner(r * r, SIN_C)


def sin_cos(z):
    n = jnp.floor(z * (1.0 / math.pi) + 0.5)
    r = z - n * 3.140625
    r = r - n * 9.67653589793e-4
    half = n * 0.5
    sign = 1.0 - 4.0 * (half - jnp.floor(half))
    r2 = r * r
    return sign * (r * horner(r2, SIN_C)), sign * horner(r2, COS_C)


def dot_full(x, y):
    return jnp.dot(x, y, precision=HIGHEST, preferred_element_type=F32)


def dot_nt(x, y, precision=None):
    return lax.dot_general(x, y, (((1,), (1,)), ((), ())), precision=precision, preferred_element_type=F32)


def dot_tn(x, y, precision=None):
    return lax.dot_general(x, y, (((0,), (0,)), ((), ())), precision=precision, preferred_element_type=F32)


def low_dot(x, y):
    return jnp.dot(x, y, preferred_element_type=F32)


def split(x):
    hi = x.astype(LOW)
    return hi, (x - hi.astype(F32)).astype(LOW)


def iota(shape, dim):
    return lax.broadcasted_iota(jnp.int32, shape, dim)


def to_column(row, size, shift):
    n = row.shape[1]
    pick = iota((size, n), 0) + shift == iota((size, n), 1)
    return jnp.sum(jnp.where(pick, jnp.broadcast_to(row, (size, n)), 0.0), axis=1, keepdims=True)


def to_row(col):
    n = col.shape[0]
    pick = iota((n, n), 0) == iota((n, n), 1)
    return jnp.sum(jnp.where(pick, jnp.broadcast_to(col, (n, n)), 0.0), axis=0, keepdims=True)


def repeat_matrix(rows, period, times):
    shape = (rows, period * times)
    j = iota(shape, 1)
    hit = j == iota(shape, 0)
    for m in range(1, times):
        hit = hit | (j == iota(shape, 0) + m * period)
    return jnp.where(hit, 1.0, 0.0)


def hi_hi_lo(w, period):
    hi = w.astype(LOW).astype(F32)
    lane = iota(w.shape, 1)
    out = jnp.where(lane < 2 * period, hi, jnp.where(lane < 3 * period, w - hi, 0.0))
    return out.astype(LOW)


class Refs:
    def __init__(self, **refs):
        self.__dict__.update(refs)


def prepare_weights(r, chan, other):
    first = jnp.where(iota((8, 64), 0) == 1, jnp.broadcast_to(r.b_in[...], (8, 64)), 0.0)
    r.w_pad[0:32, :] = r.w_in[0:32, :]
    r.w_pad[32:40, :] = jnp.where(iota((8, 64), 0) == 0, jnp.broadcast_to(r.w_in[32:33, :], (8, 64)), first)
    r.w_pad[40:48, :] = jnp.zeros((8, 64), F32)
    r.k_in[...] = hi_hi_lo(dot_tn(r.w_pad[...], repeat_matrix(48, 48, 3), HIGHEST), 48)
    rep = repeat_matrix(64, 64, 3)
    for i in range(2):
        w = r.w_mid[i]
        r.k_mid[i] = hi_hi_lo(dot_full(w, rep), 64)
        r.k_back[i] = hi_hi_lo(dot_tn(w, rep, HIGHEST), 64)
    row = iota((2 * CH, 128), 0)
    channel = jnp.where(row < CH, row + chan * CH, row - CH + other * CH)
    pick = jnp.where(iota((2 * CH, 128), 1) == channel, 1.0, 0.0)
    w_own = dot_nt(pick, r.w_out[...], HIGHEST)
    r.k_out[...] = hi_hi_lo(dot_full(w_own, rep), 64)
    r.k_outback[...] = hi_hi_lo(dot_tn(w_own, repeat_matrix(2 * CH, 2 * CH, 3), HIGHEST), 2 * CH)
    rates = jnp.sum(jnp.where(pick > 0.5, jnp.broadcast_to(r.rate[...], (2 * CH, 128)), 0.0), axis=1, keepdims=True)
    r.rate_col[...] = jnp.broadcast_to(rates, (2 * CH, 128))
    r.bias_col[0] = jnp.broadcast_to(to_column(r.b_mid[0:1, :], 64, 0), (64, 128))
    r.bias_col[1] = jnp.broadcast_to(to_column(r.b_mid[1:2, :], 64, 0), (64, 128))


def wide(block, times):
    return jnp.concatenate([block] * times, axis=1)


def fraction(base):
    pos = base + iota((2 * CH, CHUNK), 1)
    return pos.astype(F32) * (1.0 / L)


def net_forward(r, seq, core, send):
    per = CHUNK // 128

    def step(j, carry):
        base = pl.multiple_of(j * CHUNK, CHUNK)
        lanes = pl.ds(base, CHUNK)
        pos = seq * TB + (2 * core + j) * CHUNK + iota((48, CHUNK), 1)
        row = iota((48, CHUNK), 0)
        phase = ((wide(r.bands[0], per) * pos + (wide(r.bands[1], per) + L // 2)) & (L - 1)) - L // 2
        phase = jnp.where(phase > L // 4, L // 2 - phase, phase)
        phase = jnp.where(phase < -(L // 4), -(L // 2) - phase, phase)
        wave = sin_small(phase.astype(F32) * (2.0 * math.pi / L))
        frac = pos.astype(F32) * (1.0 / L)
        hi, lo = split(jnp.where(row == 0, frac, jnp.where(row == 33, 1.0, wave)))
        r.feat[0:48, lanes] = hi
        r.feat[48:64, lanes] = jnp.zeros((16, CHUNK), LOW)
        r.feat[64:112, lanes] = lo
        r.feat[112:128, lanes] = jnp.zeros((16, CHUNK), LOW)
        z = low_dot(r.k_in[...], jnp.concatenate([hi, lo, hi], axis=0))
        for layer in range(3):
            s, c = sin_cos(z)
            r.der[layer, :, lanes] = c
            hi, lo = split(s)
            r.act[layer, 0:64, lanes] = hi
            r.act[layer, 64:128, lanes] = lo
            x = jnp.concatenate([hi, lo, hi], axis=0)
            if layer < 2:
                z = low_dot(r.k_mid[layer], x) + wide(r.bias_col[layer], per)
        raw = low_dot(r.k_out[...], x) * jnp.exp(-wide(r.rate_col[...], per) * frac[0 : 2 * CH, :])
        for i in range(per):
            r.raw_all[seq * ABLK + (2 * core + j) * per + i] = raw[0:CH, 128 * i : 128 * i + 128]
            r.raw_other[j * per + i] = raw[CH:, 128 * i : 128 * i + 128]
        send(j)
        return carry

    lax.fori_loop(0, TB // CHUNK // 2, step, 0)


def net_backward(r, seq, core):
    per = CHUNK // 128
    r.acc[...] = jnp.zeros_like(r.acc)
    r.acc_out[...] = jnp.zeros_like(r.acc_out)
    r.acc_bias[...] = jnp.zeros_like(r.acc_bias)
    r.acc_rate[...] = jnp.zeros_like(r.acc_rate)

    def lane_sum(x):
        total = x[:, 0:128]
        for i in range(1, per):
            total = total + x[:, 128 * i : 128 * i + 128]
        return total

    def step(j, carry):
        lanes = pl.ds(pl.multiple_of(j * CHUNK, CHUNK), CHUNK)
        start = (2 * core + j) * per

        def rows(mine, first, others, second):
            return jnp.concatenate(
                [jnp.concatenate([mine[first + i], others[second + i]], axis=0) for i in range(per)], axis=1
            )

        grad = rows(r.grad_own, start, r.grad_other, j * per)
        raw = rows(r.raw_all, seq * ABLK + start, r.raw_other, j * per)
        frac = fraction(seq * TB + (2 * core + j) * CHUNK)
        r.acc_rate[...] -= lane_sum(grad * raw * frac)
        shaped = grad * jnp.exp(-wide(r.rate_col[...], per) * frac)
        hi = shaped.astype(LOW).astype(F32)
        lo = shaped - hi
        pair = jnp.concatenate([hi, lo], axis=0).astype(LOW)
        r.acc_out[...] += dot_nt(pair, r.act[2, :, lanes])
        d = low_dot(r.k_outback[...], jnp.concatenate([hi, lo, hi], axis=0).astype(LOW))
        for layer in (2, 1, 0):
            d = d * r.der[layer, :, lanes]
            hi, lo = split(d)
            pair = jnp.concatenate([hi, lo], axis=0)
            if layer:
                r.acc_bias[layer - 1] += lane_sum(d)
                r.acc[layer] += dot_nt(pair, r.act[layer - 1, :, lanes])
                d = low_dot(r.k_back[layer - 1], jnp.concatenate([hi, lo, hi], axis=0))
            else:
                r.acc[0] += dot_nt(pair, r.feat[:, lanes])
        return carry

    lax.fori_loop(0, TB // CHUNK // 2, step, 0)


def fold_halves(x):
    n = x.shape[0] // 2
    total = x[0:n] + x[n:]
    return total + pltpu.roll(total, 64, 1)


def pack_shares(r, core):
    lane = iota((64, 128), 1)
    r.block[0] = jnp.where(lane < 64, fold_halves(r.acc[1]), fold_halves(r.acc[2]))
    block = fold_halves(r.acc[0])
    block = jnp.where(lane == 34, jnp.sum(r.acc_bias[0], axis=1, keepdims=True), block)
    r.block[1] = jnp.where(lane == 35, jnp.sum(r.acc_bias[1], axis=1, keepdims=True), block)
    lane = iota((2 * CH, 128), 1)
    own = pltpu.roll(fold_halves(r.acc_out[...]), 48, 1)
    own = jnp.where(lane == 112, jnp.sum(r.acc_rate[...], axis=1, keepdims=True), own)
    own = jnp.where(lane > 112, 0.0, own)
    lane = iota((CH, 128), 1)
    theirs = own[CH:]
    own = jnp.where(lane == 113, r.skip_part[...], own[0:CH])

    def place(s, carry):
        rows = pl.ds(pl.multiple_of(8 * s, 8), 8)
        r.share[s, :, 0:128] = r.block[0, rows, :]
        apart = jnp.where(lax.rem(s, 2) == core, own, theirs)
        r.share[s, :, 128:256] = jnp.where(lane < 48, r.block[1, rows, :], apart)
        return carry

    lax.fori_loop(0, NSEQ, place, 0)


def to_low(x):
    return x.astype(LOW)


def channel_rows(c):
    return pl.ds(c, A, stride=CH)


def forward_pair(r, x):
    tc, ts = r.turn[0], r.turn[1]
    g = low_dot(r.w1[...], x)
    parts = []
    for n in range(2):
        re, im = g[0:A, n * B : n * B + B], g[A:, n * B : n * B + B]
        parts.append(jnp.concatenate([to_low(re * tc + im * ts), to_low(im * tc - re * ts)], axis=1))
    f = low_dot(jnp.concatenate(parts, axis=0), r.fwd[...])
    return f[0:A], f[A:]


def inverse_pair(r, specs):
    tc, ts = r.turn[0], r.turn[1]
    s = jnp.concatenate([jnp.concatenate([to_low(re), to_low(im)], axis=1) for re, im in specs], axis=0)
    t = low_dot(s, r.inv[...])
    cols = []
    for n in range(2):
        re, im = t[n * A : n * A + A, 0:B], t[n * A : n * A + A, B:]
        cols.append(jnp.concatenate([to_low(re * tc - im * ts), to_low(re * ts + im * tc)], axis=0))
    y = low_dot(r.w1t[...], jnp.concatenate(cols, axis=1))
    return y[:, 0:B], y[:, B:]


BLK = 16
VMEM_MAIN = 56 << 20


def gate_products(r, n):
    def step(j, acc):
        part = pl.ds(j * BLK, BLK)
        rows = pl.ds(pl.multiple_of(j * (BLK * CH), BLK * CH), BLK * CH)
        m = r.val[n, part].astype(F32) * r.gin[n, part].astype(F32)
        g = r.cot[n, part].astype(F32) * r.gout[n, part].astype(F32)
        r.mixed[n, rows, :] = m.reshape(BLK * CH, B)
        r.inner[n, rows, :] = g.reshape(BLK * CH, B)
        return acc + jnp.sum(m * g, axis=0)

    return lax.fori_loop(0, A // BLK, step, jnp.zeros((CH, B), F32))


def spectra(r, p):
    cross = []
    for i in range(2):
        c = 2 * p + i
        rows = channel_rows(c)
        fm = forward_pair(r, jnp.concatenate([to_low(r.mixed[n, rows, :]) for n in range(2)], axis=1))
        fg = forward_pair(r, jnp.concatenate([to_low(r.inner[n, rows, :]) for n in range(2)], axis=1))
        re = im = None
        for n in range(2):
            r.f_mixed[c, n] = fm[n]
            r.f_inner[c, n] = fg[n]
            mr, mi = fm[n][:, 0:B], fm[n][:, B:]
            gr, gi = fg[n][:, 0:B], fg[n][:, B:]
            pr, pi = mr * gr + mi * gi, mr * gi - mi * gr
            re, im = (pr, pi) if re is None else (re + pr, im + pi)
        cross.append((re, im))
    ys = inverse_pair(r, cross)
    for i in range(2):
        r.gk[2 * p + i] = ys[i]


def channel_stats(r, c):
    x = r.raw_flat[channel_rows(c), :]
    r.stat[0, pl.ds(c, 1), :] = jnp.sum(x * x, axis=0, keepdims=True)
    r.stat[1, pl.ds(c, 1), :] = jnp.sum(x * r.gk[c], axis=0, keepdims=True)


def filter_products(r, p):
    kernels = []
    for i in range(2):
        c = 2 * p + i
        square = jnp.sum(r.stat[0, pl.ds(c, 1), :], axis=1, keepdims=True)
        kernels.append(to_low(r.raw_flat[channel_rows(c), :] * (1.0 / jnp.sqrt(square + EPSILON))))
    fk = forward_pair(r, jnp.concatenate(kernels, axis=1))
    for i in range(2):
        c = 2 * p + i
        rows = channel_rows(c)
        kr, ki = fk[i][:, 0:B] * (1.0 / L), fk[i][:, B:] * (1.0 / L)
        specs = []
        for n in range(2):
            mr, mi = r.f_mixed[c, n, :, 0:B], r.f_mixed[c, n, :, B:]
            specs.append((mr * kr - mi * ki, mr * ki + mi * kr))
        ys = inverse_pair(r, specs)
        for n in range(2):
            r.conv[n, rows, :] = ys[n]
        specs = []
        for n in range(2):
            gr, gi = r.f_inner[c, n, :, 0:B], r.f_inner[c, n, :, B:]
            specs.append((gr * kr + gi * ki, gi * kr - gr * ki))
        ys = inverse_pair(r, specs)
        for n in range(2):
            r.back[n, rows, :] = ys[n]


def finish(r, n):
    gain = jnp.broadcast_to(to_column(r.skip[...], CH, 0), (CH, B))[None]

    def step(j, carry):
        part = pl.ds(j * BLK, BLK)
        rows = pl.ds(pl.multiple_of(j * (BLK * CH), BLK * CH), BLK * CH)
        shape = (BLK, CH, B)
        full = r.conv[n, rows, :].reshape(shape) + gain * r.mixed[n, rows, :].reshape(shape)
        r.o_gout[n, part] = to_low(r.cot[n, part].astype(F32) * full)
        full = r.back[n, rows, :].reshape(shape) + gain * r.inner[n, rows, :].reshape(shape)
        r.o_val[n, part] = to_low(full * r.gin[n, part].astype(F32))
        r.o_gin[n, part] = to_low(full * r.val[n, part].astype(F32))
        return carry

    lax.fori_loop(0, A // BLK, step, 0)


SMALL = ("bands", "w_in", "b_in", "w_mid", "b_mid", "w_out", "rate", "skip")
TABLES = ("w1", "w1t", "fwd", "inv", "turn")
LARGE = ("val", "gin", "cot", "gout")
OUTS = ("h_val", "h_gin", "h_gout", "own", "third", "g_skip")
BIG = (2, A, CH, B)
FULL = (2, A * CH, B)
SCRATCH = {
    "bands": ((2, 48, 128), jnp.int32),
    "w_in": ((33, 64), F32),
    "b_in": ((1, 64), F32),
    "w_mid": ((2, 64, 64), F32),
    "b_mid": ((2, 64), F32),
    "w_out": ((64, 128), F32),
    "rate": ((1, 128), F32),
    "skip": ((1, CH), F32),
    "w1": ((2 * A, A), LOW),
    "w1t": ((A, 2 * A), LOW),
    "fwd": ((2 * B, 2 * B), LOW),
    "inv": ((2 * B, 2 * B), LOW),
    "turn": ((2, A, B), F32),
    "val": (BIG, LOW),
    "gin": (BIG, LOW),
    "cot": (BIG, LOW),
    "gout": (BIG, LOW),
    "o_val": (BIG, LOW),
    "o_gin": (BIG, LOW),
    "o_gout": (BIG, LOW),
    "w_pad": ((48, 64), F32),
    "k_in": ((64, 144), LOW),
    "k_mid": ((2, 64, 192), LOW),
    "k_back": ((2, 64, 192), LOW),
    "k_out": ((2 * CH, 192), LOW),
    "k_outback": ((64, 6 * CH), LOW),
    "rate_col": ((2 * CH, 128), F32),
    "bias_col": ((2, 64, 128), F32),
    "feat": ((128, TB // 2), LOW),
    "act": ((3, 128, TB // 2), LOW),
    "der": ((3, 64, TB // 2), F32),
    "raw_all": ((A, CH, B), F32),
    "raw_other": ((ABLK // 2, CH, B), F32),
    "grad_own": ((ABLK, CH, B), F32),
    "grad_other": ((ABLK // 2, CH, B), F32),
    "total": ((CH * ABLK, B), F32),
    "half": ((CH // 2, 2, 2, 2, ABLK // 2, B), F32),
    "side_out": ((CH // 2, 2, 2, 2, ABLK, B), F32),
    "side": ((CH // 2, 5, 2, ABLK, B), F32),
    "stat": ((2, CH, B), F32),
    "along": ((NSEQ, CH, B), F32),
    "mixed": (FULL, F32),
    "inner": (FULL, F32),
    "f_mixed": ((CH, 2, A, 2 * B), F32),
    "f_inner": ((CH, 2, A, 2 * B), F32),
    "gk": ((CH, A, B), F32),
    "conv": (FULL, F32),
    "back": (FULL, F32),
    "acc": ((3, 128, 128), F32),
    "acc_out": ((4 * CH, 128), F32),
    "acc_bias": ((2, 64, 128), F32),
    "acc_rate": ((2 * CH, 128), F32),
    "skip_part": ((CH, 1), F32),
    "block": ((2, 64, 128), F32),
    "share": ((NSEQ, 8, 256), F32),
    "first": ((NSEQ, 8, 256), F32),
    "second": ((16, 8, 256), F32),
}
N_LOCAL = len(SMALL) + len(TABLES) + len(LARGE)


def main_kernel(*refs):
    ins = refs[:N_LOCAL]
    outs = refs[N_LOCAL : N_LOCAL + len(OUTS)]
    names = list(SCRATCH)
    scratch = refs[N_LOCAL + len(OUTS) :]
    r = Refs(**dict(zip(OUTS, outs)), **dict(zip(names, scratch)))
    (load_sem, out_sem, ag_send, ag_recv, cross_send, cross_recv, relay_send, relay_recv, half_send, half_recv, rs_send, rs_recv,
     sem_a, recv_a, sem_b, recv_b, sem_c, recv_c, sem_d, recv_d) = scratch[len(names) :]
    r.raw_flat = r.raw_all.reshape(A * CH, B)
    chan, seq = lax.axis_index("chan"), lax.axis_index("seq")
    barrier = pltpu.get_barrier_semaphore()

    def signal(device):
        pl.semaphore_signal(barrier, inc=1, device_id=device, device_id_type=MESH)

    x, z = lax.div(seq, 2), lax.rem(seq, 2)
    yz, core = lax.div(chan, 2), lax.rem(chan, 2)
    first_id, second_id = 2 * x + core, 2 * yz + z

    xr, xl, xo = lax.rem(x + 1, 4), lax.rem(x + 3, 4), lax.rem(x + 2, 4)
    other = 1 - z
    near_seq = (2 * x + other, 2 * xr + z, 2 * xr + other, 2 * xl + z, 2 * xl + other)
    near = tuple((chan, to) for to in near_seq)
    partner = (2 * yz + 1 - core, seq)
    to_r, to_l = near[1], near[3]

    def seq_peer(d):
        return (chan, lax.rem(seq + d, NSEQ))

    def first_peer(d):
        to = lax.rem(first_id + d, 8)
        return (2 * yz + lax.rem(to, 2), 2 * lax.div(to, 2) + z)

    def second_peer(d):
        to = lax.rem(second_id + d, 16)
        return (2 * lax.div(to, 2) + core, 2 * x + lax.rem(to, 2))

    def hail(d, carry):
        signal(seq_peer(d))
        signal(first_peer(d))
        return carry

    def hail_second(d, carry):
        signal(second_peer(d))
        return carry

    loads = {}
    for i, name in enumerate(SMALL + TABLES + LARGE):
        loads[name] = pltpu.make_async_copy(ins[i], getattr(r, name), load_sem.at[i])
    for name in SMALL:
        loads[name].start()
    lax.fori_loop(1, 8, hail, 0)
    lax.fori_loop(1, 16, hail_second, 0)
    for name in LARGE + TABLES:
        loads[name].start()
    for name in SMALL:
        loads[name].wait()

    half = ABLK // 2
    piece = CHUNK // 128
    n_piece = ABLK // piece

    def row_of(xx, zz):
        return (2 * xx + zz) * ABLK

    def gather(i, j, device=None):
        part = r.raw_all.at[pl.ds(row_of(x, z) + j * piece, piece)]
        return pltpu.make_async_remote_copy(
            src_ref=part, dst_ref=part, send_sem=ag_send.at[i, j], recv_sem=ag_recv.at[i, j],
            device_id=device or near[i], device_id_type=MESH,
        )

    def cross(j):
        return pltpu.make_async_remote_copy(
            src_ref=r.raw_other.at[pl.ds(j * piece, piece)],
            dst_ref=r.raw_all.at[pl.ds(row_of(x, z) + (2 * core + j) * piece, piece)],
            send_sem=cross_send.at[j], recv_sem=cross_recv.at[j],
            device_id=partner, device_id_type=MESH,
        )

    def send_chunk(j):
        cross(j).start()
        for i in range(5):
            gather(i, 2 * core + j).start()

    def relay(h, lane):
        row = jnp.where(h == 0, row_of(xl, (z, other)[lane]), row_of(xr, (z, other)[lane]) + half)
        part = r.raw_all.at[pl.ds(row, half)]
        i = 2 * h + lane
        return pltpu.make_async_remote_copy(
            src_ref=part, dst_ref=part, send_sem=relay_send.at[i], recv_sem=relay_recv.at[i],
            device_id=(chan, jnp.where(h == 0, near_seq[1], near_seq[3])), device_id_type=MESH,
        )

    def pass_on(h):
        for lane in range(2):
            arrived(1 + 2 * h + lane, 2 * h, 2 * h + 2)
            relay(h, lane).start()

    def arrived(i, start, stop):
        def step(j, carry):
            gather(i, j, partner).wait_recv()
            return carry

        lax.fori_loop(start, stop, step, 0)

    zs = (other, z)

    def rows_at(p, row, count):
        return r.gk.at[pl.ds(2 * p, 2), pl.ds(pl.multiple_of(row, half), count)]

    def far_half(p, w, h):
        return pltpu.make_async_remote_copy(
            src_ref=rows_at(p, row_of(xo, zs[w]) + h * half, half), dst_ref=r.half.at[p, w, h],
            send_sem=half_send.at[p, 2 * w + h], recv_sem=half_recv.at[p, 2 * w + h],
            device_id=(to_r, to_l)[h], device_id_type=MESH,
        )

    def near_block(p, i):
        w = i % 2
        src = rows_at(p, row_of(x, other), ABLK) if i == 0 else r.side_out.at[p, w, (i - 1) // 2]
        return pltpu.make_async_remote_copy(
            src_ref=src, dst_ref=r.side.at[p, i], send_sem=rs_send.at[p, i], recv_sem=rs_recv.at[p, i],
            device_id=near[i], device_id_type=MESH,
        )

    def scatter_far(p):
        for w in range(2):
            for h in range(2):
                far_half(p, w, h).start()
        near_block(p, 0).start()

    def scatter_near(p):
        for w in range(2):
            for h in range(2):
                far_half(p, w, h).wait_recv()
                row = row_of((xr, xl)[h], zs[w])
                for i in range(2):
                    mine = r.gk[2 * p + i, pl.ds(pl.multiple_of(row, half), half), :]
                    rest = r.gk[2 * p + i, pl.ds(pl.multiple_of(row + half, half), half), :]
                    extra = r.half[p, w, h, i]
                    r.side_out[p, w, h, i, 0:half, :] = mine + extra if h == 0 else mine
                    r.side_out[p, w, h, i, half:, :] = rest if h == 0 else rest + extra
        for i in range(1, 5):
            near_block(p, i).start()

    prepare_weights(r, chan, 2 * yz + 1 - core)
    pl.semaphore_wait(barrier, 7 + 7 + 15)
    net_forward(r, seq, core, send_chunk)

    for j in range(2):
        cross(j).wait_recv()
        for i in range(5):
            gather(i, 2 * (1 - core) + j).start()

    for name in LARGE:
        loads[name].wait()
    acc = gate_products(r, 0)
    acc = acc + gate_products(r, 1)
    r.skip_part[...] = jnp.sum(acc, axis=1, keepdims=True)
    for name in TABLES:
        loads[name].wait()

    spectra(r, 0)
    scatter_far(0)
    pass_on(core)
    spectra(r, 1)
    scatter_far(1)
    pass_on(1 - core)

    def pair_step(p, carry):
        spectra(r, p)
        scatter_far(p)
        scatter_near(p - 2)
        return carry

    lax.fori_loop(2, CH // 2, pair_step, 0)
    scatter_near(CH // 2 - 2)
    arrived(0, 0, n_piece)
    for lane in range(2):
        arrived(1 + lane, n_piece // 2, n_piece)
        arrived(3 + lane, 0, n_piece // 2)
    for h in range(2):
        for lane in range(2):
            relay(h, lane).wait_recv()

    def stats_step(c, carry):
        channel_stats(r, c)
        return carry

    lax.fori_loop(0, CH, stats_step, 0)

    def run(size, make):
        def start(d, carry):
            make(d).start()
            return carry

        def wait(d, carry):
            make(d).wait()
            return carry

        lax.fori_loop(1, size, start, 0)
        return lambda: lax.fori_loop(1, size, wait, 0)

    def make_a(d):
        return pltpu.make_async_remote_copy(
            src_ref=r.stat.at[1], dst_ref=r.along.at[d],
            send_sem=sem_a.at[d], recv_sem=recv_a.at[d], device_id=seq_peer(d), device_id_type=MESH,
        )

    wait_along = run(NSEQ, make_a)

    filter_products(r, 0)
    scatter_near(CH // 2 - 1)

    def product_step(p, carry):
        filter_products(r, p)
        return carry

    lax.fori_loop(1, CH // 2, product_step, 0)
    results = []

    def leave(n):
        for i, (src, dst) in enumerate(((r.o_val, r.h_val), (r.o_gin, r.h_gin), (r.o_gout, r.h_gout))):
            copy = pltpu.make_async_copy(src.at[n], dst.at[n], out_sem.at[3 * n + i])
            copy.start()
            results.append(copy)

    finish(r, 0)
    leave(0)

    def settle(p, carry):
        for i in range(5):
            near_block(p, i).wait_recv()
        row = pl.multiple_of(row_of(x, z), ABLK)
        for i in range(2):
            c = 2 * p + i
            total = r.gk[c, pl.ds(row, ABLK), :]
            for k in range(5):
                total = total + r.side[p, k, i]
            r.total[pl.ds(pl.multiple_of(c * ABLK, ABLK), ABLK), :] = total
        return carry

    lax.fori_loop(0, CH // 2, settle, 0)
    wait_along()
    along = r.stat[1]
    for d in range(1, NSEQ):
        along = along + r.along[d]
    along = jnp.sum(along, axis=1, keepdims=True) * (1.0 / L)
    norm = jnp.sqrt(jnp.sum(r.stat[0], axis=1, keepdims=True) + EPSILON)
    scale_gk = jnp.broadcast_to((1.0 / L) / norm, (CH, B))
    scale_raw = jnp.broadcast_to(along / (norm * norm * norm), (CH, B))

    def gradient(half_id):
        def step(i, carry):
            row = half_id * half + i
            total = r.total[pl.ds(row, CH, stride=ABLK), :]
            r.grad_own[row] = total * scale_gk - r.raw_all[row_of(x, z) + row] * scale_raw
            return carry

        lax.fori_loop(0, half, step, 0, unroll=4)

    gradient(1 - core)
    hand = pltpu.make_async_remote_copy(
        src_ref=r.grad_own.at[pl.ds((1 - core) * half, half)], dst_ref=r.grad_other,
        send_sem=sem_a.at[0], recv_sem=recv_a.at[0], device_id=partner, device_id_type=MESH,
    )
    hand.start()
    gradient(core)
    hand.wait()

    def sent(j, carry):
        for i in range(5):
            near_block(j, i).wait_send()
            gather(i, j).wait_send()
        for i in range(4):
            far_half(j, i // 2, i % 2).wait_send()
        return carry

    net_backward(r, seq, core)
    pack_shares(r, core)

    def make_b(d):
        return pltpu.make_async_remote_copy(
            src_ref=r.share.at[lax.rem(first_id + d, 8)], dst_ref=r.first.at[d],
            send_sem=sem_b.at[d], recv_sem=recv_b.at[d], device_id=first_peer(d), device_id_type=MESH,
        )

    def make_c(d):
        return pltpu.make_async_remote_copy(
            src_ref=r.second.at[second_id], dst_ref=r.second.at[second_id],
            send_sem=sem_c.at[d], recv_sem=recv_c.at[d], device_id=second_peer(d), device_id_type=MESH,
        )

    def make_d(d):
        return pltpu.make_async_remote_copy(
            src_ref=r.third.at[first_id], dst_ref=r.third.at[first_id],
            send_sem=sem_d.at[d], recv_sem=recv_d.at[d], device_id=first_peer(d), device_id_type=MESH,
        )

    wait = run(8, make_b)
    finish(r, 1)
    leave(1)
    wait()
    both = r.share[first_id]
    for d in range(1, 8):
        both = both + r.first[d]
    factor = 1.0 / math.sqrt(16 * L)
    r.second[second_id] = both * factor
    run(16, make_c)()
    total = r.second[0]
    for c in range(1, 16):
        total = total + r.second[c]
    r.third[first_id] = total
    for c in range(8):
        r.own[c, core] = r.second[2 * c, :, 128:256] + r.second[2 * c + 1, :, 128:256]
    wait = run(8, make_d)
    part = r.own.at[:, core]
    swap = pltpu.make_async_remote_copy(
        src_ref=part, dst_ref=part, send_sem=sem_d.at[0], recv_sem=recv_d.at[0],
        device_id=(2 * yz + 1 - core, seq), device_id_type=MESH,
    )
    swap.start()
    r.g_skip[...] = to_row(r.own[yz, core][:, 113:114])
    wait()
    swap.wait()
    lax.fori_loop(0, CH // 2, sent, 0)
    for i in range(2):
        cross(i).wait_send()
        for lane in range(2):
            relay(i, lane).wait_send()
    for copy in results:
        copy.wait()


def write_kernel(
    i_val, i_gin, i_gout, i_second, i_third, skip,
    o_val, o_gin, o_gout, o_skip, o_in, o_bin, o_mid, o_bmid, o_out, o_rate,
    stage, second, third, g_skip, g_in, g_bin, g_mid, g_bmid, g_out, g_rate, in_sem, out_sem, small_sem,
):
    loads, stores = [], []
    for i, (src, dst) in enumerate(((i_val, o_val), (i_gin, o_gin), (i_gout, o_gout))):
        for q in range(4):
            part = (q // 2, pl.ds(q % 2 * (A // 2), A // 2))
            loads.append(pltpu.make_async_copy(src.at[part], stage.at[(i,) + part], in_sem.at[4 * i + q]))
            stores.append(pltpu.make_async_copy(stage.at[(i,) + part], dst.at[part], out_sem.at[4 * i + q]))
    small = [
        pltpu.make_async_copy(i_second, second, small_sem.at[0]),
        pltpu.make_async_copy(i_third, third, small_sem.at[1]),
        pltpu.make_async_copy(skip, g_skip, small_sem.at[2]),
    ]
    for copy in small + loads:
        copy.start()
    for load, store in zip(loads, stores):
        load.wait()
        store.start()
    for copy in small:
        copy.wait()
    hidden = third[...].reshape(64, 256)
    g_mid[0] = hidden[:, 0:64]
    g_mid[1] = pltpu.roll(hidden[:, 0:128], 64, 1)[:, 0:64]
    flat = jnp.transpose(hidden[:, 128:256])
    g_in[...] = flat[0:33, :]
    g_bin[...] = flat[33:34, :]
    g_bmid[...] = flat[34:36, :]
    own = jnp.transpose(second[...].reshape(128, 128))
    g_out[...] = own[48:112, :]
    g_rate[...] = own[112:113, :]
    pairs = (
        (g_skip, o_skip), (g_in, o_in), (g_bin, o_bin), (g_mid, o_mid), (g_bmid, o_bmid), (g_out, o_out),
        (g_rate, o_rate),
    )
    for i, (src, dst) in enumerate(pairs):
        copy = pltpu.make_async_copy(src, dst, small_sem.at[3 + i])
        copy.start()
        stores.append(copy)
    for copy in stores:
        copy.wait()


def sds(shape, dtype=F32):
    return jax.ShapeDtypeStruct(shape, dtype)


VM = pl.BlockSpec(memory_space=pltpu.VMEM)
HB = pl.BlockSpec(memory_space=pltpu.HBM)
DMA = pltpu.SemaphoreType.DMA


def to_natural(x):
    return x.reshape(2, CH, A, B).transpose(0, 2, 1, 3)


def from_natural(x):
    return x.transpose(0, 2, 1, 3).reshape(2, CH, L)


def local(
    value, gate_in, gate_out, cotangent, skip_gain,
    weight_in, bias_in, weight_mid, bias_mid, weight_out, decay_rate,
):
    small = (
        row_constants(), weight_in.T, bias_in.reshape(1, 64), weight_mid, bias_mid, weight_out.T,
        decay_rate.reshape(1, 128), skip_gain.reshape(1, CH),
    )
    large = tuple(to_natural(x) for x in (value, gate_in, cotangent, gate_out))
    big = sds(BIG, LOW)
    o_val, o_gin, o_gout, own, third, g_skip = pl.pallas_call(
        main_kernel,
        out_shape=[big, big, big, sds((8, 2, 8, 128)), sds((NSEQ, 8, 256)), sds((1, CH))],
        in_specs=[HB] * N_LOCAL,
        out_specs=[HB] * 3 + [VM] * 3,
        scratch_shapes=[pltpu.VMEM(shape, dtype) for shape, dtype in SCRATCH.values()]
        + [
            DMA((N_LOCAL,)), DMA((6,)), DMA((5, 4)), DMA((5, 4)), DMA((2,)), DMA((2,)), DMA((4,)), DMA((4,)),
            DMA((4, 4)), DMA((4, 4)), DMA((4, 5)), DMA((4, 5)), DMA((NSEQ,)), DMA((NSEQ,)),
            DMA((NSEQ,)), DMA((NSEQ,)), DMA((NCHAN,)), DMA((NCHAN,)), DMA((NSEQ,)), DMA((NSEQ,)),
        ],
        compiler_params=pltpu.CompilerParams(
            collective_id=0, has_side_effects=True, vmem_limit_bytes=VMEM_MAIN
        ),
        name="hyena_backward",
    )(*small, *transform_tables(), *large)
    o_val, o_gin, o_gout, g_skip, g_in, g_bin, g_mid, g_bmid, g_out, g_rate = pl.pallas_call(
        write_kernel,
        out_shape=[
            big, big, big, sds((1, CH)), sds((33, 64)), sds((1, 64)), sds((2, 64, 64)), sds((2, 64)),
            sds((64, 128)), sds((1, 128)),
        ],
        in_specs=[HB] * 6,
        out_specs=[HB] * 10,
        scratch_shapes=[
            pltpu.VMEM((3,) + BIG, LOW), pltpu.VMEM((8, 2, 8, 128), F32), pltpu.VMEM((NSEQ, 8, 256), F32),
            pltpu.VMEM((1, CH), F32), pltpu.VMEM((33, 64), F32), pltpu.VMEM((1, 64), F32),
            pltpu.VMEM((2, 64, 64), F32), pltpu.VMEM((2, 64), F32), pltpu.VMEM((64, 128), F32),
            pltpu.VMEM((1, 128), F32),
            DMA((12,)), DMA((12,)), DMA((10,)),
        ],
        compiler_params=pltpu.CompilerParams(vmem_limit_bytes=VMEM_MAIN),
        name="write_results",
    )(o_val, o_gin, o_gout, own, third, g_skip)
    return (
        from_natural(o_val), from_natural(o_gin), from_natural(o_gout), g_skip.reshape(CH),
        g_in.T, g_bin.reshape(64), g_mid, g_bmid, g_out.T, g_rate.reshape(128),
    )


def solution(mesh):
    return jax.shard_map(
        local,
        mesh=mesh,
        in_specs=(
            P("seq", "chan", None), P("seq", "chan", None), P("seq", "chan", None), P("seq", "chan", None),
            P("chan"), P(), P(), P(), P(), P(), P(),
        ),
        out_specs=(
            P("seq", "chan", None), P("seq", "chan", None), P("seq", "chan", None),
            P("chan"), P(), P(), P(), P(), P(), P(),
        ),
        check_vma=False,
    )
```

```python
import functools
import math

import jax
import jax.numpy as jnp
import numpy as np
from jax import lax
from jax.experimental import pallas as pl
from jax.experimental.pallas import tpu as pltpu
from jax.sharding import PartitionSpec as P

EPSILON = 1e-06
HIGHEST = lax.Precision.HIGHEST
L = 32768
A = 256
B = 128
CH = 8
NSEQ = 8
NCHAN = 16
ABLK = A // NSEQ
TB = L // NSEQ
CHUNK = 1024
LOW = jnp.bfloat16
F32 = jnp.float32
MESH = pl.DeviceIdType.MESH


def band_table(length, bands):
    highest = length / 4.0
    return np.array(
        [math.floor(highest ** (number / (bands - 1)) + 0.5) for number in range(bands)], np.int64
    )


def row_constants():
    freq = np.zeros((48, 128), np.int32)
    off = np.zeros((48, 128), np.int32)
    bands = band_table(L, 16)
    freq[1:17] = bands[:, None]
    off[1:17] = L // 4
    freq[17:33] = bands[:, None]
    return np.stack([freq, off])


def transform_tables():
    k = np.arange(A)[:, None]
    rows = 2.0 * np.pi * (((4 * k + 1) * np.arange(A)[None, :]) % 1024) / 1024.0
    w1 = np.concatenate([np.cos(rows), -np.sin(rows)], axis=0)
    turn = 2.0 * np.pi * (((4 * k + 1) * np.arange(B)[None, :]) % (4 * L)) / (4.0 * L)
    q = np.arange(B)
    cols = 2.0 * np.pi * ((q[:, None] * q[None, :]) % B) / B
    c, s = np.cos(cols), np.sin(cols)
    fwd = np.block([[c, -s], [s, c]])
    inv = np.block([[c, s], [-s, c]])
    low = np.dtype(LOW)
    return (
        w1.astype(low),
        w1.T.astype(low),
        fwd.astype(low),
        inv.astype(low),
        np.stack([np.cos(turn), np.sin(turn)]).astype(np.float32),
    )


def poly_fit():
    x = (np.cos(np.pi * (np.arange(64) + 0.5) / 64) + 1) / 2 * (np.pi / 2 * 1.002) ** 2
    r = np.sqrt(x)
    sin_c = np.polynomial.polynomial.polyfit(x, np.sin(r) / r, 4)
    cos_c = np.polynomial.polynomial.polyfit(x, np.cos(r), 5)
    return [float(v) for v in sin_c], [float(v) for v in cos_c]


SIN_C, COS_C = poly_fit()


def horner(x, coefs):
    acc = jnp.full_like(x, coefs[-1])
    for value in coefs[-2::-1]:
        acc = acc * x + value
    return acc


def sin_small(r):
    return r * horner(r * r, SIN_C)


def sin_cos(z):
    n = jnp.floor(z * (1.0 / math.pi) + 0.5)
    r = z - n * 3.140625
    r = r - n * 9.67653589793e-4
    half = n * 0.5
    sign = 1.0 - 4.0 * (half - jnp.floor(half))
    r2 = r * r
    return sign * (r * horner(r2, SIN_C)), sign * horner(r2, COS_C)


def dot_full(x, y):
    return jnp.dot(x, y, precision=HIGHEST, preferred_element_type=F32)


def dot_nt(x, y, precision=None):
    return lax.dot_general(x, y, (((1,), (1,)), ((), ())), precision=precision, preferred_element_type=F32)


def dot_tn(x, y, precision=None):
    return lax.dot_general(x, y, (((0,), (0,)), ((), ())), precision=precision, preferred_element_type=F32)


def low_dot(x, y):
    return jnp.dot(x, y, preferred_element_type=F32)


def split(x):
    hi = x.astype(LOW)
    return hi, (x - hi.astype(F32)).astype(LOW)


def iota(shape, dim):
    return lax.broadcasted_iota(jnp.int32, shape, dim)


def to_column(row, size, shift):
    n = row.shape[1]
    pick = iota((size, n), 0) + shift == iota((size, n), 1)
    return jnp.sum(jnp.where(pick, jnp.broadcast_to(row, (size, n)), 0.0), axis=1, keepdims=True)


def to_row(col):
    n = col.shape[0]
    pick = iota((n, n), 0) == iota((n, n), 1)
    return jnp.sum(jnp.where(pick, jnp.broadcast_to(col, (n, n)), 0.0), axis=0, keepdims=True)


def repeat_matrix(rows, period, times):
    shape = (rows, period * times)
    j = iota(shape, 1)
    hit = j == iota(shape, 0)
    for m in range(1, times):
        hit = hit | (j == iota(shape, 0) + m * period)
    return jnp.where(hit, 1.0, 0.0)


def hi_hi_lo(w, period):
    hi = w.astype(LOW).astype(F32)
    lane = iota(w.shape, 1)
    out = jnp.where(lane < 2 * period, hi, jnp.where(lane < 3 * period, w - hi, 0.0))
    return out.astype(LOW)


class Refs:
    def __init__(self, **refs):
        self.__dict__.update(refs)


def prepare_weights(r, chan, other):
    first = jnp.where(iota((8, 64), 0) == 1, jnp.broadcast_to(r.b_in[...], (8, 64)), 0.0)
    r.w_pad[0:32, :] = r.w_in[0:32, :]
    r.w_pad[32:40, :] = jnp.where(iota((8, 64), 0) == 0, jnp.broadcast_to(r.w_in[32:33, :], (8, 64)), first)
    r.w_pad[40:48, :] = jnp.zeros((8, 64), F32)
    r.k_in[...] = hi_hi_lo(dot_tn(r.w_pad[...], repeat_matrix(48, 48, 3), HIGHEST), 48)
    rep = repeat_matrix(64, 64, 3)
    for i in range(2):
        w = r.w_mid[i]
        r.k_mid[i] = hi_hi_lo(dot_full(w, rep), 64)
    row = iota((2 * CH, 128), 0)
    channel = jnp.where(row < CH, row + chan * CH, row - CH + other * CH)
    pick = jnp.where(iota((2 * CH, 128), 1) == channel, 1.0, 0.0)
    w_own = dot_nt(pick, r.w_out[...], HIGHEST)
    r.k_out[...] = hi_hi_lo(dot_full(w_own, rep), 64)
    r.w_own[...] = w_own
    rates = jnp.sum(jnp.where(pick > 0.5, jnp.broadcast_to(r.rate[...], (2 * CH, 128)), 0.0), axis=1, keepdims=True)
    r.rate_col[...] = jnp.broadcast_to(rates, (2 * CH, 128))
    r.bias_col[0] = jnp.broadcast_to(to_column(r.b_mid[0:1, :], 64, 0), (64, 128))
    r.bias_col[1] = jnp.broadcast_to(to_column(r.b_mid[1:2, :], 64, 0), (64, 128))


def prepare_backward(r):
    rep = repeat_matrix(64, 64, 3)
    for i in range(2):
        r.k_back[i] = hi_hi_lo(dot_tn(r.w_mid[i], rep, HIGHEST), 64)
    r.k_outback[...] = hi_hi_lo(dot_tn(r.w_own[...], repeat_matrix(2 * CH, 2 * CH, 3), HIGHEST), 2 * CH)


def wide(block, times):
    return jnp.concatenate([block] * times, axis=1)


def fraction(base):
    pos = base + iota((2 * CH, CHUNK), 1)
    return pos.astype(F32) * (1.0 / L)


def net_chunk(r, seq, core, j):
    per = CHUNK // 128
    lanes = pl.ds(j * CHUNK, CHUNK)
    pos = seq * TB + (2 * core + j) * CHUNK + iota((48, CHUNK), 1)
    row = iota((48, CHUNK), 0)
    phase = ((wide(r.bands[0], per) * pos + (wide(r.bands[1], per) + L // 2)) & (L - 1)) - L // 2
    phase = jnp.where(phase > L // 4, L // 2 - phase, phase)
    phase = jnp.where(phase < -(L // 4), -(L // 2) - phase, phase)
    wave = sin_small(phase.astype(F32) * (2.0 * math.pi / L))
    frac = pos.astype(F32) * (1.0 / L)
    hi, lo = split(jnp.where(row == 0, frac, jnp.where(row == 33, 1.0, wave)))
    r.feat[0:48, lanes] = hi
    r.feat[48:64, lanes] = jnp.zeros((16, CHUNK), LOW)
    r.feat[64:112, lanes] = lo
    r.feat[112:128, lanes] = jnp.zeros((16, CHUNK), LOW)
    z = low_dot(r.k_in[...], jnp.concatenate([hi, lo, hi], axis=0))
    for layer in range(3):
        s, c = sin_cos(z)
        r.der[layer, :, lanes] = c
        hi, lo = split(s)
        r.act[layer, 0:64, lanes] = hi
        r.act[layer, 64:128, lanes] = lo
        x = jnp.concatenate([hi, lo, hi], axis=0)
        if layer < 2:
            z = low_dot(r.k_mid[layer], x) + wide(r.bias_col[layer], per)
    raw = low_dot(r.k_out[...], x) * jnp.exp(-wide(r.rate_col[...], per) * frac[0 : 2 * CH, :])
    for i in range(per):
        r.raw_all[seq * ABLK + (2 * core + j) * per + i] = raw[0:CH, 128 * i : 128 * i + 128]
        r.raw_other[j * per + i] = raw[CH:, 128 * i : 128 * i + 128]


def net_backward(r, seq, core):
    per = CHUNK // 128
    r.acc[...] = jnp.zeros_like(r.acc)
    r.acc_out[...] = jnp.zeros_like(r.acc_out)
    r.acc_bias[...] = jnp.zeros_like(r.acc_bias)
    r.acc_rate[...] = jnp.zeros_like(r.acc_rate)

    def lane_sum(x):
        total = x[:, 0:128]
        for i in range(1, per):
            total = total + x[:, 128 * i : 128 * i + 128]
        return total

    def step(j, carry):
        lanes = pl.ds(pl.multiple_of(j * CHUNK, CHUNK), CHUNK)
        start = (2 * core + j) * per

        def rows(mine, first, others, second):
            return jnp.concatenate(
                [jnp.concatenate([mine[first + i], others[second + i]], axis=0) for i in range(per)], axis=1
            )

        grad = rows(r.grad_own, start, r.grad_other, j * per)
        raw = rows(r.raw_all, seq * ABLK + start, r.raw_other, j * per)
        frac = fraction(seq * TB + (2 * core + j) * CHUNK)
        r.acc_rate[...] -= lane_sum(grad * raw * frac)
        shaped = grad * jnp.exp(-wide(r.rate_col[...], per) * frac)
        hi = shaped.astype(LOW).astype(F32)
        lo = shaped - hi
        pair = jnp.concatenate([hi, lo], axis=0).astype(LOW)
        r.acc_out[...] += dot_nt(pair, r.act[2, :, lanes])
        d = low_dot(r.k_outback[...], jnp.concatenate([hi, lo, hi], axis=0).astype(LOW))
        for layer in (2, 1, 0):
            d = d * r.der[layer, :, lanes]
            hi, lo = split(d)
            pair = jnp.concatenate([hi, lo], axis=0)
            if layer:
                r.acc_bias[layer - 1] += lane_sum(d)
                r.acc[layer] += dot_nt(pair, r.act[layer - 1, :, lanes])
                d = low_dot(r.k_back[layer - 1], jnp.concatenate([hi, lo, hi], axis=0))
            else:
                r.acc[0] += dot_nt(pair, r.feat[:, lanes])
        return carry

    lax.fori_loop(0, TB // CHUNK // 2, step, 0)


def fold_halves(x):
    n = x.shape[0] // 2
    total = x[0:n] + x[n:]
    return total + pltpu.roll(total, 64, 1)


def pack_shares(r, core):
    lane = iota((64, 128), 1)
    r.block[0] = jnp.where(lane < 64, fold_halves(r.acc[1]), fold_halves(r.acc[2]))
    block = fold_halves(r.acc[0])
    block = jnp.where(lane == 34, jnp.sum(r.acc_bias[0], axis=1, keepdims=True), block)
    r.block[1] = jnp.where(lane == 35, jnp.sum(r.acc_bias[1], axis=1, keepdims=True), block)
    lane = iota((2 * CH, 128), 1)
    own = pltpu.roll(fold_halves(r.acc_out[...]), 48, 1)
    own = jnp.where(lane == 112, jnp.sum(r.acc_rate[...], axis=1, keepdims=True), own)
    own = jnp.where(lane > 112, 0.0, own)
    lane = iota((CH, 128), 1)
    theirs = own[CH:]
    own = jnp.where(lane == 113, r.skip_part[...], own[0:CH])

    def place(s, carry):
        rows = pl.ds(pl.multiple_of(8 * s, 8), 8)
        r.share[s, :, 0:128] = r.block[0, rows, :]
        apart = jnp.where(lax.rem(s, 2) == core, own, theirs)
        r.share[s, :, 128:256] = jnp.where(lane < 48, r.block[1, rows, :], apart)
        return carry

    lax.fori_loop(0, NSEQ, place, 0)


def to_low(x):
    return x.astype(LOW)


def channel_rows(c):
    return pl.ds(c, A, stride=CH)


def forward_pair(r, x):
    tc, ts = r.turn[0], r.turn[1]
    g = low_dot(r.w1[...], x)
    parts = []
    for n in range(2):
        re, im = g[0:A, n * B : n * B + B], g[A:, n * B : n * B + B]
        parts.append(jnp.concatenate([to_low(re * tc + im * ts), to_low(im * tc - re * ts)], axis=1))
    f = low_dot(jnp.concatenate(parts, axis=0), r.fwd[...])
    return f[0:A], f[A:]


def inverse_pair(r, specs):
    tc, ts = r.turn[0], r.turn[1]
    s = jnp.concatenate([jnp.concatenate([to_low(re), to_low(im)], axis=1) for re, im in specs], axis=0)
    t = low_dot(s, r.inv[...])
    cols = []
    for n in range(2):
        re, im = t[n * A : n * A + A, 0:B], t[n * A : n * A + A, B:]
        cols.append(jnp.concatenate([to_low(re * tc - im * ts), to_low(re * ts + im * tc)], axis=0))
    y = low_dot(r.w1t[...], jnp.concatenate(cols, axis=1))
    return y[:, 0:B], y[:, B:]


BLK = 16
EARLY = 2
UNDER_FIRST = 1
VMEM_MAIN = 56 << 20


def gate_products(r, n):
    def step(j, acc):
        part = pl.ds(j * BLK, BLK)
        rows = pl.ds(pl.multiple_of(j * (BLK * CH), BLK * CH), BLK * CH)
        m = r.val[n, part].astype(F32) * r.gin[n, part].astype(F32)
        g = r.cot[n, part].astype(F32) * r.gout[n, part].astype(F32)
        r.mixed[n, rows, :] = m.reshape(BLK * CH, B)
        r.inner[n, rows, :] = g.reshape(BLK * CH, B)
        return acc + jnp.sum(m * g, axis=0)

    return lax.fori_loop(0, A // BLK, step, jnp.zeros((CH, B), F32))


def spectra(r, p):
    cross = []
    for i in range(2):
        c = 2 * p + i
        rows = channel_rows(c)
        fm = forward_pair(r, jnp.concatenate([to_low(r.mixed[n, rows, :]) for n in range(2)], axis=1))
        fg = forward_pair(r, jnp.concatenate([to_low(r.inner[n, rows, :]) for n in range(2)], axis=1))
        re = im = None
        for n in range(2):
            r.f_mixed[c, n] = fm[n]
            r.f_inner[c, n] = fg[n]
            mr, mi = fm[n][:, 0:B], fm[n][:, B:]
            gr, gi = fg[n][:, 0:B], fg[n][:, B:]
            pr, pi = mr * gr + mi * gi, mr * gi - mi * gr
            re, im = (pr, pi) if re is None else (re + pr, im + pi)
        cross.append((re, im))
    ys = inverse_pair(r, cross)
    for i in range(2):
        r.gk[2 * p + i] = ys[i]


def channel_stats(r, c):
    x = r.raw_flat[channel_rows(c), :]
    r.stat[0, pl.ds(c, 1), :] = jnp.sum(x * x, axis=0, keepdims=True)
    r.stat[1, pl.ds(c, 1), :] = jnp.sum(x * r.gk[c], axis=0, keepdims=True)


def filter_products(r, p):
    kernels = []
    for i in range(2):
        c = 2 * p + i
        square = jnp.sum(r.stat[0, pl.ds(c, 1), :], axis=1, keepdims=True)
        kernels.append(to_low(r.raw_flat[channel_rows(c), :] * (1.0 / jnp.sqrt(square + EPSILON))))
    fk = forward_pair(r, jnp.concatenate(kernels, axis=1))
    for i in range(2):
        c = 2 * p + i
        rows = channel_rows(c)
        kr, ki = fk[i][:, 0:B] * (1.0 / L), fk[i][:, B:] * (1.0 / L)
        specs = []
        for n in range(2):
            mr, mi = r.f_mixed[c, n, :, 0:B], r.f_mixed[c, n, :, B:]
            specs.append((mr * kr - mi * ki, mr * ki + mi * kr))
        ys = inverse_pair(r, specs)
        for n in range(2):
            r.conv[n, rows, :] = ys[n]
        specs = []
        for n in range(2):
            gr, gi = r.f_inner[c, n, :, 0:B], r.f_inner[c, n, :, B:]
            specs.append((gr * kr + gi * ki, gi * kr - gr * ki))
        ys = inverse_pair(r, specs)
        for n in range(2):
            r.back[n, rows, :] = ys[n]


def finish(r, n):
    gain = jnp.broadcast_to(to_column(r.skip[...], CH, 0), (CH, B))[None]

    def step(j, carry):
        part = pl.ds(j * BLK, BLK)
        rows = pl.ds(pl.multiple_of(j * (BLK * CH), BLK * CH), BLK * CH)
        shape = (BLK, CH, B)
        full = r.conv[n, rows, :].reshape(shape) + gain * r.mixed[n, rows, :].reshape(shape)
        r.o_gout[n, part] = to_low(r.cot[n, part].astype(F32) * full)
        full = r.back[n, rows, :].reshape(shape) + gain * r.inner[n, rows, :].reshape(shape)
        r.o_val[n, part] = to_low(full * r.gin[n, part].astype(F32))
        r.o_gin[n, part] = to_low(full * r.val[n, part].astype(F32))
        return carry

    lax.fori_loop(0, A // BLK, step, 0)


SMALL = ("bands", "w_in", "b_in", "w_mid", "b_mid", "w_out", "rate", "skip")
TABLES = ("w1", "w1t", "fwd", "inv", "turn")
LARGE = ("val", "gin", "cot", "gout")
OUTS = ("h_val", "h_gin", "h_gout", "own", "third", "g_skip")
BIG = (2, A, CH, B)
FULL = (2, A * CH, B)
SCRATCH = {
    "bands": ((2, 48, 128), jnp.int32),
    "w_in": ((33, 64), F32),
    "b_in": ((1, 64), F32),
    "w_mid": ((2, 64, 64), F32),
    "b_mid": ((2, 64), F32),
    "w_out": ((64, 128), F32),
    "rate": ((1, 128), F32),
    "skip": ((1, CH), F32),
    "w1": ((2 * A, A), LOW),
    "w1t": ((A, 2 * A), LOW),
    "fwd": ((2 * B, 2 * B), LOW),
    "inv": ((2 * B, 2 * B), LOW),
    "turn": ((2, A, B), F32),
    "val": (BIG, LOW),
    "gin": (BIG, LOW),
    "cot": (BIG, LOW),
    "gout": (BIG, LOW),
    "o_val": (BIG, LOW),
    "o_gin": (BIG, LOW),
    "o_gout": (BIG, LOW),
    "w_pad": ((48, 64), F32),
    "k_in": ((64, 144), LOW),
    "k_mid": ((2, 64, 192), LOW),
    "k_back": ((2, 64, 192), LOW),
    "w_own": ((2 * CH, 64), F32),
    "k_out": ((2 * CH, 192), LOW),
    "k_outback": ((64, 6 * CH), LOW),
    "rate_col": ((2 * CH, 128), F32),
    "bias_col": ((2, 64, 128), F32),
    "feat": ((128, TB // 2), LOW),
    "act": ((3, 128, TB // 2), LOW),
    "der": ((3, 64, TB // 2), F32),
    "raw_all": ((A, CH, B), F32),
    "raw_other": ((ABLK // 2, CH, B), F32),
    "grad_own": ((ABLK, CH, B), F32),
    "grad_other": ((ABLK // 2, CH, B), F32),
    "total": ((CH * ABLK, B), F32),
    "half": ((CH // 2, 2, 2, 2, ABLK // 2, B), F32),
    "side_out": ((CH // 2, 2, 2, 2, ABLK, B), F32),
    "side": ((CH // 2, 5, 2, ABLK, B), F32),
    "stat": ((2, CH, B), F32),
    "along": ((NSEQ, CH, B), F32),
    "mixed": (FULL, F32),
    "inner": (FULL, F32),
    "f_mixed": ((CH, 2, A, 2 * B), F32),
    "f_inner": ((CH, 2, A, 2 * B), F32),
    "gk": ((CH, A, B), F32),
    "conv": (FULL, F32),
    "back": (FULL, F32),
    "acc": ((3, 128, 128), F32),
    "acc_out": ((4 * CH, 128), F32),
    "acc_bias": ((2, 64, 128), F32),
    "acc_rate": ((2 * CH, 128), F32),
    "skip_part": ((CH, 1), F32),
    "block": ((2, 64, 128), F32),
    "share": ((NSEQ, 8, 256), F32),
    "first": ((NSEQ, 8, 256), F32),
    "second": ((16, 8, 256), F32),
}
N_LOCAL = len(SMALL) + len(TABLES) + len(LARGE)


def main_kernel(*refs):
    ins = refs[:N_LOCAL]
    outs = refs[N_LOCAL : N_LOCAL + len(OUTS)]
    names = list(SCRATCH)
    scratch = refs[N_LOCAL + len(OUTS) :]
    r = Refs(**dict(zip(OUTS, outs)), **dict(zip(names, scratch)))
    (load_sem, out_sem, ag_send, ag_recv, cross_send, cross_recv, relay_send, relay_recv, half_send, half_recv, rs_send, rs_recv,
     sem_a, recv_a, sem_b, recv_b, sem_c, recv_c, sem_d, recv_d) = scratch[len(names) :]
    r.raw_flat = r.raw_all.reshape(A * CH, B)
    chan, seq = lax.axis_index("chan"), lax.axis_index("seq")
    barrier = pltpu.get_barrier_semaphore()

    def signal(device):
        pl.semaphore_signal(barrier, inc=1, device_id=device, device_id_type=MESH)

    x, z = lax.div(seq, 2), lax.rem(seq, 2)
    yz, core = lax.div(chan, 2), lax.rem(chan, 2)
    first_id, second_id = 2 * x + core, 2 * yz + z

    xr, xl, xo = lax.rem(x + 1, 4), lax.rem(x + 3, 4), lax.rem(x + 2, 4)
    other = 1 - z
    near_seq = (2 * x + other, 2 * xr + z, 2 * xr + other, 2 * xl + z, 2 * xl + other)
    near = tuple((chan, to) for to in near_seq)
    partner = (2 * yz + 1 - core, seq)
    to_r, to_l = near[1], near[3]

    def seq_peer(d):
        return (chan, lax.rem(seq + d, NSEQ))

    def first_peer(d):
        to = lax.rem(first_id + d, 8)
        return (2 * yz + lax.rem(to, 2), 2 * lax.div(to, 2) + z)

    def second_peer(d):
        to = lax.rem(second_id + d, 16)
        return (2 * lax.div(to, 2) + core, 2 * x + lax.rem(to, 2))

    def hail(d, carry):
        signal(seq_peer(d))
        signal(first_peer(d))
        return carry

    def hail_second(d, carry):
        signal(second_peer(d))
        return carry

    loads = {}
    for i, name in enumerate(SMALL + TABLES + LARGE):
        loads[name] = pltpu.make_async_copy(ins[i], getattr(r, name), load_sem.at[i])
    for name in SMALL:
        loads[name].start()
    lax.fori_loop(1, 8, hail, 0)
    lax.fori_loop(1, 16, hail_second, 0)
    for name in LARGE + TABLES:
        loads[name].start()
    for name in SMALL:
        loads[name].wait()

    half = ABLK // 2
    piece = CHUNK // 128
    n_piece = ABLK // piece

    def row_of(xx, zz):
        return (2 * xx + zz) * ABLK

    def gather(i, j, device=None):
        part = r.raw_all.at[pl.ds(row_of(x, z) + j * piece, piece)]
        return pltpu.make_async_remote_copy(
            src_ref=part, dst_ref=part, send_sem=ag_send.at[i, j], recv_sem=ag_recv.at[i, j],
            device_id=device or near[i], device_id_type=MESH,
        )

    def cross(j):
        return pltpu.make_async_remote_copy(
            src_ref=r.raw_other.at[pl.ds(j * piece, piece)],
            dst_ref=r.raw_all.at[pl.ds(row_of(x, z) + (2 * core + j) * piece, piece)],
            send_sem=cross_send.at[j], recv_sem=cross_recv.at[j],
            device_id=partner, device_id_type=MESH,
        )

    def send_chunk(j):
        cross(j).start()
        for i in range(5):
            gather(i, 2 * core + j).start()

    def relay(h, lane):
        row = jnp.where(h == 0, row_of(xl, (z, other)[lane]), row_of(xr, (z, other)[lane]) + half)
        part = r.raw_all.at[pl.ds(row, half)]
        i = 2 * h + lane
        return pltpu.make_async_remote_copy(
            src_ref=part, dst_ref=part, send_sem=relay_send.at[i], recv_sem=relay_recv.at[i],
            device_id=(chan, jnp.where(h == 0, near_seq[1], near_seq[3])), device_id_type=MESH,
        )

    def pass_on(h):
        for lane in range(2):
            arrived(1 + 2 * h + lane, 2 * h, 2 * h + 2)
            relay(h, lane).start()

    def arrived(i, start, stop):
        def step(j, carry):
            gather(i, j, partner).wait_recv()
            return carry

        lax.fori_loop(start, stop, step, 0)

    zs = (other, z)

    def rows_at(p, row, count):
        return r.gk.at[pl.ds(2 * p, 2), pl.ds(pl.multiple_of(row, half), count)]

    def far_half(p, w, h):
        return pltpu.make_async_remote_copy(
            src_ref=rows_at(p, row_of(xo, zs[w]) + h * half, half), dst_ref=r.half.at[p, w, h],
            send_sem=half_send.at[p, 2 * w + h], recv_sem=half_recv.at[p, 2 * w + h],
            device_id=(to_r, to_l)[h], device_id_type=MESH,
        )

    def near_block(p, i):
        w = i % 2
        src = rows_at(p, row_of(x, other), ABLK) if i == 0 else r.side_out.at[p, w, (i - 1) // 2]
        return pltpu.make_async_remote_copy(
            src_ref=src, dst_ref=r.side.at[p, i], send_sem=rs_send.at[p, i], recv_sem=rs_recv.at[p, i],
            device_id=near[i], device_id_type=MESH,
        )

    def scatter_far(p):
        for w in range(2):
            for h in range(2):
                far_half(p, w, h).start()
        near_block(p, 0).start()

    def scatter_near(p):
        for w in range(2):
            for h in range(2):
                far_half(p, w, h).wait_recv()
                row = row_of((xr, xl)[h], zs[w])
                for i in range(2):
                    mine = r.gk[2 * p + i, pl.ds(pl.multiple_of(row, half), half), :]
                    rest = r.gk[2 * p + i, pl.ds(pl.multiple_of(row + half, half), half), :]
                    extra = r.half[p, w, h, i]
                    r.side_out[p, w, h, i, 0:half, :] = mine + extra if h == 0 else mine
                    r.side_out[p, w, h, i, half:, :] = rest if h == 0 else rest + extra
        for i in range(1, 5):
            near_block(p, i).start()

    prepare_weights(r, chan, 2 * yz + 1 - core)
    net_chunk(r, seq, core, 0)
    pl.semaphore_wait(barrier, 7 + 7 + 15)
    send_chunk(0)
    net_chunk(r, seq, core, 1)
    send_chunk(1)

    for j in range(2):
        cross(j).wait_recv()
        for i in range(5):
            gather(i, 2 * (1 - core) + j).start()

    prepare_backward(r)
    for name in LARGE:
        loads[name].wait()
    acc = gate_products(r, 0)
    acc = acc + gate_products(r, 1)
    r.skip_part[...] = jnp.sum(acc, axis=1, keepdims=True)
    for name in TABLES:
        loads[name].wait()

    spectra(r, 0)
    scatter_far(0)
    pass_on(core)
    spectra(r, 1)
    scatter_far(1)
    pass_on(1 - core)

    def pair_step(p, carry):
        spectra(r, p)
        scatter_far(p)
        scatter_near(p - 2)
        return carry

    lax.fori_loop(2, CH // 2, pair_step, 0)
    scatter_near(CH // 2 - 2)
    arrived(0, 0, n_piece)
    for lane in range(2):
        arrived(1 + lane, n_piece // 2, n_piece)
        arrived(3 + lane, 0, n_piece // 2)
    for h in range(2):
        for lane in range(2):
            relay(h, lane).wait_recv()

    def stats_step(c, carry):
        channel_stats(r, c)
        return carry

    lax.fori_loop(0, CH, stats_step, 0)

    def run(size, make):
        def start(d, carry):
            make(d).start()
            return carry

        def wait(d, carry):
            make(d).wait()
            return carry

        lax.fori_loop(1, size, start, 0)
        return lambda: lax.fori_loop(1, size, wait, 0)

    def make_a(d):
        return pltpu.make_async_remote_copy(
            src_ref=r.stat.at[1], dst_ref=r.along.at[d],
            send_sem=sem_a.at[d], recv_sem=recv_a.at[d], device_id=seq_peer(d), device_id_type=MESH,
        )

    wait_along = run(NSEQ, make_a)

    filter_products(r, 0)
    scatter_near(CH // 2 - 1)

    def product_step(p, carry):
        filter_products(r, p)
        return carry

    lax.fori_loop(1, EARLY, product_step, 0)
    results = []

    def leave(n):
        for i, (src, dst) in enumerate(((r.o_val, r.h_val), (r.o_gin, r.h_gin), (r.o_gout, r.h_gout))):
            copy = pltpu.make_async_copy(src.at[n], dst.at[n], out_sem.at[3 * n + i])
            copy.start()
            results.append(copy)

    def settle(p, carry):
        for i in range(5):
            near_block(p, i).wait_recv()
        row = pl.multiple_of(row_of(x, z), ABLK)
        for i in range(2):
            c = 2 * p + i
            total = r.gk[c, pl.ds(row, ABLK), :]
            for k in range(5):
                total = total + r.side[p, k, i]
            r.total[pl.ds(pl.multiple_of(c * ABLK, ABLK), ABLK), :] = total
        return carry

    lax.fori_loop(0, CH // 2, settle, 0)
    wait_along()
    along = r.stat[1]
    for d in range(1, NSEQ):
        along = along + r.along[d]
    along = jnp.sum(along, axis=1, keepdims=True) * (1.0 / L)
    norm = jnp.sqrt(jnp.sum(r.stat[0], axis=1, keepdims=True) + EPSILON)
    scale_gk = jnp.broadcast_to((1.0 / L) / norm, (CH, B))
    scale_raw = jnp.broadcast_to(along / (norm * norm * norm), (CH, B))

    def gradient(half_id):
        def step(i, carry):
            row = half_id * half + i
            total = r.total[pl.ds(row, CH, stride=ABLK), :]
            r.grad_own[row] = total * scale_gk - r.raw_all[row_of(x, z) + row] * scale_raw
            return carry

        lax.fori_loop(0, half, step, 0, unroll=8)

    gradient(1 - core)
    hand = pltpu.make_async_remote_copy(
        src_ref=r.grad_own.at[pl.ds((1 - core) * half, half)], dst_ref=r.grad_other,
        send_sem=sem_a.at[0], recv_sem=recv_a.at[0], device_id=partner, device_id_type=MESH,
    )
    hand.start()
    gradient(core)
    hand.wait()

    def sent(j, carry):
        for i in range(5):
            near_block(j, i).wait_send()
            gather(i, j).wait_send()
        for i in range(4):
            far_half(j, i // 2, i % 2).wait_send()
        return carry

    net_backward(r, seq, core)
    pack_shares(r, core)

    def make_b(d):
        return pltpu.make_async_remote_copy(
            src_ref=r.share.at[lax.rem(first_id + d, 8)], dst_ref=r.first.at[d],
            send_sem=sem_b.at[d], recv_sem=recv_b.at[d], device_id=first_peer(d), device_id_type=MESH,
        )

    def make_c(d):
        return pltpu.make_async_remote_copy(
            src_ref=r.second.at[second_id], dst_ref=r.second.at[second_id],
            send_sem=sem_c.at[d], recv_sem=recv_c.at[d], device_id=second_peer(d), device_id_type=MESH,
        )

    def make_d(d):
        return pltpu.make_async_remote_copy(
            src_ref=r.third.at[first_id], dst_ref=r.third.at[first_id],
            send_sem=sem_d.at[d], recv_sem=recv_d.at[d], device_id=first_peer(d), device_id_type=MESH,
        )

    wait = run(8, make_b)
    lax.fori_loop(EARLY, EARLY + UNDER_FIRST, product_step, 0)
    wait()
    both = r.share[first_id]
    for d in range(1, 8):
        both = both + r.first[d]
    factor = 1.0 / math.sqrt(16 * L)
    r.second[second_id] = both * factor
    wait = run(16, make_c)
    lax.fori_loop(EARLY + UNDER_FIRST, CH // 2, product_step, 0)
    for n in range(2):
        finish(r, n)
        leave(n)
    wait()
    total = r.second[0]
    for c in range(1, 16):
        total = total + r.second[c]
    r.third[first_id] = total
    for c in range(8):
        r.own[c, core] = r.second[2 * c, :, 128:256] + r.second[2 * c + 1, :, 128:256]
    wait = run(8, make_d)
    part = r.own.at[:, core]
    swap = pltpu.make_async_remote_copy(
        src_ref=part, dst_ref=part, send_sem=sem_d.at[0], recv_sem=recv_d.at[0],
        device_id=(2 * yz + 1 - core, seq), device_id_type=MESH,
    )
    swap.start()
    r.g_skip[...] = to_row(r.own[yz, core][:, 113:114])
    wait()
    swap.wait()
    lax.fori_loop(0, CH // 2, sent, 0)
    for i in range(2):
        cross(i).wait_send()
        for lane in range(2):
            relay(i, lane).wait_send()
    for copy in results:
        copy.wait()


def write_kernel(
    i_val, i_gin, i_gout, i_second, i_third, skip,
    o_val, o_gin, o_gout, o_skip, o_in, o_bin, o_mid, o_bmid, o_out, o_rate,
    stage, second, third, g_skip, g_in, g_bin, g_mid, g_bmid, g_out, g_rate, in_sem, out_sem, small_sem,
):
    loads, stores = [], []
    for i, (src, dst) in enumerate(((i_val, o_val), (i_gin, o_gin), (i_gout, o_gout))):
        for q in range(4):
            part = (q // 2, pl.ds(q % 2 * (A // 2), A // 2))
            loads.append(pltpu.make_async_copy(src.at[part], stage.at[(i,) + part], in_sem.at[4 * i + q]))
            stores.append(pltpu.make_async_copy(stage.at[(i,) + part], dst.at[part], out_sem.at[4 * i + q]))
    small = [
        pltpu.make_async_copy(i_second, second, small_sem.at[0]),
        pltpu.make_async_copy(i_third, third, small_sem.at[1]),
        pltpu.make_async_copy(skip, g_skip, small_sem.at[2]),
    ]
    for copy in small + loads:
        copy.start()
    for load, store in zip(loads, stores):
        load.wait()
        store.start()
    for copy in small:
        copy.wait()
    hidden = third[...].reshape(64, 256)
    g_mid[0] = hidden[:, 0:64]
    g_mid[1] = pltpu.roll(hidden[:, 0:128], 64, 1)[:, 0:64]
    flat = jnp.transpose(hidden[:, 128:256])
    g_in[...] = flat[0:33, :]
    g_bin[...] = flat[33:34, :]
    g_bmid[...] = flat[34:36, :]
    own = jnp.transpose(second[...].reshape(128, 128))
    g_out[...] = own[48:112, :]
    g_rate[...] = own[112:113, :]
    pairs = (
        (g_skip, o_skip), (g_in, o_in), (g_bin, o_bin), (g_mid, o_mid), (g_bmid, o_bmid), (g_out, o_out),
        (g_rate, o_rate),
    )
    for i, (src, dst) in enumerate(pairs):
        copy = pltpu.make_async_copy(src, dst, small_sem.at[3 + i])
        copy.start()
        stores.append(copy)
    for copy in stores:
        copy.wait()


def sds(shape, dtype=F32):
    return jax.ShapeDtypeStruct(shape, dtype)


VM = pl.BlockSpec(memory_space=pltpu.VMEM)
HB = pl.BlockSpec(memory_space=pltpu.HBM)
DMA = pltpu.SemaphoreType.DMA


def to_natural(x):
    return x.reshape(2, CH, A, B).transpose(0, 2, 1, 3)


def from_natural(x):
    return x.transpose(0, 2, 1, 3).reshape(2, CH, L)


def local(
    value, gate_in, gate_out, cotangent, skip_gain,
    weight_in, bias_in, weight_mid, bias_mid, weight_out, decay_rate,
):
    small = (
        row_constants(), weight_in.T, bias_in.reshape(1, 64), weight_mid, bias_mid, weight_out.T,
        decay_rate.reshape(1, 128), skip_gain.reshape(1, CH),
    )
    large = tuple(to_natural(x) for x in (value, gate_in, cotangent, gate_out))
    big = sds(BIG, LOW)
    o_val, o_gin, o_gout, own, third, g_skip = pl.pallas_call(
        main_kernel,
        out_shape=[big, big, big, sds((8, 2, 8, 128)), sds((NSEQ, 8, 256)), sds((1, CH))],
        in_specs=[HB] * N_LOCAL,
        out_specs=[HB] * 3 + [VM] * 3,
        scratch_shapes=[pltpu.VMEM(shape, dtype) for shape, dtype in SCRATCH.values()]
        + [
            DMA((N_LOCAL,)), DMA((6,)), DMA((5, 4)), DMA((5, 4)), DMA((2,)), DMA((2,)), DMA((4,)), DMA((4,)),
            DMA((4, 4)), DMA((4, 4)), DMA((4, 5)), DMA((4, 5)), DMA((NSEQ,)), DMA((NSEQ,)),
            DMA((NSEQ,)), DMA((NSEQ,)), DMA((NCHAN,)), DMA((NCHAN,)), DMA((NSEQ,)), DMA((NSEQ,)),
        ],
        compiler_params=pltpu.CompilerParams(
            collective_id=0, has_side_effects=True, vmem_limit_bytes=VMEM_MAIN
        ),
        name="hyena_backward",
    )(*small, *transform_tables(), *large)
    o_val, o_gin, o_gout, g_skip, g_in, g_bin, g_mid, g_bmid, g_out, g_rate = pl.pallas_call(
        write_kernel,
        out_shape=[
            big, big, big, sds((1, CH)), sds((33, 64)), sds((1, 64)), sds((2, 64, 64)), sds((2, 64)),
            sds((64, 128)), sds((1, 128)),
        ],
        in_specs=[HB] * 6,
        out_specs=[HB] * 10,
        scratch_shapes=[
            pltpu.VMEM((3,) + BIG, LOW), pltpu.VMEM((8, 2, 8, 128), F32), pltpu.VMEM((NSEQ, 8, 256), F32),
            pltpu.VMEM((1, CH), F32), pltpu.VMEM((33, 64), F32), pltpu.VMEM((1, 64), F32),
            pltpu.VMEM((2, 64, 64), F32), pltpu.VMEM((2, 64), F32), pltpu.VMEM((64, 128), F32),
            pltpu.VMEM((1, 128), F32),
            DMA((12,)), DMA((12,)), DMA((10,)),
        ],
        compiler_params=pltpu.CompilerParams(vmem_limit_bytes=VMEM_MAIN),
        name="write_results",
    )(o_val, o_gin, o_gout, own, third, g_skip)
    return (
        from_natural(o_val), from_natural(o_gin), from_natural(o_gout), g_skip.reshape(CH),
        g_in.T, g_bin.reshape(64), g_mid, g_bmid, g_out.T, g_rate.reshape(128),
    )


def solution(mesh):
    return jax.shard_map(
        local,
        mesh=mesh,
        in_specs=(
            P("seq", "chan", None), P("seq", "chan", None), P("seq", "chan", None), P("seq", "chan", None),
            P("chan"), P(), P(), P(), P(), P(), P(),
        ),
        out_specs=(
            P("seq", "chan", None), P("seq", "chan", None), P("seq", "chan", None),
            P("chan"), P(), P(), P(), P(), P(), P(),
        ),
        check_vma=False,
    )
```

```python
import functools
import math

import jax
import jax.numpy as jnp
import numpy as np
from jax import lax
from jax.experimental import pallas as pl
from jax.experimental.pallas import tpu as pltpu
from jax.sharding import PartitionSpec as P

EPSILON = 1e-06
HIGHEST = lax.Precision.HIGHEST
L = 32768
A = 256
B = 128
CH = 8
NSEQ = 8
NCHAN = 16
ABLK = A // NSEQ
TB = L // NSEQ
CHUNK = 1024
LOW = jnp.bfloat16
F32 = jnp.float32
MESH = pl.DeviceIdType.MESH


def band_table(length, bands):
    highest = length / 4.0
    return np.array(
        [math.floor(highest ** (number / (bands - 1)) + 0.5) for number in range(bands)], np.int64
    )


def row_constants():
    freq = np.zeros((48, 128), np.int32)
    off = np.zeros((48, 128), np.int32)
    bands = band_table(L, 16)
    freq[1:17] = bands[:, None]
    off[1:17] = L // 4
    freq[17:33] = bands[:, None]
    return np.stack([freq, off])


def transform_tables():
    k = np.arange(A)[:, None]
    rows = 2.0 * np.pi * (((4 * k + 1) * np.arange(A)[None, :]) % 1024) / 1024.0
    w1 = np.concatenate([np.cos(rows), -np.sin(rows)], axis=0)
    turn = 2.0 * np.pi * (((4 * k + 1) * np.arange(B)[None, :]) % (4 * L)) / (4.0 * L)
    q = np.arange(B)
    cols = 2.0 * np.pi * ((q[:, None] * q[None, :]) % B) / B
    c, s = np.cos(cols), np.sin(cols)
    fwd = np.block([[c, -s], [s, c]])
    inv = np.block([[c, s], [-s, c]])
    low = np.dtype(LOW)
    return (
        w1.astype(low),
        w1.T.astype(low),
        fwd.astype(low),
        inv.astype(low),
        np.stack([np.cos(turn), np.sin(turn)]).astype(np.float32),
    )


def poly_fit():
    x = (np.cos(np.pi * (np.arange(64) + 0.5) / 64) + 1) / 2 * (np.pi / 2 * 1.002) ** 2
    r = np.sqrt(x)
    sin_c = np.polynomial.polynomial.polyfit(x, np.sin(r) / r, 4)
    cos_c = np.polynomial.polynomial.polyfit(x, np.cos(r), 5)
    return [float(v) for v in sin_c], [float(v) for v in cos_c]


SIN_C, COS_C = poly_fit()


def horner(x, coefs):
    acc = jnp.full_like(x, coefs[-1])
    for value in coefs[-2::-1]:
        acc = acc * x + value
    return acc


def sin_small(r):
    return r * horner(r * r, SIN_C)


def sin_cos(z):
    n = jnp.floor(z * (1.0 / math.pi) + 0.5)
    r = z - n * 3.140625
    r = r - n * 9.67653589793e-4
    half = n * 0.5
    sign = 1.0 - 4.0 * (half - jnp.floor(half))
    r2 = r * r
    return sign * (r * horner(r2, SIN_C)), sign * horner(r2, COS_C)


def dot_full(x, y):
    return jnp.dot(x, y, precision=HIGHEST, preferred_element_type=F32)


def dot_nt(x, y, precision=None):
    return lax.dot_general(x, y, (((1,), (1,)), ((), ())), precision=precision, preferred_element_type=F32)


def dot_tn(x, y, precision=None):
    return lax.dot_general(x, y, (((0,), (0,)), ((), ())), precision=precision, preferred_element_type=F32)


def low_dot(x, y):
    return jnp.dot(x, y, preferred_element_type=F32)


def split(x):
    hi = x.astype(LOW)
    return hi, (x - hi.astype(F32)).astype(LOW)


def iota(shape, dim):
    return lax.broadcasted_iota(jnp.int32, shape, dim)


def to_column(row, size, shift):
    n = row.shape[1]
    pick = iota((size, n), 0) + shift == iota((size, n), 1)
    return jnp.sum(jnp.where(pick, jnp.broadcast_to(row, (size, n)), 0.0), axis=1, keepdims=True)


def to_row(col):
    n = col.shape[0]
    pick = iota((n, n), 0) == iota((n, n), 1)
    return jnp.sum(jnp.where(pick, jnp.broadcast_to(col, (n, n)), 0.0), axis=0, keepdims=True)


def repeat_matrix(rows, period, times):
    shape = (rows, period * times)
    j = iota(shape, 1)
    hit = j == iota(shape, 0)
    for m in range(1, times):
        hit = hit | (j == iota(shape, 0) + m * period)
    return jnp.where(hit, 1.0, 0.0)


def hi_hi_lo(w, period):
    hi = w.astype(LOW).astype(F32)
    lane = iota(w.shape, 1)
    out = jnp.where(lane < 2 * period, hi, jnp.where(lane < 3 * period, w - hi, 0.0))
    return out.astype(LOW)


class Refs:
    def __init__(self, **refs):
        self.__dict__.update(refs)


def prepare_weights(r, chan, other):
    first = jnp.where(iota((8, 64), 0) == 1, jnp.broadcast_to(r.b_in[...], (8, 64)), 0.0)
    r.w_pad[0:32, :] = r.w_in[0:32, :]
    r.w_pad[32:40, :] = jnp.where(iota((8, 64), 0) == 0, jnp.broadcast_to(r.w_in[32:33, :], (8, 64)), first)
    r.w_pad[40:48, :] = jnp.zeros((8, 64), F32)
    r.k_in[...] = hi_hi_lo(dot_tn(r.w_pad[...], repeat_matrix(48, 48, 3), HIGHEST), 48)
    rep = repeat_matrix(64, 64, 3)
    for i in range(2):
        w = r.w_mid[i]
        r.k_mid[i] = hi_hi_lo(dot_full(w, rep), 64)
    row = iota((2 * CH, 128), 0)
    channel = jnp.where(row < CH, row + chan * CH, row - CH + other * CH)
    pick = jnp.where(iota((2 * CH, 128), 1) == channel, 1.0, 0.0)
    w_own = dot_nt(pick, r.w_out[...], HIGHEST)
    r.k_out[...] = hi_hi_lo(dot_full(w_own, rep), 64)
    r.w_own[...] = w_own
    rates = jnp.sum(jnp.where(pick > 0.5, jnp.broadcast_to(r.rate[...], (2 * CH, 128)), 0.0), axis=1, keepdims=True)
    r.rate_col[...] = jnp.broadcast_to(rates, (2 * CH, 128))
    r.bias_col[0] = jnp.broadcast_to(to_column(r.b_mid[0:1, :], 64, 0), (64, 128))
    r.bias_col[1] = jnp.broadcast_to(to_column(r.b_mid[1:2, :], 64, 0), (64, 128))


def prepare_backward(r):
    rep = repeat_matrix(64, 64, 3)
    for i in range(2):
        r.k_back[i] = hi_hi_lo(dot_tn(r.w_mid[i], rep, HIGHEST), 64)
    r.k_outback[...] = hi_hi_lo(dot_tn(r.w_own[...], repeat_matrix(2 * CH, 2 * CH, 3), HIGHEST), 2 * CH)


def wide(block, times):
    return jnp.concatenate([block] * times, axis=1)


def fraction(base):
    pos = base + iota((2 * CH, CHUNK), 1)
    return pos.astype(F32) * (1.0 / L)


def net_chunk(r, seq, core, j):
    per = CHUNK // 128
    lanes = pl.ds(j * CHUNK, CHUNK)
    pos = seq * TB + (2 * core + j) * CHUNK + iota((48, CHUNK), 1)
    row = iota((48, CHUNK), 0)
    phase = ((wide(r.bands[0], per) * pos + (wide(r.bands[1], per) + L // 2)) & (L - 1)) - L // 2
    phase = jnp.where(phase > L // 4, L // 2 - phase, phase)
    phase = jnp.where(phase < -(L // 4), -(L // 2) - phase, phase)
    wave = sin_small(phase.astype(F32) * (2.0 * math.pi / L))
    frac = pos.astype(F32) * (1.0 / L)
    hi, lo = split(jnp.where(row == 0, frac, jnp.where(row == 33, 1.0, wave)))
    r.feat[0:48, lanes] = hi
    r.feat[48:64, lanes] = jnp.zeros((16, CHUNK), LOW)
    r.feat[64:112, lanes] = lo
    r.feat[112:128, lanes] = jnp.zeros((16, CHUNK), LOW)
    z = low_dot(r.k_in[...], jnp.concatenate([hi, lo, hi], axis=0))
    for layer in range(3):
        s, c = sin_cos(z)
        r.der[layer, :, lanes] = c
        hi, lo = split(s)
        r.act[layer, 0:64, lanes] = hi
        r.act[layer, 64:128, lanes] = lo
        x = jnp.concatenate([hi, lo, hi], axis=0)
        if layer < 2:
            z = low_dot(r.k_mid[layer], x) + wide(r.bias_col[layer], per)
    raw = low_dot(r.k_out[...], x) * jnp.exp(-wide(r.rate_col[...], per) * frac[0 : 2 * CH, :])
    for i in range(per):
        r.raw_all[seq * ABLK + (2 * core + j) * per + i] = raw[0:CH, 128 * i : 128 * i + 128]
        r.raw_other[j * per + i] = raw[CH:, 128 * i : 128 * i + 128]


def net_backward(r, seq, core):
    per = CHUNK // 128
    r.acc[...] = jnp.zeros_like(r.acc)
    r.acc_out[...] = jnp.zeros_like(r.acc_out)
    r.acc_bias[...] = jnp.zeros_like(r.acc_bias)
    r.acc_rate[...] = jnp.zeros_like(r.acc_rate)

    def lane_sum(x):
        total = x[:, 0:128]
        for i in range(1, per):
            total = total + x[:, 128 * i : 128 * i + 128]
        return total

    def step(j, carry):
        lanes = pl.ds(pl.multiple_of(j * CHUNK, CHUNK), CHUNK)
        start = (2 * core + j) * per

        def rows(mine, first, others, second):
            return jnp.concatenate(
                [jnp.concatenate([mine[first + i], others[second + i]], axis=0) for i in range(per)], axis=1
            )

        grad = rows(r.grad_own, start, r.grad_other, j * per)
        raw = rows(r.raw_all, seq * ABLK + start, r.raw_other, j * per)
        frac = fraction(seq * TB + (2 * core + j) * CHUNK)
        r.acc_rate[...] -= lane_sum(grad * raw * frac)
        shaped = grad * jnp.exp(-wide(r.rate_col[...], per) * frac)
        hi = shaped.astype(LOW).astype(F32)
        lo = shaped - hi
        pair = jnp.concatenate([hi, lo], axis=0).astype(LOW)
        r.acc_out[...] += dot_nt(pair, r.act[2, :, lanes])
        d = low_dot(r.k_outback[...], jnp.concatenate([hi, lo, hi], axis=0).astype(LOW))
        for layer in (2, 1, 0):
            d = d * r.der[layer, :, lanes]
            hi, lo = split(d)
            pair = jnp.concatenate([hi, lo], axis=0)
            if layer:
                r.acc_bias[layer - 1] += lane_sum(d)
                r.acc[layer] += dot_nt(pair, r.act[layer - 1, :, lanes])
                d = low_dot(r.k_back[layer - 1], jnp.concatenate([hi, lo, hi], axis=0))
            else:
                r.acc[0] += dot_nt(pair, r.feat[:, lanes])
        return carry

    lax.fori_loop(0, TB // CHUNK // 2, step, 0, unroll=True)


def fold_halves(x):
    n = x.shape[0] // 2
    total = x[0:n] + x[n:]
    return total + pltpu.roll(total, 64, 1)


def pack_shares(r, core):
    lane = iota((64, 128), 1)
    r.block[0] = jnp.where(lane < 64, fold_halves(r.acc[1]), fold_halves(r.acc[2]))
    block = fold_halves(r.acc[0])
    block = jnp.where(lane == 34, jnp.sum(r.acc_bias[0], axis=1, keepdims=True), block)
    r.block[1] = jnp.where(lane == 35, jnp.sum(r.acc_bias[1], axis=1, keepdims=True), block)
    lane = iota((2 * CH, 128), 1)
    own = pltpu.roll(fold_halves(r.acc_out[...]), 48, 1)
    own = jnp.where(lane == 112, jnp.sum(r.acc_rate[...], axis=1, keepdims=True), own)
    own = jnp.where(lane > 112, 0.0, own)
    lane = iota((CH, 128), 1)
    theirs = own[CH:]
    own = jnp.where(lane == 113, r.skip_part[...], own[0:CH])

    def place(s, carry):
        rows = pl.ds(pl.multiple_of(8 * s, 8), 8)
        r.share[s, :, 0:128] = r.block[0, rows, :]
        apart = jnp.where(lax.rem(s, 2) == core, own, theirs)
        r.share[s, :, 128:256] = jnp.where(lane < 48, r.block[1, rows, :], apart)
        return carry

    lax.fori_loop(0, NSEQ, place, 0)


def to_low(x):
    return x.astype(LOW)


def channel_rows(c):
    return pl.ds(c, A, stride=CH)


def forward_pair(r, x):
    tc, ts = r.turn[0], r.turn[1]
    g = low_dot(r.w1[...], x)
    parts = []
    for n in range(2):
        re, im = g[0:A, n * B : n * B + B], g[A:, n * B : n * B + B]
        parts.append(jnp.concatenate([to_low(re * tc + im * ts), to_low(im * tc - re * ts)], axis=1))
    f = low_dot(jnp.concatenate(parts, axis=0), r.fwd[...])
    return f[0:A], f[A:]


def inverse_pair(r, specs):
    tc, ts = r.turn[0], r.turn[1]
    s = jnp.concatenate([jnp.concatenate([to_low(re), to_low(im)], axis=1) for re, im in specs], axis=0)
    t = low_dot(s, r.inv[...])
    cols = []
    for n in range(2):
        re, im = t[n * A : n * A + A, 0:B], t[n * A : n * A + A, B:]
        cols.append(jnp.concatenate([to_low(re * tc - im * ts), to_low(re * ts + im * tc)], axis=0))
    y = low_dot(r.w1t[...], jnp.concatenate(cols, axis=1))
    return y[:, 0:B], y[:, B:]


BLK = 16
EARLY = 2
UNDER_FIRST = 1
VMEM_MAIN = 56 << 20


def gate_products(r, n):
    def step(j, acc):
        part = pl.ds(j * BLK, BLK)
        rows = pl.ds(pl.multiple_of(j * (BLK * CH), BLK * CH), BLK * CH)
        m = r.val[n, part].astype(F32) * r.gin[n, part].astype(F32)
        g = r.cot[n, part].astype(F32) * r.gout[n, part].astype(F32)
        r.mixed[n, rows, :] = m.reshape(BLK * CH, B)
        r.inner[n, rows, :] = g.reshape(BLK * CH, B)
        return acc + jnp.sum(m * g, axis=0)

    return lax.fori_loop(0, A // BLK, step, jnp.zeros((CH, B), F32))


def spectra(r, p):
    cross = []
    for i in range(2):
        c = 2 * p + i
        rows = channel_rows(c)
        fm = forward_pair(r, jnp.concatenate([to_low(r.mixed[n, rows, :]) for n in range(2)], axis=1))
        fg = forward_pair(r, jnp.concatenate([to_low(r.inner[n, rows, :]) for n in range(2)], axis=1))
        re = im = None
        for n in range(2):
            r.f_mixed[c, n] = fm[n]
            r.f_inner[c, n] = fg[n]
            mr, mi = fm[n][:, 0:B], fm[n][:, B:]
            gr, gi = fg[n][:, 0:B], fg[n][:, B:]
            pr, pi = mr * gr + mi * gi, mr * gi - mi * gr
            re, im = (pr, pi) if re is None else (re + pr, im + pi)
        cross.append((re, im))
    ys = inverse_pair(r, cross)
    for i in range(2):
        r.gk[2 * p + i] = ys[i]


def channel_stats(r, c):
    x = r.raw_flat[channel_rows(c), :]
    r.stat[0, pl.ds(c, 1), :] = jnp.sum(x * x, axis=0, keepdims=True)
    r.stat[1, pl.ds(c, 1), :] = jnp.sum(x * r.gk[c], axis=0, keepdims=True)


def filter_products(r, p):
    kernels = []
    for i in range(2):
        c = 2 * p + i
        square = jnp.sum(r.stat[0, pl.ds(c, 1), :], axis=1, keepdims=True)
        kernels.append(to_low(r.raw_flat[channel_rows(c), :] * (1.0 / jnp.sqrt(square + EPSILON))))
    fk = forward_pair(r, jnp.concatenate(kernels, axis=1))
    for i in range(2):
        c = 2 * p + i
        rows = channel_rows(c)
        kr, ki = fk[i][:, 0:B] * (1.0 / L), fk[i][:, B:] * (1.0 / L)
        specs = []
        for n in range(2):
            mr, mi = r.f_mixed[c, n, :, 0:B], r.f_mixed[c, n, :, B:]
            specs.append((mr * kr - mi * ki, mr * ki + mi * kr))
        ys = inverse_pair(r, specs)
        for n in range(2):
            r.conv[n, rows, :] = ys[n]
        specs = []
        for n in range(2):
            gr, gi = r.f_inner[c, n, :, 0:B], r.f_inner[c, n, :, B:]
            specs.append((gr * kr + gi * ki, gi * kr - gr * ki))
        ys = inverse_pair(r, specs)
        for n in range(2):
            r.back[n, rows, :] = ys[n]


def finish(r, n):
    gain = jnp.broadcast_to(to_column(r.skip[...], CH, 0), (CH, B))[None]

    def step(j, carry):
        part = pl.ds(j * BLK, BLK)
        rows = pl.ds(pl.multiple_of(j * (BLK * CH), BLK * CH), BLK * CH)
        shape = (BLK, CH, B)
        full = r.conv[n, rows, :].reshape(shape) + gain * r.mixed[n, rows, :].reshape(shape)
        r.o_gout[n, part] = to_low(r.cot[n, part].astype(F32) * full)
        full = r.back[n, rows, :].reshape(shape) + gain * r.inner[n, rows, :].reshape(shape)
        r.o_val[n, part] = to_low(full * r.gin[n, part].astype(F32))
        r.o_gin[n, part] = to_low(full * r.val[n, part].astype(F32))
        return carry

    lax.fori_loop(0, A // BLK, step, 0)


SMALL = ("bands", "w_in", "b_in", "w_mid", "b_mid", "w_out", "rate", "skip")
TABLES = ("w1", "w1t", "fwd", "inv", "turn")
LARGE = ("val", "gin", "cot", "gout")
OUTS = ("h_val", "h_gin", "h_gout", "own", "third", "g_skip")
BIG = (2, A, CH, B)
FULL = (2, A * CH, B)
SCRATCH = {
    "bands": ((2, 48, 128), jnp.int32),
    "w_in": ((33, 64), F32),
    "b_in": ((1, 64), F32),
    "w_mid": ((2, 64, 64), F32),
    "b_mid": ((2, 64), F32),
    "w_out": ((64, 128), F32),
    "rate": ((1, 128), F32),
    "skip": ((1, CH), F32),
    "w1": ((2 * A, A), LOW),
    "w1t": ((A, 2 * A), LOW),
    "fwd": ((2 * B, 2 * B), LOW),
    "inv": ((2 * B, 2 * B), LOW),
    "turn": ((2, A, B), F32),
    "val": (BIG, LOW),
    "gin": (BIG, LOW),
    "cot": (BIG, LOW),
    "gout": (BIG, LOW),
    "o_val": (BIG, LOW),
    "o_gin": (BIG, LOW),
    "o_gout": (BIG, LOW),
    "w_pad": ((48, 64), F32),
    "k_in": ((64, 144), LOW),
    "k_mid": ((2, 64, 192), LOW),
    "k_back": ((2, 64, 192), LOW),
    "w_own": ((2 * CH, 64), F32),
    "k_out": ((2 * CH, 192), LOW),
    "k_outback": ((64, 6 * CH), LOW),
    "rate_col": ((2 * CH, 128), F32),
    "bias_col": ((2, 64, 128), F32),
    "feat": ((128, TB // 2), LOW),
    "act": ((3, 128, TB // 2), LOW),
    "der": ((3, 64, TB // 2), F32),
    "raw_all": ((A, CH, B), F32),
    "raw_other": ((ABLK // 2, CH, B), F32),
    "grad_own": ((ABLK, CH, B), F32),
    "grad_other": ((ABLK // 2, CH, B), F32),
    "total": ((CH * ABLK, B), F32),
    "half": ((CH // 2, 2, 2, 2, ABLK // 2, B), F32),
    "side_out": ((CH // 2, 2, 2, 2, ABLK, B), F32),
    "side": ((CH // 2, 5, 2, ABLK, B), F32),
    "stat": ((2, CH, B), F32),
    "along": ((NSEQ, CH, B), F32),
    "mixed": (FULL, F32),
    "inner": (FULL, F32),
    "f_mixed": ((CH, 2, A, 2 * B), F32),
    "f_inner": ((CH, 2, A, 2 * B), F32),
    "gk": ((CH, A, B), F32),
    "conv": (FULL, F32),
    "back": (FULL, F32),
    "acc": ((3, 128, 128), F32),
    "acc_out": ((4 * CH, 128), F32),
    "acc_bias": ((2, 64, 128), F32),
    "acc_rate": ((2 * CH, 128), F32),
    "skip_part": ((CH, 1), F32),
    "block": ((2, 64, 128), F32),
    "share": ((NSEQ, 8, 256), F32),
    "first": ((NSEQ, 8, 256), F32),
    "second": ((16, 8, 256), F32),
}
N_LOCAL = len(SMALL) + len(TABLES) + len(LARGE)


def main_kernel(*refs):
    ins = refs[:N_LOCAL]
    outs = refs[N_LOCAL : N_LOCAL + len(OUTS)]
    names = list(SCRATCH)
    scratch = refs[N_LOCAL + len(OUTS) :]
    r = Refs(**dict(zip(OUTS, outs)), **dict(zip(names, scratch)))
    (load_sem, out_sem, ag_send, ag_recv, cross_send, cross_recv, relay_send, relay_recv, half_send, half_recv, rs_send, rs_recv,
     sem_a, recv_a, sem_b, recv_b, sem_c, recv_c, sem_d, recv_d) = scratch[len(names) :]
    r.raw_flat = r.raw_all.reshape(A * CH, B)
    chan, seq = lax.axis_index("chan"), lax.axis_index("seq")
    barrier = pltpu.get_barrier_semaphore()

    def signal(device):
        pl.semaphore_signal(barrier, inc=1, device_id=device, device_id_type=MESH)

    x, z = lax.div(seq, 2), lax.rem(seq, 2)
    yz, core = lax.div(chan, 2), lax.rem(chan, 2)
    first_id, second_id = 2 * x + core, 2 * yz + z

    xr, xl, xo = lax.rem(x + 1, 4), lax.rem(x + 3, 4), lax.rem(x + 2, 4)
    other = 1 - z
    near_seq = (2 * x + other, 2 * xr + z, 2 * xr + other, 2 * xl + z, 2 * xl + other)
    near = tuple((chan, to) for to in near_seq)
    partner = (2 * yz + 1 - core, seq)
    to_r, to_l = near[1], near[3]

    def seq_peer(d):
        return (chan, lax.rem(seq + d, NSEQ))

    def first_peer(d):
        to = lax.rem(first_id + d, 8)
        return (2 * yz + lax.rem(to, 2), 2 * lax.div(to, 2) + z)

    def second_peer(d):
        to = lax.rem(second_id + d, 16)
        return (2 * lax.div(to, 2) + core, 2 * x + lax.rem(to, 2))

    def hail(d, carry):
        signal(seq_peer(d))
        signal(first_peer(d))
        return carry

    def hail_second(d, carry):
        signal(second_peer(d))
        return carry

    loads = {}
    for i, name in enumerate(SMALL + TABLES + LARGE):
        loads[name] = pltpu.make_async_copy(ins[i], getattr(r, name), load_sem.at[i])
    for name in SMALL:
        loads[name].start()
    lax.fori_loop(1, 8, hail, 0)
    lax.fori_loop(1, 16, hail_second, 0)
    for name in LARGE + TABLES:
        loads[name].start()
    for name in SMALL:
        loads[name].wait()

    half = ABLK // 2
    piece = CHUNK // 128
    n_piece = ABLK // piece

    def row_of(xx, zz):
        return (2 * xx + zz) * ABLK

    def gather(i, j, device=None):
        part = r.raw_all.at[pl.ds(row_of(x, z) + j * piece, piece)]
        return pltpu.make_async_remote_copy(
            src_ref=part, dst_ref=part, send_sem=ag_send.at[i, j], recv_sem=ag_recv.at[i, j],
            device_id=device or near[i], device_id_type=MESH,
        )

    def cross(j):
        return pltpu.make_async_remote_copy(
            src_ref=r.raw_other.at[pl.ds(j * piece, piece)],
            dst_ref=r.raw_all.at[pl.ds(row_of(x, z) + (2 * core + j) * piece, piece)],
            send_sem=cross_send.at[j], recv_sem=cross_recv.at[j],
            device_id=partner, device_id_type=MESH,
        )

    def send_chunk(j):
        cross(j).start()
        for i in (1, 3, 2, 4, 0):
            gather(i, 2 * core + j).start()

    def relay(h, lane):
        row = jnp.where(h == 0, row_of(xl, (z, other)[lane]), row_of(xr, (z, other)[lane]) + half)
        part = r.raw_all.at[pl.ds(row, half)]
        i = 2 * h + lane
        return pltpu.make_async_remote_copy(
            src_ref=part, dst_ref=part, send_sem=relay_send.at[i], recv_sem=relay_recv.at[i],
            device_id=(chan, jnp.where(h == 0, near_seq[1], near_seq[3])), device_id_type=MESH,
        )

    def pass_on(h):
        for lane in range(2):
            arrived(1 + 2 * h + lane, 2 * h, 2 * h + 2)
            relay(h, lane).start()

    def arrived(i, start, stop):
        def step(j, carry):
            gather(i, j, partner).wait_recv()
            return carry

        lax.fori_loop(start, stop, step, 0)

    zs = (other, z)

    def rows_at(p, row, count):
        return r.gk.at[pl.ds(2 * p, 2), pl.ds(pl.multiple_of(row, half), count)]

    def far_half(p, w, h):
        return pltpu.make_async_remote_copy(
            src_ref=rows_at(p, row_of(xo, zs[w]) + h * half, half), dst_ref=r.half.at[p, w, h],
            send_sem=half_send.at[p, 2 * w + h], recv_sem=half_recv.at[p, 2 * w + h],
            device_id=(to_r, to_l)[h], device_id_type=MESH,
        )

    def near_block(p, i):
        w = i % 2
        src = rows_at(p, row_of(x, other), ABLK) if i == 0 else r.side_out.at[p, w, (i - 1) // 2]
        return pltpu.make_async_remote_copy(
            src_ref=src, dst_ref=r.side.at[p, i], send_sem=rs_send.at[p, i], recv_sem=rs_recv.at[p, i],
            device_id=near[i], device_id_type=MESH,
        )

    def scatter_far(p):
        for w in range(2):
            for h in range(2):
                far_half(p, w, h).start()
        near_block(p, 0).start()

    def scatter_near(p):
        for w in range(2):
            for h in range(2):
                far_half(p, w, h).wait_recv()
                row = row_of((xr, xl)[h], zs[w])
                for i in range(2):
                    mine = r.gk[2 * p + i, pl.ds(pl.multiple_of(row, half), half), :]
                    rest = r.gk[2 * p + i, pl.ds(pl.multiple_of(row + half, half), half), :]
                    extra = r.half[p, w, h, i]
                    r.side_out[p, w, h, i, 0:half, :] = mine + extra if h == 0 else mine
                    r.side_out[p, w, h, i, half:, :] = rest if h == 0 else rest + extra
        for i in range(1, 5):
            near_block(p, i).start()

    prepare_weights(r, chan, 2 * yz + 1 - core)
    net_chunk(r, seq, core, 0)
    pl.semaphore_wait(barrier, 7 + 7 + 15)
    send_chunk(0)
    net_chunk(r, seq, core, 1)
    send_chunk(1)

    for j in range(2):
        cross(j).wait_recv()
        for i in (1, 3, 2, 4, 0):
            gather(i, 2 * (1 - core) + j).start()

    prepare_backward(r)
    for name in LARGE:
        loads[name].wait()
    acc = gate_products(r, 0)
    acc = acc + gate_products(r, 1)
    r.skip_part[...] = jnp.sum(acc, axis=1, keepdims=True)
    for name in TABLES:
        loads[name].wait()

    spectra(r, 0)
    pass_on(core)
    scatter_far(0)
    spectra(r, 1)
    pass_on(1 - core)
    scatter_far(1)

    def pair_step(p, carry):
        spectra(r, p)
        scatter_far(p)
        scatter_near(p - 2)
        return carry

    lax.fori_loop(2, CH // 2, pair_step, 0)
    scatter_near(CH // 2 - 2)
    arrived(0, 0, n_piece)
    for lane in range(2):
        arrived(1 + lane, n_piece // 2, n_piece)
        arrived(3 + lane, 0, n_piece // 2)
    for h in range(2):
        for lane in range(2):
            relay(h, lane).wait_recv()

    def stats_step(c, carry):
        channel_stats(r, c)
        return carry

    lax.fori_loop(0, CH, stats_step, 0, unroll=2)

    def run(size, make):
        def start(d, carry):
            make(d).start()
            return carry

        def wait(d, carry):
            make(d).wait()
            return carry

        lax.fori_loop(1, size, start, 0)
        return lambda: lax.fori_loop(1, size, wait, 0)

    def make_a(d):
        return pltpu.make_async_remote_copy(
            src_ref=r.stat.at[1], dst_ref=r.along.at[d],
            send_sem=sem_a.at[d], recv_sem=recv_a.at[d], device_id=seq_peer(d), device_id_type=MESH,
        )

    wait_along = run(NSEQ, make_a)

    filter_products(r, 0)
    scatter_near(CH // 2 - 1)

    def product_step(p, carry):
        filter_products(r, p)
        return carry

    lax.fori_loop(1, EARLY, product_step, 0)
    results = []

    def leave(n):
        for i, (src, dst) in enumerate(((r.o_val, r.h_val), (r.o_gin, r.h_gin), (r.o_gout, r.h_gout))):
            copy = pltpu.make_async_copy(src.at[n], dst.at[n], out_sem.at[3 * n + i])
            copy.start()
            results.append(copy)

    def settle(p, carry):
        for i in range(5):
            near_block(p, i).wait_recv()
        row = pl.multiple_of(row_of(x, z), ABLK)
        for i in range(2):
            c = 2 * p + i
            total = r.gk[c, pl.ds(row, ABLK), :]
            for k in range(5):
                total = total + r.side[p, k, i]
            r.total[pl.ds(pl.multiple_of(c * ABLK, ABLK), ABLK), :] = total
        return carry

    lax.fori_loop(0, CH // 2, settle, 0, unroll=True)
    wait_along()
    along = r.stat[1]
    for d in range(1, NSEQ):
        along = along + r.along[d]
    along = jnp.sum(along, axis=1, keepdims=True) * (1.0 / L)
    norm = jnp.sqrt(jnp.sum(r.stat[0], axis=1, keepdims=True) + EPSILON)
    scale_gk = jnp.broadcast_to((1.0 / L) / norm, (CH, B))
    scale_raw = jnp.broadcast_to(along / (norm * norm * norm), (CH, B))

    def gradient(half_id):
        def step(i, carry):
            row = half_id * half + i
            total = r.total[pl.ds(row, CH, stride=ABLK), :]
            r.grad_own[row] = total * scale_gk - r.raw_all[row_of(x, z) + row] * scale_raw
            return carry

        lax.fori_loop(0, half, step, 0, unroll=True)

    gradient(1 - core)
    hand = pltpu.make_async_remote_copy(
        src_ref=r.grad_own.at[pl.ds((1 - core) * half, half)], dst_ref=r.grad_other,
        send_sem=sem_a.at[0], recv_sem=recv_a.at[0], device_id=partner, device_id_type=MESH,
    )
    hand.start()
    gradient(core)
    hand.wait()

    def sent(j, carry):
        for i in range(5):
            near_block(j, i).wait_send()
            gather(i, j).wait_send()
        for i in range(4):
            far_half(j, i // 2, i % 2).wait_send()
        return carry

    net_backward(r, seq, core)
    pack_shares(r, core)

    def make_b(d):
        return pltpu.make_async_remote_copy(
            src_ref=r.share.at[lax.rem(first_id + d, 8)], dst_ref=r.first.at[d],
            send_sem=sem_b.at[d], recv_sem=recv_b.at[d], device_id=first_peer(d), device_id_type=MESH,
        )

    def make_c(d):
        return pltpu.make_async_remote_copy(
            src_ref=r.second.at[second_id], dst_ref=r.second.at[second_id],
            send_sem=sem_c.at[d], recv_sem=recv_c.at[d], device_id=second_peer(d), device_id_type=MESH,
        )

    def make_d(d):
        return pltpu.make_async_remote_copy(
            src_ref=r.third.at[first_id], dst_ref=r.third.at[first_id],
            send_sem=sem_d.at[d], recv_sem=recv_d.at[d], device_id=first_peer(d), device_id_type=MESH,
        )

    wait = run(8, make_b)
    lax.fori_loop(EARLY, EARLY + UNDER_FIRST, product_step, 0)
    wait()
    both = r.share[first_id]
    for d in range(1, 8):
        both = both + r.first[d]
    factor = 1.0 / math.sqrt(16 * L)
    r.second[second_id] = both * factor
    wait = run(16, make_c)
    lax.fori_loop(EARLY + UNDER_FIRST, CH // 2, product_step, 0)
    for n in range(2):
        finish(r, n)
        leave(n)
    wait()
    total = r.second[0]
    for c in range(1, 16):
        total = total + r.second[c]
    r.third[first_id] = total
    for c in range(8):
        r.own[c, core] = r.second[2 * c, :, 128:256] + r.second[2 * c + 1, :, 128:256]
    wait = run(8, make_d)
    part = r.own.at[:, core]
    swap = pltpu.make_async_remote_copy(
        src_ref=part, dst_ref=part, send_sem=sem_d.at[0], recv_sem=recv_d.at[0],
        device_id=(2 * yz + 1 - core, seq), device_id_type=MESH,
    )
    swap.start()
    r.g_skip[...] = to_row(r.own[yz, core][:, 113:114])
    wait()
    swap.wait()
    lax.fori_loop(0, CH // 2, sent, 0)
    for i in range(2):
        cross(i).wait_send()
        for lane in range(2):
            relay(i, lane).wait_send()
    for copy in results:
        copy.wait()


def write_kernel(
    i_val, i_gin, i_gout, i_second, i_third, skip,
    o_val, o_gin, o_gout, o_skip, o_in, o_bin, o_mid, o_bmid, o_out, o_rate,
    stage, second, third, g_skip, g_in, g_bin, g_mid, g_bmid, g_out, g_rate, in_sem, out_sem, small_sem,
):
    loads, stores = [], []
    for i, (src, dst) in enumerate(((i_val, o_val), (i_gin, o_gin), (i_gout, o_gout))):
        for q in range(4):
            part = (q // 2, pl.ds(q % 2 * (A // 2), A // 2))
            loads.append(pltpu.make_async_copy(src.at[part], stage.at[(i,) + part], in_sem.at[4 * i + q]))
            stores.append(pltpu.make_async_copy(stage.at[(i,) + part], dst.at[part], out_sem.at[4 * i + q]))
    small = [
        pltpu.make_async_copy(i_second, second, small_sem.at[0]),
        pltpu.make_async_copy(i_third, third, small_sem.at[1]),
        pltpu.make_async_copy(skip, g_skip, small_sem.at[2]),
    ]
    for copy in small + loads:
        copy.start()
    for load, store in zip(loads, stores):
        load.wait()
        store.start()
    for copy in small:
        copy.wait()
    hidden = third[...].reshape(64, 256)
    g_mid[0] = hidden[:, 0:64]
    g_mid[1] = pltpu.roll(hidden[:, 0:128], 64, 1)[:, 0:64]
    flat = jnp.transpose(hidden[:, 128:256])
    g_in[...] = flat[0:33, :]
    g_bin[...] = flat[33:34, :]
    g_bmid[...] = flat[34:36, :]
    own = jnp.transpose(second[...].reshape(128, 128))
    g_out[...] = own[48:112, :]
    g_rate[...] = own[112:113, :]
    pairs = (
        (g_skip, o_skip), (g_in, o_in), (g_bin, o_bin), (g_mid, o_mid), (g_bmid, o_bmid), (g_out, o_out),
        (g_rate, o_rate),
    )
    for i, (src, dst) in enumerate(pairs):
        copy = pltpu.make_async_copy(src, dst, small_sem.at[3 + i])
        copy.start()
        stores.append(copy)
    for copy in stores:
        copy.wait()


def sds(shape, dtype=F32):
    return jax.ShapeDtypeStruct(shape, dtype)


VM = pl.BlockSpec(memory_space=pltpu.VMEM)
HB = pl.BlockSpec(memory_space=pltpu.HBM)
DMA = pltpu.SemaphoreType.DMA


def to_natural(x):
    return x.reshape(2, CH, A, B).transpose(0, 2, 1, 3)


def from_natural(x):
    return x.transpose(0, 2, 1, 3).reshape(2, CH, L)


def local(
    value, gate_in, gate_out, cotangent, skip_gain,
    weight_in, bias_in, weight_mid, bias_mid, weight_out, decay_rate,
):
    small = (
        row_constants(), weight_in.T, bias_in.reshape(1, 64), weight_mid, bias_mid, weight_out.T,
        decay_rate.reshape(1, 128), skip_gain.reshape(1, CH),
    )
    large = tuple(to_natural(x) for x in (value, gate_in, cotangent, gate_out))
    big = sds(BIG, LOW)
    o_val, o_gin, o_gout, own, third, g_skip = pl.pallas_call(
        main_kernel,
        out_shape=[big, big, big, sds((8, 2, 8, 128)), sds((NSEQ, 8, 256)), sds((1, CH))],
        in_specs=[HB] * N_LOCAL,
        out_specs=[HB] * 3 + [VM] * 3,
        scratch_shapes=[pltpu.VMEM(shape, dtype) for shape, dtype in SCRATCH.values()]
        + [
            DMA((N_LOCAL,)), DMA((6,)), DMA((5, 4)), DMA((5, 4)), DMA((2,)), DMA((2,)), DMA((4,)), DMA((4,)),
            DMA((4, 4)), DMA((4, 4)), DMA((4, 5)), DMA((4, 5)), DMA((NSEQ,)), DMA((NSEQ,)),
            DMA((NSEQ,)), DMA((NSEQ,)), DMA((NCHAN,)), DMA((NCHAN,)), DMA((NSEQ,)), DMA((NSEQ,)),
        ],
        compiler_params=pltpu.CompilerParams(
            collective_id=0, has_side_effects=True, vmem_limit_bytes=VMEM_MAIN
        ),
        name="hyena_backward",
    )(*small, *transform_tables(), *large)
    o_val, o_gin, o_gout, g_skip, g_in, g_bin, g_mid, g_bmid, g_out, g_rate = pl.pallas_call(
        write_kernel,
        out_shape=[
            big, big, big, sds((1, CH)), sds((33, 64)), sds((1, 64)), sds((2, 64, 64)), sds((2, 64)),
            sds((64, 128)), sds((1, 128)),
        ],
        in_specs=[HB] * 6,
        out_specs=[HB] * 10,
        scratch_shapes=[
            pltpu.VMEM((3,) + BIG, LOW), pltpu.VMEM((8, 2, 8, 128), F32), pltpu.VMEM((NSEQ, 8, 256), F32),
            pltpu.VMEM((1, CH), F32), pltpu.VMEM((33, 64), F32), pltpu.VMEM((1, 64), F32),
            pltpu.VMEM((2, 64, 64), F32), pltpu.VMEM((2, 64), F32), pltpu.VMEM((64, 128), F32),
            pltpu.VMEM((1, 128), F32),
            DMA((12,)), DMA((12,)), DMA((10,)),
        ],
        compiler_params=pltpu.CompilerParams(vmem_limit_bytes=VMEM_MAIN),
        name="write_results",
    )(o_val, o_gin, o_gout, own, third, g_skip)
    return (
        from_natural(o_val), from_natural(o_gin), from_natural(o_gout), g_skip.reshape(CH),
        g_in.T, g_bin.reshape(64), g_mid, g_bmid, g_out.T, g_rate.reshape(128),
    )


def solution(mesh):
    return jax.shard_map(
        local,
        mesh=mesh,
        in_specs=(
            P("seq", "chan", None), P("seq", "chan", None), P("seq", "chan", None), P("seq", "chan", None),
            P("chan"), P(), P(), P(), P(), P(), P(),
        ),
        out_specs=(
            P("seq", "chan", None), P("seq", "chan", None), P("seq", "chan", None),
            P("chan"), P(), P(), P(), P(), P(), P(),
        ),
        check_vma=False,
    )
```

```python
import functools
import math

import jax
import jax.numpy as jnp
import numpy as np
from jax import lax
from jax.experimental import pallas as pl
from jax.experimental.pallas import tpu as pltpu
from jax.sharding import PartitionSpec as P

EPSILON = 1e-06
HIGHEST = lax.Precision.HIGHEST
L = 32768
A = 256
B = 128
CH = 8
NSEQ = 8
NCHAN = 16
ABLK = A // NSEQ
TB = L // NSEQ
CHUNK = 1024
LOW = jnp.bfloat16
F32 = jnp.float32
MESH = pl.DeviceIdType.MESH


def band_table(length, bands):
    highest = length / 4.0
    return np.array(
        [math.floor(highest ** (number / (bands - 1)) + 0.5) for number in range(bands)], np.int64
    )


def row_constants():
    freq = np.zeros((48, 128), np.int32)
    off = np.zeros((48, 128), np.int32)
    bands = band_table(L, 16)
    freq[1:17] = bands[:, None]
    off[1:17] = L // 4
    freq[17:33] = bands[:, None]
    return np.stack([freq, off])


def transform_tables():
    k = np.arange(A)[:, None]
    rows = 2.0 * np.pi * (((4 * k + 1) * np.arange(A)[None, :]) % 1024) / 1024.0
    w1 = np.concatenate([np.cos(rows), -np.sin(rows)], axis=0)
    turn = 2.0 * np.pi * (((4 * k + 1) * np.arange(B)[None, :]) % (4 * L)) / (4.0 * L)
    q = np.arange(B)
    cols = 2.0 * np.pi * ((q[:, None] * q[None, :]) % B) / B
    c, s = np.cos(cols), np.sin(cols)
    fwd = np.block([[c, -s], [s, c]])
    inv = np.block([[c, s], [-s, c]])
    low = np.dtype(LOW)
    return (
        w1.astype(low),
        w1.T.astype(low),
        fwd.astype(low),
        inv.astype(low),
        np.stack([np.cos(turn), np.sin(turn)]).astype(np.float32),
    )


def poly_fit():
    x = (np.cos(np.pi * (np.arange(64) + 0.5) / 64) + 1) / 2 * (np.pi / 2 * 1.002) ** 2
    r = np.sqrt(x)
    sin_c = np.polynomial.polynomial.polyfit(x, np.sin(r) / r, 4)
    cos_c = np.polynomial.polynomial.polyfit(x, np.cos(r), 5)
    return [float(v) for v in sin_c], [float(v) for v in cos_c]


SIN_C, COS_C = poly_fit()


def horner(x, coefs):
    acc = jnp.full_like(x, coefs[-1])
    for value in coefs[-2::-1]:
        acc = acc * x + value
    return acc


def sin_small(r):
    return r * horner(r * r, SIN_C)


def sin_cos(z):
    n = jnp.floor(z * (1.0 / math.pi) + 0.5)
    r = z - n * 3.140625
    r = r - n * 9.67653589793e-4
    half = n * 0.5
    sign = 1.0 - 4.0 * (half - jnp.floor(half))
    r2 = r * r
    return sign * (r * horner(r2, SIN_C)), sign * horner(r2, COS_C)


def dot_full(x, y):
    return jnp.dot(x, y, precision=HIGHEST, preferred_element_type=F32)


def dot_nt(x, y, precision=None):
    return lax.dot_general(x, y, (((1,), (1,)), ((), ())), precision=precision, preferred_element_type=F32)


def dot_tn(x, y, precision=None):
    return lax.dot_general(x, y, (((0,), (0,)), ((), ())), precision=precision, preferred_element_type=F32)


def low_dot(x, y):
    return jnp.dot(x, y, preferred_element_type=F32)


def split(x):
    hi = x.astype(LOW)
    return hi, (x - hi.astype(F32)).astype(LOW)


def iota(shape, dim):
    return lax.broadcasted_iota(jnp.int32, shape, dim)


def to_column(row, size, shift):
    n = row.shape[1]
    pick = iota((size, n), 0) + shift == iota((size, n), 1)
    return jnp.sum(jnp.where(pick, jnp.broadcast_to(row, (size, n)), 0.0), axis=1, keepdims=True)


def to_row(col):
    n = col.shape[0]
    pick = iota((n, n), 0) == iota((n, n), 1)
    return jnp.sum(jnp.where(pick, jnp.broadcast_to(col, (n, n)), 0.0), axis=0, keepdims=True)


def repeat_matrix(rows, period, times):
    shape = (rows, period * times)
    j = iota(shape, 1)
    hit = j == iota(shape, 0)
    for m in range(1, times):
        hit = hit | (j == iota(shape, 0) + m * period)
    return jnp.where(hit, 1.0, 0.0)


def hi_hi_lo(w, period):
    hi = w.astype(LOW).astype(F32)
    lane = iota(w.shape, 1)
    out = jnp.where(lane < 2 * period, hi, jnp.where(lane < 3 * period, w - hi, 0.0))
    return out.astype(LOW)


class Refs:
    def __init__(self, **refs):
        self.__dict__.update(refs)


def prepare_weights(r, chan, other):
    first = jnp.where(iota((8, 64), 0) == 1, jnp.broadcast_to(r.b_in[...], (8, 64)), 0.0)
    r.w_pad[0:32, :] = r.w_in[0:32, :]
    r.w_pad[32:40, :] = jnp.where(iota((8, 64), 0) == 0, jnp.broadcast_to(r.w_in[32:33, :], (8, 64)), first)
    r.w_pad[40:48, :] = jnp.zeros((8, 64), F32)
    r.k_in[...] = hi_hi_lo(dot_tn(r.w_pad[...], repeat_matrix(48, 48, 3), HIGHEST), 48)
    rep = repeat_matrix(64, 64, 3)
    for i in range(2):
        w = r.w_mid[i]
        r.k_mid[i] = hi_hi_lo(dot_full(w, rep), 64)
    row = iota((2 * CH, 128), 0)
    channel = jnp.where(row < CH, row + chan * CH, row - CH + other * CH)
    pick = jnp.where(iota((2 * CH, 128), 1) == channel, 1.0, 0.0)
    w_own = dot_nt(pick, r.w_out[...], HIGHEST)
    r.k_out[...] = hi_hi_lo(dot_full(w_own, rep), 64)
    r.w_own[...] = w_own
    rates = jnp.sum(jnp.where(pick > 0.5, jnp.broadcast_to(r.rate[...], (2 * CH, 128)), 0.0), axis=1, keepdims=True)
    r.rate_col[...] = jnp.broadcast_to(rates, (2 * CH, 128))
    r.bias_col[0] = jnp.broadcast_to(to_column(r.b_mid[0:1, :], 64, 0), (64, 128))
    r.bias_col[1] = jnp.broadcast_to(to_column(r.b_mid[1:2, :], 64, 0), (64, 128))


def prepare_backward(r):
    rep = repeat_matrix(64, 64, 3)
    for i in range(2):
        r.k_back[i] = hi_hi_lo(dot_tn(r.w_mid[i], rep, HIGHEST), 64)
    r.k_outback[...] = hi_hi_lo(dot_tn(r.w_own[...], repeat_matrix(2 * CH, 2 * CH, 3), HIGHEST), 2 * CH)


def wide(block, times):
    return jnp.concatenate([block] * times, axis=1)


def fraction(base):
    pos = base + iota((2 * CH, CHUNK), 1)
    return pos.astype(F32) * (1.0 / L)


def net_chunk(r, seq, core, j):
    per = CHUNK // 128
    lanes = pl.ds(j * CHUNK, CHUNK)
    pos = seq * TB + (2 * core + j) * CHUNK + iota((48, CHUNK), 1)
    row = iota((48, CHUNK), 0)
    phase = ((wide(r.bands[0], per) * pos + (wide(r.bands[1], per) + L // 2)) & (L - 1)) - L // 2
    phase = jnp.where(phase > L // 4, L // 2 - phase, phase)
    phase = jnp.where(phase < -(L // 4), -(L // 2) - phase, phase)
    wave = sin_small(phase.astype(F32) * (2.0 * math.pi / L))
    frac = pos.astype(F32) * (1.0 / L)
    hi, lo = split(jnp.where(row == 0, frac, jnp.where(row == 33, 1.0, wave)))
    r.feat[0:48, lanes] = hi
    r.feat[48:64, lanes] = jnp.zeros((16, CHUNK), LOW)
    r.feat[64:112, lanes] = lo
    r.feat[112:128, lanes] = jnp.zeros((16, CHUNK), LOW)
    z = low_dot(r.k_in[...], jnp.concatenate([hi, lo, hi], axis=0))
    for layer in range(3):
        s, c = sin_cos(z)
        r.der[layer, :, lanes] = c
        hi, lo = split(s)
        r.act[layer, 0:64, lanes] = hi
        r.act[layer, 64:128, lanes] = lo
        x = jnp.concatenate([hi, lo, hi], axis=0)
        if layer < 2:
            z = low_dot(r.k_mid[layer], x) + wide(r.bias_col[layer], per)
    raw = low_dot(r.k_out[...], x) * jnp.exp(-wide(r.rate_col[...], per) * frac[0 : 2 * CH, :])
    for i in range(per):
        r.raw_all[seq * ABLK + (2 * core + j) * per + i] = raw[0:CH, 128 * i : 128 * i + 128]
        r.raw_other[j * per + i] = raw[CH:, 128 * i : 128 * i + 128]


def net_backward(r, seq, core):
    per = CHUNK // 128
    r.acc[...] = jnp.zeros_like(r.acc)
    r.acc_out[...] = jnp.zeros_like(r.acc_out)
    r.acc_bias[...] = jnp.zeros_like(r.acc_bias)
    r.acc_rate[...] = jnp.zeros_like(r.acc_rate)

    def lane_sum(x):
        total = x[:, 0:128]
        for i in range(1, per):
            total = total + x[:, 128 * i : 128 * i + 128]
        return total

    def step(j, carry):
        lanes = pl.ds(pl.multiple_of(j * CHUNK, CHUNK), CHUNK)
        start = (2 * core + j) * per

        def rows(mine, first, others, second):
            return jnp.concatenate(
                [jnp.concatenate([mine[first + i], others[second + i]], axis=0) for i in range(per)], axis=1
            )

        grad = rows(r.grad_own, start, r.grad_other, j * per)
        raw = rows(r.raw_all, seq * ABLK + start, r.raw_other, j * per)
        frac = fraction(seq * TB + (2 * core + j) * CHUNK)
        r.acc_rate[...] -= lane_sum(grad * raw * frac)
        shaped = grad * jnp.exp(-wide(r.rate_col[...], per) * frac)
        hi = shaped.astype(LOW).astype(F32)
        lo = shaped - hi
        pair = jnp.concatenate([hi, lo], axis=0).astype(LOW)
        r.acc_out[...] += dot_nt(pair, r.act[2, :, lanes])
        d = low_dot(r.k_outback[...], jnp.concatenate([hi, lo, hi], axis=0).astype(LOW))
        for layer in (2, 1, 0):
            d = d * r.der[layer, :, lanes]
            hi, lo = split(d)
            pair = jnp.concatenate([hi, lo], axis=0)
            if layer:
                r.acc_bias[layer - 1] += lane_sum(d)
                r.acc[layer] += dot_nt(pair, r.act[layer - 1, :, lanes])
                d = low_dot(r.k_back[layer - 1], jnp.concatenate([hi, lo, hi], axis=0))
            else:
                r.acc[0] += dot_nt(pair, r.feat[:, lanes])
        return carry

    lax.fori_loop(0, TB // CHUNK // 2, step, 0, unroll=True)


def fold_halves(x):
    n = x.shape[0] // 2
    total = x[0:n] + x[n:]
    return total + pltpu.roll(total, 64, 1)


def pack_shares(r, core):
    lane = iota((64, 128), 1)
    r.block[0] = jnp.where(lane < 64, fold_halves(r.acc[1]), fold_halves(r.acc[2]))
    block = fold_halves(r.acc[0])
    block = jnp.where(lane == 34, jnp.sum(r.acc_bias[0], axis=1, keepdims=True), block)
    r.block[1] = jnp.where(lane == 35, jnp.sum(r.acc_bias[1], axis=1, keepdims=True), block)
    lane = iota((2 * CH, 128), 1)
    own = pltpu.roll(fold_halves(r.acc_out[...]), 48, 1)
    own = jnp.where(lane == 112, jnp.sum(r.acc_rate[...], axis=1, keepdims=True), own)
    own = jnp.where(lane > 112, 0.0, own)
    lane = iota((CH, 128), 1)
    theirs = own[CH:]
    own = jnp.where(lane == 113, r.skip_part[...], own[0:CH])

    def place(s, carry):
        rows = pl.ds(pl.multiple_of(8 * s, 8), 8)
        r.share[s, :, 0:128] = r.block[0, rows, :]
        apart = jnp.where(lax.rem(s, 2) == core, own, theirs)
        r.share[s, :, 128:256] = jnp.where(lane < 48, r.block[1, rows, :], apart)
        return carry

    lax.fori_loop(0, NSEQ, place, 0)


def to_low(x):
    return x.astype(LOW)


def channel_rows(c):
    return pl.ds(c, A, stride=CH)


def forward_pair(r, x):
    tc, ts = r.turn[0], r.turn[1]
    g = low_dot(r.w1[...], x)
    parts = []
    for n in range(2):
        re, im = g[0:A, n * B : n * B + B], g[A:, n * B : n * B + B]
        parts.append(jnp.concatenate([to_low(re * tc + im * ts), to_low(im * tc - re * ts)], axis=1))
    f = low_dot(jnp.concatenate(parts, axis=0), r.fwd[...])
    return f[0:A], f[A:]


def inverse_pair(r, specs):
    tc, ts = r.turn[0], r.turn[1]
    s = jnp.concatenate([jnp.concatenate([to_low(re), to_low(im)], axis=1) for re, im in specs], axis=0)
    t = low_dot(s, r.inv[...])
    cols = []
    for n in range(2):
        re, im = t[n * A : n * A + A, 0:B], t[n * A : n * A + A, B:]
        cols.append(jnp.concatenate([to_low(re * tc - im * ts), to_low(re * ts + im * tc)], axis=0))
    y = low_dot(r.w1t[...], jnp.concatenate(cols, axis=1))
    return y[:, 0:B], y[:, B:]


BLK = 16
EARLY = 2
UNDER_FIRST = 1
VMEM_MAIN = 56 << 20


def gate_products(r, n):
    def step(j, acc):
        part = pl.ds(j * BLK, BLK)
        rows = pl.ds(pl.multiple_of(j * (BLK * CH), BLK * CH), BLK * CH)
        m = r.val[n, part].astype(F32) * r.gin[n, part].astype(F32)
        g = r.cot[n, part].astype(F32) * r.gout[n, part].astype(F32)
        r.mixed[n, rows, :] = m.reshape(BLK * CH, B)
        r.inner[n, rows, :] = g.reshape(BLK * CH, B)
        return acc + jnp.sum(m * g, axis=0)

    return lax.fori_loop(0, A // BLK, step, jnp.zeros((CH, B), F32))


def spectra(r, p):
    cross = []
    for i in range(2):
        c = 2 * p + i
        rows = channel_rows(c)
        fm = forward_pair(r, jnp.concatenate([to_low(r.mixed[n, rows, :]) for n in range(2)], axis=1))
        fg = forward_pair(r, jnp.concatenate([to_low(r.inner[n, rows, :]) for n in range(2)], axis=1))
        re = im = None
        for n in range(2):
            r.f_mixed[c, n] = fm[n]
            r.f_inner[c, n] = fg[n]
            mr, mi = fm[n][:, 0:B], fm[n][:, B:]
            gr, gi = fg[n][:, 0:B], fg[n][:, B:]
            pr, pi = mr * gr + mi * gi, mr * gi - mi * gr
            re, im = (pr, pi) if re is None else (re + pr, im + pi)
        cross.append((re, im))
    ys = inverse_pair(r, cross)
    for i in range(2):
        r.gk[2 * p + i] = ys[i]


def channel_stats(r, c):
    x = r.raw_flat[channel_rows(c), :]
    r.stat[0, pl.ds(c, 1), :] = jnp.sum(x * x, axis=0, keepdims=True)
    r.stat[1, pl.ds(c, 1), :] = jnp.sum(x * r.gk[c], axis=0, keepdims=True)


def filter_products(r, p):
    kernels = []
    for i in range(2):
        c = 2 * p + i
        square = jnp.sum(r.stat[0, pl.ds(c, 1), :], axis=1, keepdims=True)
        kernels.append(to_low(r.raw_flat[channel_rows(c), :] * (1.0 / jnp.sqrt(square + EPSILON))))
    fk = forward_pair(r, jnp.concatenate(kernels, axis=1))
    for i in range(2):
        c = 2 * p + i
        rows = channel_rows(c)
        kr, ki = fk[i][:, 0:B] * (1.0 / L), fk[i][:, B:] * (1.0 / L)
        specs = []
        for n in range(2):
            mr, mi = r.f_mixed[c, n, :, 0:B], r.f_mixed[c, n, :, B:]
            specs.append((mr * kr - mi * ki, mr * ki + mi * kr))
        ys = inverse_pair(r, specs)
        for n in range(2):
            r.conv[n, rows, :] = ys[n]
        specs = []
        for n in range(2):
            gr, gi = r.f_inner[c, n, :, 0:B], r.f_inner[c, n, :, B:]
            specs.append((gr * kr + gi * ki, gi * kr - gr * ki))
        ys = inverse_pair(r, specs)
        for n in range(2):
            r.back[n, rows, :] = ys[n]


def finish(r, n):
    gain = jnp.broadcast_to(to_column(r.skip[...], CH, 0), (CH, B))[None]

    def step(j, carry):
        part = pl.ds(j * BLK, BLK)
        rows = pl.ds(pl.multiple_of(j * (BLK * CH), BLK * CH), BLK * CH)
        shape = (BLK, CH, B)
        full = r.conv[n, rows, :].reshape(shape) + gain * r.mixed[n, rows, :].reshape(shape)
        r.o_gout[n, part] = to_low(r.cot[n, part].astype(F32) * full)
        full = r.back[n, rows, :].reshape(shape) + gain * r.inner[n, rows, :].reshape(shape)
        r.o_val[n, part] = to_low(full * r.gin[n, part].astype(F32))
        r.o_gin[n, part] = to_low(full * r.val[n, part].astype(F32))
        return carry

    lax.fori_loop(0, A // BLK, step, 0)


SMALL = ("bands", "w_in", "b_in", "w_mid", "b_mid", "w_out", "rate", "skip")
TABLES = ("w1", "w1t", "fwd", "inv", "turn")
LARGE = ("val", "gin", "cot", "gout")
OUTS = ("h_val", "h_gin", "h_gout", "own", "third", "g_skip")
BIG = (2, A, CH, B)
FULL = (2, A * CH, B)
SCRATCH = {
    "bands": ((2, 48, 128), jnp.int32),
    "w_in": ((33, 64), F32),
    "b_in": ((1, 64), F32),
    "w_mid": ((2, 64, 64), F32),
    "b_mid": ((2, 64), F32),
    "w_out": ((64, 128), F32),
    "rate": ((1, 128), F32),
    "skip": ((1, CH), F32),
    "w1": ((2 * A, A), LOW),
    "w1t": ((A, 2 * A), LOW),
    "fwd": ((2 * B, 2 * B), LOW),
    "inv": ((2 * B, 2 * B), LOW),
    "turn": ((2, A, B), F32),
    "val": (BIG, LOW),
    "gin": (BIG, LOW),
    "cot": (BIG, LOW),
    "gout": (BIG, LOW),
    "o_val": (BIG, LOW),
    "o_gin": (BIG, LOW),
    "o_gout": (BIG, LOW),
    "w_pad": ((48, 64), F32),
    "k_in": ((64, 144), LOW),
    "k_mid": ((2, 64, 192), LOW),
    "k_back": ((2, 64, 192), LOW),
    "w_own": ((2 * CH, 64), F32),
    "k_out": ((2 * CH, 192), LOW),
    "k_outback": ((64, 6 * CH), LOW),
    "rate_col": ((2 * CH, 128), F32),
    "bias_col": ((2, 64, 128), F32),
    "feat": ((128, TB // 2), LOW),
    "act": ((3, 128, TB // 2), LOW),
    "der": ((3, 64, TB // 2), F32),
    "raw_all": ((A, CH, B), F32),
    "raw_other": ((ABLK // 2, CH, B), F32),
    "grad_own": ((ABLK, CH, B), F32),
    "grad_other": ((ABLK // 2, CH, B), F32),
    "total": ((CH * ABLK, B), F32),
    "half": ((CH // 2, 2, 2, 2, ABLK // 2, B), F32),
    "side_out": ((CH // 2, 2, 2, 2, ABLK, B), F32),
    "side": ((CH // 2, 5, 2, ABLK, B), F32),
    "stat": ((2, CH, B), F32),
    "along": ((NSEQ, CH, B), F32),
    "mixed": (FULL, F32),
    "inner": (FULL, F32),
    "f_mixed": ((CH, 2, A, 2 * B), F32),
    "f_inner": ((CH, 2, A, 2 * B), F32),
    "gk": ((CH, A, B), F32),
    "conv": (FULL, F32),
    "back": (FULL, F32),
    "acc": ((3, 128, 128), F32),
    "acc_out": ((4 * CH, 128), F32),
    "acc_bias": ((2, 64, 128), F32),
    "acc_rate": ((2 * CH, 128), F32),
    "skip_part": ((CH, 1), F32),
    "block": ((2, 64, 128), F32),
    "share": ((NSEQ, 8, 256), F32),
    "first": ((NSEQ, 8, 256), F32),
    "second": ((16, 8, 256), F32),
}
N_LOCAL = len(SMALL) + len(TABLES) + len(LARGE)


def main_kernel(*refs):
    ins = refs[:N_LOCAL]
    outs = refs[N_LOCAL : N_LOCAL + len(OUTS)]
    names = list(SCRATCH)
    scratch = refs[N_LOCAL + len(OUTS) :]
    r = Refs(**dict(zip(OUTS, outs)), **dict(zip(names, scratch)))
    (load_sem, out_sem, ag_send, ag_recv, cross_send, cross_recv, relay_send, relay_recv, half_send, half_recv, rs_send, rs_recv,
     sem_a, recv_a, sem_b, recv_b, sem_c, recv_c, sem_d, recv_d) = scratch[len(names) :]
    r.raw_flat = r.raw_all.reshape(A * CH, B)
    chan, seq = lax.axis_index("chan"), lax.axis_index("seq")
    barrier = pltpu.get_barrier_semaphore()

    def signal(device):
        pl.semaphore_signal(barrier, inc=1, device_id=device, device_id_type=MESH)

    x, z = lax.div(seq, 2), lax.rem(seq, 2)
    yz, core = lax.div(chan, 2), lax.rem(chan, 2)
    first_id, second_id = 2 * x + core, 2 * yz + z

    xr, xl, xo = lax.rem(x + 1, 4), lax.rem(x + 3, 4), lax.rem(x + 2, 4)
    other = 1 - z
    near_seq = (2 * x + other, 2 * xr + z, 2 * xr + other, 2 * xl + z, 2 * xl + other)
    near = tuple((chan, to) for to in near_seq)
    partner = (2 * yz + 1 - core, seq)
    to_r, to_l = near[1], near[3]

    def seq_peer(d):
        return (chan, lax.rem(seq + d, NSEQ))

    def first_peer(d):
        to = lax.rem(first_id + d, 8)
        return (2 * yz + lax.rem(to, 2), 2 * lax.div(to, 2) + z)

    def second_peer(d):
        to = lax.rem(second_id + d, 16)
        return (2 * lax.div(to, 2) + core, 2 * x + lax.rem(to, 2))

    def hail(d, carry):
        signal(seq_peer(d))
        signal(first_peer(d))
        return carry

    def hail_second(d, carry):
        signal(second_peer(d))
        return carry

    loads = {}
    for i, name in enumerate(SMALL + TABLES + LARGE):
        loads[name] = pltpu.make_async_copy(ins[i], getattr(r, name), load_sem.at[i])
    for name in SMALL:
        loads[name].start()
    lax.fori_loop(1, 8, hail, 0)
    lax.fori_loop(1, 16, hail_second, 0)
    for name in LARGE + TABLES:
        loads[name].start()
    for name in SMALL:
        loads[name].wait()

    half = ABLK // 2
    piece = CHUNK // 128
    n_piece = ABLK // piece

    def row_of(xx, zz):
        return (2 * xx + zz) * ABLK

    def gather(i, j, device=None):
        part = r.raw_all.at[pl.ds(row_of(x, z) + j * piece, piece)]
        return pltpu.make_async_remote_copy(
            src_ref=part, dst_ref=part, send_sem=ag_send.at[i, j], recv_sem=ag_recv.at[i, j],
            device_id=device or near[i], device_id_type=MESH,
        )

    def cross(j):
        return pltpu.make_async_remote_copy(
            src_ref=r.raw_other.at[pl.ds(j * piece, piece)],
            dst_ref=r.raw_all.at[pl.ds(row_of(x, z) + (2 * core + j) * piece, piece)],
            send_sem=cross_send.at[j], recv_sem=cross_recv.at[j],
            device_id=partner, device_id_type=MESH,
        )

    def send_chunk(j):
        cross(j).start()
        for i in (1, 3, 2, 4, 0):
            gather(i, 2 * core + j).start()

    def relay(h, lane):
        row = jnp.where(h == 0, row_of(xl, (z, other)[lane]), row_of(xr, (z, other)[lane]) + half)
        part = r.raw_all.at[pl.ds(row, half)]
        i = 2 * h + lane
        return pltpu.make_async_remote_copy(
            src_ref=part, dst_ref=part, send_sem=relay_send.at[i], recv_sem=relay_recv.at[i],
            device_id=(chan, jnp.where(h == 0, near_seq[1], near_seq[3])), device_id_type=MESH,
        )

    def pass_on(h):
        for lane in range(2):
            arrived(1 + 2 * h + lane, 2 * h, 2 * h + 2)
            relay(h, lane).start()

    def arrived(i, start, stop):
        def step(j, carry):
            gather(i, j, partner).wait_recv()
            return carry

        lax.fori_loop(start, stop, step, 0)

    zs = (other, z)

    def rows_at(p, row, count):
        return r.gk.at[pl.ds(2 * p, 2), pl.ds(pl.multiple_of(row, half), count)]

    def far_half(p, w, h):
        return pltpu.make_async_remote_copy(
            src_ref=rows_at(p, row_of(xo, zs[w]) + h * half, half), dst_ref=r.half.at[p, w, h],
            send_sem=half_send.at[p, 2 * w + h], recv_sem=half_recv.at[p, 2 * w + h],
            device_id=(to_r, to_l)[h], device_id_type=MESH,
        )

    def near_block(p, i):
        w = i % 2
        src = rows_at(p, row_of(x, other), ABLK) if i == 0 else r.side_out.at[p, w, (i - 1) // 2]
        return pltpu.make_async_remote_copy(
            src_ref=src, dst_ref=r.side.at[p, i], send_sem=rs_send.at[p, i], recv_sem=rs_recv.at[p, i],
            device_id=near[i], device_id_type=MESH,
        )

    def scatter_far(p):
        for w in range(2):
            for h in range(2):
                far_half(p, w, h).start()
        near_block(p, 0).start()

    def scatter_near(p):
        for w in range(2):
            for h in range(2):
                far_half(p, w, h).wait_recv()
                row = row_of((xr, xl)[h], zs[w])
                for i in range(2):
                    mine = r.gk[2 * p + i, pl.ds(pl.multiple_of(row, half), half), :]
                    rest = r.gk[2 * p + i, pl.ds(pl.multiple_of(row + half, half), half), :]
                    extra = r.half[p, w, h, i]
                    r.side_out[p, w, h, i, 0:half, :] = mine + extra if h == 0 else mine
                    r.side_out[p, w, h, i, half:, :] = rest if h == 0 else rest + extra
        for i in range(1, 5):
            near_block(p, i).start()

    prepare_weights(r, chan, 2 * yz + 1 - core)
    net_chunk(r, seq, core, 0)
    pl.semaphore_wait(barrier, 7 + 7 + 15)
    send_chunk(0)
    net_chunk(r, seq, core, 1)
    send_chunk(1)

    for j in range(2):
        cross(j).wait_recv()
        for i in (1, 3, 2, 4, 0):
            gather(i, 2 * (1 - core) + j).start()

    prepare_backward(r)
    for name in LARGE:
        loads[name].wait()
    acc = gate_products(r, 0)
    acc = acc + gate_products(r, 1)
    r.skip_part[...] = jnp.sum(acc, axis=1, keepdims=True)
    for name in TABLES:
        loads[name].wait()

    spectra(r, 0)
    pass_on(core)
    scatter_far(0)
    spectra(r, 1)
    pass_on(1 - core)
    scatter_far(1)

    def pair_step(p, carry):
        spectra(r, p)
        scatter_far(p)
        scatter_near(p - 2)
        return carry

    lax.fori_loop(2, CH // 2, pair_step, 0)
    scatter_near(CH // 2 - 2)
    arrived(0, 0, n_piece)
    for lane in range(2):
        arrived(1 + lane, n_piece // 2, n_piece)
        arrived(3 + lane, 0, n_piece // 2)
    for h in range(2):
        for lane in range(2):
            relay(h, lane).wait_recv()

    def stats_step(c, carry):
        channel_stats(r, c)
        return carry

    lax.fori_loop(0, CH, stats_step, 0, unroll=2)

    def run(size, make):
        def start(d, carry):
            make(d).start()
            return carry

        def wait(d, carry):
            make(d).wait()
            return carry

        lax.fori_loop(1, size, start, 0)
        return lambda: lax.fori_loop(1, size, wait, 0)

    def make_a(d):
        return pltpu.make_async_remote_copy(
            src_ref=r.stat.at[1], dst_ref=r.along.at[d],
            send_sem=sem_a.at[d], recv_sem=recv_a.at[d], device_id=seq_peer(d), device_id_type=MESH,
        )

    wait_along = run(NSEQ, make_a)

    filter_products(r, 0)
    scatter_near(CH // 2 - 1)

    def product_step(p, carry):
        filter_products(r, p)
        return carry

    lax.fori_loop(1, EARLY, product_step, 0)
    results = []

    def leave(n):
        for i, (src, dst) in enumerate(((r.o_val, r.h_val), (r.o_gin, r.h_gin), (r.o_gout, r.h_gout))):
            copy = pltpu.make_async_copy(src.at[n], dst.at[n], out_sem.at[3 * n + i])
            copy.start()
            results.append(copy)

    def settle(p, carry):
        for i in range(5):
            near_block(p, i).wait_recv()
        row = pl.multiple_of(row_of(x, z), ABLK)
        for i in range(2):
            c = 2 * p + i
            total = r.gk[c, pl.ds(row, ABLK), :]
            for k in range(5):
                total = total + r.side[p, k, i]
            r.total[pl.ds(pl.multiple_of(c * ABLK, ABLK), ABLK), :] = total
        return carry

    lax.fori_loop(0, CH // 2, settle, 0, unroll=True)
    wait_along()
    along = r.stat[1]
    for d in range(1, NSEQ):
        along = along + r.along[d]
    along = jnp.sum(along, axis=1, keepdims=True) * (1.0 / L)
    norm = jnp.sqrt(jnp.sum(r.stat[0], axis=1, keepdims=True) + EPSILON)
    scale_gk = jnp.broadcast_to((1.0 / L) / norm, (CH, B))
    scale_raw = jnp.broadcast_to(along / (norm * norm * norm), (CH, B))

    def gradient(half_id):
        def step(i, carry):
            row = half_id * half + i
            total = r.total[pl.ds(row, CH, stride=ABLK), :]
            r.grad_own[row] = total * scale_gk - r.raw_all[row_of(x, z) + row] * scale_raw
            return carry

        lax.fori_loop(0, half, step, 0, unroll=True)

    gradient(1 - core)
    hand = pltpu.make_async_remote_copy(
        src_ref=r.grad_own.at[pl.ds((1 - core) * half, half)], dst_ref=r.grad_other,
        send_sem=sem_a.at[0], recv_sem=recv_a.at[0], device_id=partner, device_id_type=MESH,
    )
    hand.start()
    gradient(core)
    hand.wait()

    def sent(j, carry):
        for i in range(5):
            near_block(j, i).wait_send()
            gather(i, j).wait_send()
        for i in range(4):
            far_half(j, i // 2, i % 2).wait_send()
        return carry

    net_backward(r, seq, core)
    pack_shares(r, core)

    def make_b(d):
        return pltpu.make_async_remote_copy(
            src_ref=r.share.at[lax.rem(first_id + d, 8)], dst_ref=r.first.at[d],
            send_sem=sem_b.at[d], recv_sem=recv_b.at[d], device_id=first_peer(d), device_id_type=MESH,
        )

    def make_c(d):
        return pltpu.make_async_remote_copy(
            src_ref=r.second.at[second_id], dst_ref=r.second.at[second_id],
            send_sem=sem_c.at[d], recv_sem=recv_c.at[d], device_id=second_peer(d), device_id_type=MESH,
        )

    def make_d(d):
        return pltpu.make_async_remote_copy(
            src_ref=r.third.at[first_id], dst_ref=r.third.at[first_id],
            send_sem=sem_d.at[d], recv_sem=recv_d.at[d], device_id=first_peer(d), device_id_type=MESH,
        )

    wait = run(8, make_b)
    lax.fori_loop(EARLY, EARLY + UNDER_FIRST, product_step, 0)
    wait()
    both = r.share[first_id]
    for d in range(1, 8):
        both = both + r.first[d]
    factor = 1.0 / math.sqrt(16 * L)
    r.second[second_id] = both * factor
    wait = run(16, make_c)
    lax.fori_loop(EARLY + UNDER_FIRST, CH // 2, product_step, 0)
    for n in range(2):
        finish(r, n)
        leave(n)
    wait()
    total = r.second[0]
    for c in range(1, 16):
        total = total + r.second[c]
    r.third[first_id] = total
    for c in range(8):
        r.own[c, core] = r.second[2 * c, :, 128:256] + r.second[2 * c + 1, :, 128:256]
    wait = run(8, make_d)
    part = r.own.at[:, core]
    swap = pltpu.make_async_remote_copy(
        src_ref=part, dst_ref=part, send_sem=sem_d.at[0], recv_sem=recv_d.at[0],
        device_id=(2 * yz + 1 - core, seq), device_id_type=MESH,
    )
    swap.start()
    r.g_skip[...] = to_row(r.own[yz, core][:, 113:114])
    lax.fori_loop(0, CH // 2, sent, 0)
    for i in range(2):
        cross(i).wait_send()
        for lane in range(2):
            relay(i, lane).wait_send()
    for copy in results:
        copy.wait()
    wait()
    swap.wait()


def write_kernel(
    i_val, i_gin, i_gout, i_second, i_third, skip,
    o_val, o_gin, o_gout, o_skip, o_in, o_bin, o_mid, o_bmid, o_out, o_rate,
    stage, second, third, g_skip, g_in, g_bin, g_mid, g_bmid, g_out, g_rate, in_sem, out_sem, small_sem,
):
    loads, stores = [], []
    for i, (src, dst) in enumerate(((i_val, o_val), (i_gin, o_gin), (i_gout, o_gout))):
        for q in range(4):
            part = (q // 2, pl.ds(q % 2 * (A // 2), A // 2))
            loads.append(pltpu.make_async_copy(src.at[part], stage.at[(i,) + part], in_sem.at[4 * i + q]))
            stores.append(pltpu.make_async_copy(stage.at[(i,) + part], dst.at[part], out_sem.at[4 * i + q]))
    small = [
        pltpu.make_async_copy(i_second, second, small_sem.at[0]),
        pltpu.make_async_copy(i_third, third, small_sem.at[1]),
        pltpu.make_async_copy(skip, g_skip, small_sem.at[2]),
    ]
    for copy in small + loads:
        copy.start()
    for load, store in zip(loads, stores):
        load.wait()
        store.start()
    for copy in small:
        copy.wait()
    hidden = third[...].reshape(64, 256)
    g_mid[0] = hidden[:, 0:64]
    g_mid[1] = pltpu.roll(hidden[:, 0:128], 64, 1)[:, 0:64]
    flat = jnp.transpose(hidden[:, 128:256])
    g_in[...] = flat[0:33, :]
    g_bin[...] = flat[33:34, :]
    g_bmid[...] = flat[34:36, :]
    own = jnp.transpose(second[...].reshape(128, 128))
    g_out[...] = own[48:112, :]
    g_rate[...] = own[112:113, :]
    pairs = (
        (g_skip, o_skip), (g_in, o_in), (g_bin, o_bin), (g_mid, o_mid), (g_bmid, o_bmid), (g_out, o_out),
        (g_rate, o_rate),
    )
    for i, (src, dst) in enumerate(pairs):
        copy = pltpu.make_async_copy(src, dst, small_sem.at[3 + i])
        copy.start()
        stores.append(copy)
    for copy in stores:
        copy.wait()


def sds(shape, dtype=F32):
    return jax.ShapeDtypeStruct(shape, dtype)


VM = pl.BlockSpec(memory_space=pltpu.VMEM)
HB = pl.BlockSpec(memory_space=pltpu.HBM)
DMA = pltpu.SemaphoreType.DMA


def to_natural(x):
    return x.reshape(2, CH, A, B).transpose(0, 2, 1, 3)


def from_natural(x):
    return x.transpose(0, 2, 1, 3).reshape(2, CH, L)


def local(
    value, gate_in, gate_out, cotangent, skip_gain,
    weight_in, bias_in, weight_mid, bias_mid, weight_out, decay_rate,
):
    small = (
        row_constants(), weight_in.T, bias_in.reshape(1, 64), weight_mid, bias_mid, weight_out.T,
        decay_rate.reshape(1, 128), skip_gain.reshape(1, CH),
    )
    large = tuple(to_natural(x) for x in (value, gate_in, cotangent, gate_out))
    big = sds(BIG, LOW)
    o_val, o_gin, o_gout, own, third, g_skip = pl.pallas_call(
        main_kernel,
        out_shape=[big, big, big, sds((8, 2, 8, 128)), sds((NSEQ, 8, 256)), sds((1, CH))],
        in_specs=[HB] * N_LOCAL,
        out_specs=[HB] * 3 + [VM] * 3,
        scratch_shapes=[pltpu.VMEM(shape, dtype) for shape, dtype in SCRATCH.values()]
        + [
            DMA((N_LOCAL,)), DMA((6,)), DMA((5, 4)), DMA((5, 4)), DMA((2,)), DMA((2,)), DMA((4,)), DMA((4,)),
            DMA((4, 4)), DMA((4, 4)), DMA((4, 5)), DMA((4, 5)), DMA((NSEQ,)), DMA((NSEQ,)),
            DMA((NSEQ,)), DMA((NSEQ,)), DMA((NCHAN,)), DMA((NCHAN,)), DMA((NSEQ,)), DMA((NSEQ,)),
        ],
        compiler_params=pltpu.CompilerParams(
            collective_id=0, has_side_effects=True, vmem_limit_bytes=VMEM_MAIN
        ),
        name="hyena_backward",
    )(*small, *transform_tables(), *large)
    o_val, o_gin, o_gout, g_skip, g_in, g_bin, g_mid, g_bmid, g_out, g_rate = pl.pallas_call(
        write_kernel,
        out_shape=[
            big, big, big, sds((1, CH)), sds((33, 64)), sds((1, 64)), sds((2, 64, 64)), sds((2, 64)),
            sds((64, 128)), sds((1, 128)),
        ],
        in_specs=[HB] * 6,
        out_specs=[HB] * 10,
        scratch_shapes=[
            pltpu.VMEM((3,) + BIG, LOW), pltpu.VMEM((8, 2, 8, 128), F32), pltpu.VMEM((NSEQ, 8, 256), F32),
            pltpu.VMEM((1, CH), F32), pltpu.VMEM((33, 64), F32), pltpu.VMEM((1, 64), F32),
            pltpu.VMEM((2, 64, 64), F32), pltpu.VMEM((2, 64), F32), pltpu.VMEM((64, 128), F32),
            pltpu.VMEM((1, 128), F32),
            DMA((12,)), DMA((12,)), DMA((10,)),
        ],
        compiler_params=pltpu.CompilerParams(vmem_limit_bytes=VMEM_MAIN),
        name="write_results",
    )(o_val, o_gin, o_gout, own, third, g_skip)
    return (
        from_natural(o_val), from_natural(o_gin), from_natural(o_gout), g_skip.reshape(CH),
        g_in.T, g_bin.reshape(64), g_mid, g_bmid, g_out.T, g_rate.reshape(128),
    )


def solution(mesh):
    return jax.shard_map(
        local,
        mesh=mesh,
        in_specs=(
            P("seq", "chan", None), P("seq", "chan", None), P("seq", "chan", None), P("seq", "chan", None),
            P("chan"), P(), P(), P(), P(), P(), P(),
        ),
        out_specs=(
            P("seq", "chan", None), P("seq", "chan", None), P("seq", "chan", None),
            P("chan"), P(), P(), P(), P(), P(), P(),
        ),
        check_vma=False,
    )
```
